32 devices in a mesh: expert: 4 (over z), seq: 4 (over y, x), dp: 2 (over core).
Axes of the slice: x: 2, y: 2, z: 4, core: 2. Of those that a mesh axis runs over, the one named last changes fastest.
Arguments:
- grad_out: bfloat16 [8, 512, 2048], P(('expert', 'dp'), 'seq'), may hold values from -6 to 6
- expert_ids: int32 [8, 512, 2], P(('expert', 'dp'), 'seq'), may hold values from 0 to 3, all different within a row; in each aligned block of 128 rows (0 to 127, 128 to 255, ..., all dimensions but the last counted through in order) at most 112 rows name the same one
- gate_weights: float32 [8, 512, 2], P(('expert', 'dp'), 'seq'), may hold values from 0.1 to 0.9
- hidden: bfloat16 [8, 512, 2, 7168], P(('expert', 'dp'), 'seq'), may hold values from -0.3125 to 0.3125
- queries: bfloat16 [8, 512, 2048], P(('expert', 'dp'), 'seq')
- keys: bfloat16 [8, 512, 512], P(('expert', 'dp'), 'seq')
- values: bfloat16 [8, 512, 512], P(('expert', 'dp'), 'seq'), may hold values from -6 to 6
Outputs:
- expert_grad: bfloat16 [4, 7168, 2048], P('expert', ('seq', 'dp'))
- grad_queries: bfloat16 [8, 512, 2048], P(('expert', 'dp'), 'seq')
- grad_keys: bfloat16 [8, 512, 512], P(('expert', 'dp'), 'seq')
- grad_values: bfloat16 [8, 512, 512], P(('expert', 'dp'), 'seq')
The draws below stay inside these ranges and needn't reach their ends.
Inputs may be any that keep to these rules, and one draw needn't show every extreme that they name: `expert_ids`: each position names two different experts; among the 128 positions of one device no expert is named more than 112 times.
All inputs are finite; a program needn't handle non-finite values.
Results may differ from the reference program's by a relative error of at most 0.018.
Values may be sent and summed in bfloat16 or wider, within the bound.
A program may use at most 128 MiB of HBM per device.

```python
import math
import jax
import jax.numpy as jnp
import numpy as np
from jax import lax

D = 2048
FF = 7168
HEADS = 16
KV_HEADS = 4
HEAD_DIM = 128
TOK_DEV = 128
LENGTH = 512
BATCH = 8
EXPERTS = 4
CAP = 112
N_SEQ = 4
N_DP = 2


def drawn_pair(key):
    queries = jax.random.normal(jax.random.fold_in(key, 101), (BATCH, LENGTH, HEADS * HEAD_DIM), jnp.float32)
    keys = jax.random.normal(jax.random.fold_in(key, 202), (BATCH, LENGTH, KV_HEADS, HEAD_DIM), jnp.float32)
    return (queries, keys.reshape(BATCH, LENGTH, KV_HEADS * HEAD_DIM))


def draw_queries(key, part):
    return drawn_pair(key)[0].astype(jnp.bfloat16)


def draw_keys(key, part):
    return drawn_pair(key)[1].astype(jnp.bfloat16)


def spiked(drawn, key, source, target, blocks, factor):
    def block_of(axis_at):
        return (jnp.arange(drawn.shape[axis_at]) // (drawn.shape[axis_at] // blocks)).reshape((-1,) + (1,) * (drawn.ndim - 1 - axis_at))

    one_side = jax.random.permutation(key, blocks)[block_of(target)]
    other_side = (block_of(target) + blocks // 2) % blocks
    return jnp.where((block_of(source) == one_side) | (block_of(source) == other_side), factor * drawn, drawn)


def levels(rng, dims, pieces, low, largest):
    def one(dim, parts):
        steps = jax.random.uniform(jax.random.fold_in(jax.random.fold_in(rng, 6), dim), (parts,), jnp.float32, low / len(pieces), largest / len(pieces))
        return jnp.repeat(jnp.exp(steps), dims[dim] // parts).reshape((-1,) + (1,) * (len(dims) - dim - 1))

    loudness = one(*pieces[0])
    for cut in pieces[1:]:
        loudness = loudness * one(*cut)
    return loudness


def assign_block(own_key, own, number, rows, number_of, top, reach, lean):
    ranking = jax.random.permutation(own_key, number_of)
    heavy_load, common = portions_of(number_of, rows * top, reach, lean, True), portions_of(number_of, rows * top, reach, lean, False)
    places = jnp.arange(number_of)

    def named(lengths, rotation):
        used = int((lengths > 0).sum())
        fixed = max(1, used // 4)
        shifted = fixed + (places - fixed + rotation * (used - fixed)) % max(1, number_of - fixed)
        return jnp.zeros((number_of,), jnp.int32).at[ranking[jnp.where(places < fixed, places, shifted)]].set(jnp.asarray(lengths, jnp.int32))

    lengths = jnp.where(number % 4 == 0, named(heavy_load, number // 4), named(common, number - number // 4 - 1))
    mixed = jax.random.permutation(jax.random.fold_in(own, 3), number_of)
    source_of, taker = mixed[0:number_of // 2 * 2:2], mixed[1:number_of // 2 * 2:2]
    slack = jnp.minimum(lengths[source_of] - 1, reach - lengths[taker]) // 2
    slack = jnp.where((source_of == ranking[0]) | (taker == ranking[0]) | (lengths[taker] == 0), 0, jnp.maximum(slack, 0))
    shifted = jax.random.randint(jax.random.fold_in(own, 4), (number_of // 2,), 0, 1 << 20) % (slack + 1)
    lengths = lengths.at[source_of].add(-shifted).at[taker].add(shifted)
    items = jnp.searchsorted(jnp.cumsum(lengths), jnp.arange(rows * top), side="right").astype(jnp.int32)
    table = items.reshape(top, rows).T
    table = table[jax.random.permutation(jax.random.fold_in(own, 1), rows)]
    rotation = jax.random.randint(jax.random.fold_in(own, 2), (rows, 1), 0, top)
    return jnp.take_along_axis(table, (jnp.arange(top)[None, :] + rotation) % top, axis=1)


def portions_of(count, total, reach, skew, full):
    weights = [(1 << 20) // math.isqrt(rank ** skew) + 1 for rank in range(1, count + 1)]
    largest = reach if full else min(reach, max(-(-total // count), total * weights[0] // sum(weights)))
    least = 1 if total - largest >= count - 1 else 0
    given, rest = [largest] + [least] * (count - 1), total - largest - least * (count - 1)
    while rest > 0:
        movable = [i for i in range(1, count) if given[i] < largest] or [i for i in range(1, count) if given[i] < reach]
        mass, budget = sum([weights[i] for i in movable]), rest
        for i in movable:
            more = min(reach - given[i], max(1, budget * weights[i] // mass), rest)
            given[i] = given[i] + more
            rest = rest - more
    return np.array(given)


def scatter_about(rng, dims, spread, limit, split=(), held_as=jnp.bfloat16):
    drawn = jax.random.normal(rng, dims, jnp.float32) * spread
    if len(split) > 0:
        drawn = levels(rng, dims, split, -0.22, 0.18) * drawn
    return jnp.clip(drawn, min=-limit, max=limit).astype(held_as)


def gaussian_with(key, shape, scale, reach, shards, heavy, held_as=jnp.bfloat16):
    result = scale * jax.random.normal(key, shape, jnp.float32)
    if shards:
        result = result * levels(key, shape, shards, -0.22, 0.18)
    return jnp.clip(spiked(result, jax.random.fold_in(key, 3), *heavy), -reach, reach).astype(held_as)


def setup_inputs(seed: int = 0) -> dict:
    streams_of = jax.random.split(jax.random.key(seed), 8)
    grad_out = scatter_about(streams_of[0], (BATCH, LENGTH, D), 1.0, 6.0, ((0, 8), (1, 4)))
    expert_ids_keys = jax.random.split(jax.random.fold_in(streams_of[1], 1), BATCH * LENGTH // TOK_DEV)
    expert_ids_turns = jax.random.permutation(jax.random.fold_in(streams_of[1], 3), BATCH * LENGTH // TOK_DEV)
    expert_ids = jax.vmap(lambda own, number: assign_block(jax.random.fold_in(streams_of[1], 2), own, number, TOK_DEV, EXPERTS, 2, CAP, 2))(expert_ids_keys, expert_ids_turns).reshape((BATCH, LENGTH, 2))
    gate_weights = jnp.clip(0.1 + 0.79999997 * jax.random.uniform(streams_of[2], (BATCH, LENGTH, 2), jnp.float32) ** levels(streams_of[2], (BATCH, LENGTH, 2), ((0, 8), (1, 4)), -0.2, 0.2), 0.1, 0.9)
    hidden = gaussian_with(streams_of[3], (BATCH, LENGTH, 2, FF), (0.5 * (N_DP * N_SEQ * TOK_DEV) ** -0.5), 0.3125, ((0, 8), (1, 4)), (0, 3, 8, 2.0))
    queries = draw_queries(jax.random.fold_in(streams_of[7], 71), 0)
    keys = draw_keys(jax.random.fold_in(streams_of[7], 71), 0)
    values = scatter_about(streams_of[6], (BATCH, LENGTH, KV_HEADS * HEAD_DIM), 1.0, 6.0, ((0, 8), (1, 4)))
    return {"grad_out": grad_out, "expert_ids": expert_ids, "gate_weights": gate_weights, "hidden": hidden, "queries": queries, "keys": keys, "values": values}


def expert_grads(grad_out, expert_ids, gate_weights, hidden):
    row_total = BATCH * LENGTH * 2
    flat_ids = expert_ids.reshape(row_total).astype(jnp.int32)
    scaled = (gate_weights[..., None] * grad_out[:, :, None, :].astype(jnp.float32)).astype(jnp.bfloat16)
    scaled = scaled.reshape(row_total, D)
    flat_hidden = hidden.reshape(row_total, FF)
    row_order = jnp.argsort(flat_ids, stable=True).astype(jnp.int32)
    onehot = (flat_ids[:, None] == jnp.arange(EXPERTS, dtype=jnp.int32)[None, :]).astype(jnp.int32)
    counts = jnp.sum(onehot, axis=0).astype(jnp.int32)
    starts = (jnp.cumsum(counts) - counts).astype(jnp.int32)
    most_rows = BATCH * N_SEQ * CAP
    padded = jnp.concatenate([row_order, jnp.zeros((most_rows,), jnp.int32)])

    def one_expert(expert):
        picked = lax.dynamic_slice(padded, (starts[expert],), (most_rows,))
        usable = jnp.arange(most_rows, dtype=jnp.int32) < counts[expert]
        picked_hidden = jnp.where(usable[:, None], flat_hidden[picked], jnp.zeros((), jnp.bfloat16))
        picked_scaled = jnp.where(usable[:, None], scaled[picked], jnp.zeros((), jnp.bfloat16))
        total = jnp.dot(picked_hidden.T, picked_scaled, preferred_element_type=jnp.float32)
        return total.astype(jnp.bfloat16)

    return lax.map(one_expert, jnp.arange(EXPERTS, dtype=jnp.int32))


def attention_grads(queries, keys, values, grad_out):
    per_group = HEADS // KV_HEADS
    score_scale = HEAD_DIM ** -0.5

    def one_sequence(operands):
        query_rows, key_rows, value_rows, out_rows = operands
        query_heads = query_rows.astype(jnp.float32).reshape(LENGTH, KV_HEADS, per_group, HEAD_DIM)
        out_heads = out_rows.astype(jnp.float32).reshape(LENGTH, KV_HEADS, per_group, HEAD_DIM)
        key_heads = key_rows.astype(jnp.float32).reshape(LENGTH, KV_HEADS, HEAD_DIM)
        value_heads = value_rows.astype(jnp.float32).reshape(LENGTH, KV_HEADS, HEAD_DIM)
        scores = jnp.einsum("qhgd,khd->hgqk", query_heads, key_heads) * score_scale
        row_max = jnp.max(scores, axis=-1, keepdims=True)
        raised = jnp.exp(scores - row_max)
        probabilities = raised / jnp.sum(raised, axis=-1, keepdims=True)
        probs_low = probabilities.astype(jnp.bfloat16)
        dprobs = jnp.einsum("qhgd,khd->hgqk", out_heads, value_heads)
        row_delta = jnp.sum(probabilities * dprobs, axis=-1, keepdims=True)
        dscores = (probabilities * (dprobs - row_delta)).astype(jnp.bfloat16)
        grad_v = jnp.einsum("hgqk,qhgd->khd", probs_low.astype(jnp.float32), out_heads)
        grad_q = jnp.einsum("hgqk,khd->qhgd", dscores.astype(jnp.float32), key_heads) * score_scale
        grad_k = jnp.einsum("hgqk,qhgd->khd", dscores.astype(jnp.float32), query_heads) * score_scale
        return (grad_q.reshape(LENGTH, HEADS * HEAD_DIM).astype(jnp.bfloat16),
                grad_k.reshape(LENGTH, KV_HEADS * HEAD_DIM).astype(jnp.bfloat16),
                grad_v.reshape(LENGTH, KV_HEADS * HEAD_DIM).astype(jnp.bfloat16))

    return lax.map(one_sequence, (queries, keys, values, grad_out))


def reference(grad_out, expert_ids, gate_weights, hidden, queries, keys, values):
    expert_grad = expert_grads(grad_out, expert_ids, gate_weights, hidden)
    grad_queries, grad_keys, grad_values = attention_grads(queries, keys, values, grad_out)
    return (expert_grad, grad_queries, grad_keys, grad_values)
```

```python
import functools

import jax
import jax.numpy as jnp
from jax import lax
from jax.experimental import pallas as pl
from jax.experimental.pallas import tpu as pltpu
from jax.sharding import PartitionSpec as P

HEADS = 16
KV_HEADS = 4
HEAD_DIM = 128
GROUP = HEADS // KV_HEADS
MESH = pl.DeviceIdType.MESH


def dot(a, b, contract):
    return lax.dot_general(a, b, (contract, ((), ())), preferred_element_type=jnp.float32)


def routing_codes(ids, order_row, order_col, experts, capacity):
    count = max(8, experts)
    rows = ids.shape[1]
    expert_of = lax.broadcasted_iota(jnp.int32, (count, rows), 0).astype(jnp.float32)
    onehot = (expert_of == ids).astype(jnp.float32)
    earlier = (order_col < order_row).astype(jnp.float32)
    before = dot(onehot.astype(jnp.bfloat16), earlier.astype(jnp.bfloat16), ((1,), (0,)))
    slot = jnp.sum(before * onehot, axis=0, keepdims=True)
    return ids * float(capacity) + slot


def spreads(experts):
    return experts <= 8 and experts & (experts - 1) == 0


def kernel(
    dims,
    ids_t, info, go, q, k, v, hid,
    eg_out, gq_out, gk_out, gv_out,
    kbuf, vbuf, idbuf, hraw, hsend, hrecv, gsend, grecv, infos,
    kpart, vpart, kown, vown, kin, vin, precv,
    small_send, small_recv, local_sem, hraw_send, hraw_recv,
    gz_send, gz_recv, gi_send, gi_recv, gs_send, gs_recv, hz_send, hz_recv,
    part_send, part_recv, pair_send, pair_recv,
):
    E, S, T, C, U, D = dims
    half = U // 2
    first = -(-half // 256) * 128
    pieces = [(n, o, w) for n in range(2) for o, w in ((0, first), (first, half - first)) if w > 0]
    spread = spreads(E)
    e = lax.axis_index("expert")
    s = lax.axis_index("seq")
    d = lax.axis_index("dp")
    seq_peer = [lax.rem(s + i, S) for i in range(S)]
    bases = [
        pl.multiple_of((d if n else 1 - d) * half + o, 128) for n, o, _ in pieces
    ]

    def ex_peer(j):
        return lax.rem(e + j, E)

    barrier = pltpu.get_barrier_semaphore()
    for i in range(1, S):
        pl.semaphore_signal(barrier, inc=1, device_id={"seq": seq_peer[i]}, device_id_type=MESH)

    @pl.loop(1, E)
    def _(j):
        pl.semaphore_signal(barrier, inc=1, device_id={"expert": ex_peer(j)}, device_id_type=MESH)

    pl.semaphore_signal(barrier, inc=1, device_id={"dp": 1 - d}, device_id_type=MESH)
    pl.semaphore_wait(barrier, S + E - 1)

    def send(src, dst, ssem, rsem, where):
        return pltpu.make_async_remote_copy(
            src_ref=src, dst_ref=dst, send_sem=ssem, recv_sem=rsem,
            device_id=where, device_id_type=MESH,
        )

    def small_copy(n, i, slot):
        src, dst = ((ids_t, idbuf), (k, kbuf), (v, vbuf))[n]
        return send(src, dst.at[slot], small_send.at[n, i], small_recv.at[n, slot], {"seq": seq_peer[i]})

    def raw_copy(c, i, slot):
        width = pieces[c][2]
        cols = pl.ds(pl.multiple_of(seq_peer[i] * U + bases[c], 128), width)
        return send(
            hid.at[:, :, cols], hraw.at[slot, :, :, pl.ds(bases[c], width)],
            hraw_send.at[c, i], hraw_recv.at[c, slot], {"seq": seq_peer[i]},
        )

    own_cols = pl.ds(pl.multiple_of(s * U, 128), U)
    own_raw = pltpu.make_async_copy(hid.at[:, :, own_cols], hraw.at[s], local_sem.at[0])
    own_raw.start()
    for i in range(1, S):
        for n in range(3):
            small_copy(n, i, s).start()
    for c in range(len(pieces)):
        for i in range(1, S):
            raw_copy(c, i, s).start()
    kbuf[s] = k[...]
    vbuf[s] = v[...]
    idbuf[s] = ids_t[...]

    rows = 2 * T
    col = lax.broadcasted_iota(jnp.int32, (rows, rows), 1)
    row = lax.broadcasted_iota(jnp.int32, (rows, rows), 0)
    place = lax.broadcasted_iota(jnp.int32, (E * C, rows), 0).astype(jnp.float32)

    def expert_rows(p):
        return pl.ds(pl.multiple_of(p * C, 16), C)

    def gs_copy(i, z, slot):
        return send(grecv.at[s, z], grecv.at[slot, z], gs_send.at[i, z], gs_recv.at[slot, z], {"seq": seq_peer[i]})

    def gs_wait(i, z):
        slot = seq_peer[i]
        send(grecv.at[s, z], grecv.at[slot, z], gs_send.at[i, z], gs_recv.at[slot, z], {"seq": slot}).wait_recv()

    def packed_grads(ids, gates, grads, wanted):
        code = routing_codes(
            ids, 2 * lax.rem(col, T) + col // T, 2 * lax.rem(row, T) + row // T, E, C
        )
        picks = (wanted == code).astype(jnp.float32)
        gate = jnp.sum(picks * gates, axis=1, keepdims=True)
        token_picks = (picks[:, :T] + picks[:, T:]).astype(jnp.bfloat16)
        return (dot(token_picks, grads, ((1,), (0,))) * gate).astype(jnp.bfloat16)

    if spread:
        def flip(at, b):
            return at + b - 2 * b * lax.rem(at // b, 2)

        bits = []
        b = E // 2
        while b >= 1:
            bits.append(b)
            b //= 2

        def masks(n):
            held = [0]
            for bit in bits[:n]:
                held = held + [m + bit for m in held]
            return held

        def at_mask(m):
            at = e
            for bit in bits:
                if m & bit:
                    at = flip(at, bit)
            return at

        def gz_pair(m, n, slot):
            to = {"expert": flip(e, bits[n])}
            key = m + bits[n]
            return (
                send(gsend.at[slot], gsend.at[slot], gz_send.at[key], gz_recv.at[slot], to),
                send(infos.at[slot], infos.at[slot], gi_send.at[key], gi_recv.at[slot], to),
            )

        def forward(m):
            z = at_mask(m)
            wanted = (
                lax.broadcasted_iota(jnp.int32, (C, rows), 0) + e * C
            ).astype(jnp.float32)
            grecv[s, z] = packed_grads(infos[z, 0:1, :], infos[z, 8:9, :], gsend[z], wanted)
            for i in range(1, S):
                gs_copy(i, z, s).start()

        def arrive(m, n):
            for copy in gz_pair(m, n, at_mask(m + bits[n])):
                copy.wait_recv()
            for later in range(n + 1, len(bits)):
                for copy in gz_pair(m + bits[n], later, at_mask(m + bits[n])):
                    copy.start()

        gsend[e] = go[...]
        infos[e] = info[...]
        for n in range(len(bits)):
            for copy in gz_pair(0, n, e):
                copy.start()
    else:

        def gz_copy(j, slot):
            p = ex_peer(j)
            return send(gsend.at[expert_rows(p)], grecv.at[s, slot], gz_send.at[j], gz_recv.at[slot], {"expert": p})

        gsend[...] = packed_grads(info[0:1, :], info[8:9, :], go[...], place)

        @pl.loop(1, E)
        def _(j):
            gz_copy(j, e).start()

        grecv[s, e] = gsend[expert_rows(e)]
        for i in range(1, S):
            gs_copy(i, e, s).start()

    def hz_copy(c, i, j, slot):
        p = ex_peer(j)
        src = seq_peer[i]
        units = pl.ds(bases[c], pieces[c][2])
        return send(
            hsend.at[src, expert_rows(p), units], hrecv.at[src, slot, :, units],
            hz_send.at[c, src, j], hz_recv.at[c, src, slot], {"expert": p},
        )

    def pack_hidden(c, i):
        src = seq_peer[i]
        width = pieces[c][2]
        units = pl.ds(bases[c], width)
        hcode = routing_codes(idbuf[src, 0:1, :], col, row, E, C)
        hpicks = (place == hcode).astype(jnp.bfloat16)
        hsend[src, :, units] = dot(
            hpicks, hraw[src, :, :, units].reshape(rows, width), ((1,), (0,))
        ).astype(jnp.bfloat16)

        @pl.loop(1, E)
        def _(j):
            hz_copy(c, i, j, e).start()

        hrecv[src, e, :, units] = hsend[src, expert_rows(e), units]

    own_raw.wait()
    for c in range(len(pieces)):
        pack_hidden(c, 0)
    if spread:
        forward(0)

    scale = HEAD_DIM ** (-0.5)
    length = S * T

    def attention(j):
        lanes = slice(j * HEAD_DIM, (j + 1) * HEAD_DIM)
        heads = [slice(h * HEAD_DIM, (h + 1) * HEAD_DIM) for h in range(j * GROUP, (j + 1) * GROUP)]
        qs = jnp.concatenate([q[:, h] for h in heads], axis=0)
        gs = jnp.concatenate([go[:, h] for h in heads], axis=0)
        kj = kbuf[:, :, lanes].reshape(length, HEAD_DIM)
        vj = vbuf[:, :, lanes].reshape(length, HEAD_DIM)
        scores = dot(qs, kj, ((1,), (1,))) * scale
        raised = jnp.exp(scores - jnp.max(scores, axis=-1, keepdims=True))
        probs = raised / jnp.sum(raised, axis=-1, keepdims=True)
        dprobs = dot(gs, vj, ((1,), (1,)))
        delta = jnp.sum(probs * dprobs, axis=-1, keepdims=True)
        ds = (probs * (dprobs - delta)).astype(jnp.bfloat16)
        dv = dot(probs.astype(jnp.bfloat16), gs, ((0,), (0,)))
        dk = dot(ds, qs, ((0,), (0,))) * scale
        dq = dot(ds, kj, ((1,), (0,))) * scale
        for n, h in enumerate(heads):
            gq_out[:, h] = dq[n * T : (n + 1) * T].astype(jnp.bfloat16)
        dk = dk.reshape(S, T, HEAD_DIM)
        dv = dv.reshape(S, T, HEAD_DIM)
        kown[:, :, lanes] = dk
        vown[:, :, lanes] = dv
        kpart[:, :, lanes] = dk.astype(jnp.bfloat16)
        vpart[:, :, lanes] = dv.astype(jnp.bfloat16)

    for i in range(1, S):
        for n in range(3):
            small_copy(n, i, seq_peer[i]).wait_recv()

    attention(0)

    if spread:
        attention(1)
        for n in range(len(bits)):
            for m in masks(n):
                arrive(m, n)
                forward(m + bits[n])
    else:

        @pl.loop(1, E)
        def _(j):
            z = ex_peer(j)
            gz_copy(j, z).wait_recv()
            for i in range(1, S):
                gs_copy(i, z, s).start()

        attention(1)
    for c in range(len(pieces)):
        for i in range(1, S):
            raw_copy(c, i, seq_peer[i]).wait_recv()
            pack_hidden(c, i)
        if c + 2 < KV_HEADS:
            attention(c + 2)
    for j in range(len(pieces) + 2, KV_HEADS):
        attention(j)

    def part_copy(n, i, slot):
        src, dst = ((kpart, kin), (vpart, vin))[n]
        return send(src.at[seq_peer[i]], dst.at[slot], part_send.at[n, i], part_recv.at[n, slot], {"seq": seq_peer[i]})

    for i in range(1, S):
        for n in range(2):
            part_copy(n, i, s).start()
    for n, (own, got, out) in enumerate(((kown, kin, gk_out), (vown, vin, gv_out))):
        total = own[s]
        for i in range(1, S):
            part_copy(n, i, seq_peer[i]).wait_recv()
            total = total + got[seq_peer[i]].astype(jnp.float32)
        out[...] = total.astype(jnp.bfloat16)

    @pl.loop(0, E)
    def _(z):
        for i in range(1, S):
            gs_wait(i, z)

    wide = 256
    tiles = [
        (o + t, min(wide, w - t)) for n, o, w in pieces if n == 0 for t in range(0, w, wide)
    ]

    def arrived(n, off):
        for c, (m, o, _) in enumerate(pieces):
            if m == n and o == off:

                @pl.loop(1, E)
                def _(j):
                    for i in range(S):
                        hz_copy(c, i, j, ex_peer(j)).wait_recv()

    def product(base, off, width):
        units = pl.ds(pl.multiple_of(base + off, 128), width)
        h = hrecv[:, :, :, units].reshape(S * E * C, width)
        return dot(h, grecv[...].reshape(S * E * C, D), ((0,), (0,)))

    def pair_copy(n):
        off, width = tiles[n]
        return send(eg_out.at[off : off + width], precv.at[off : off + width], pair_send.at[n], pair_recv.at[n], {"dp": 1 - d})

    for n, (off, width) in enumerate(tiles):
        arrived(0, off)
        eg_out[off : off + width, :] = product((1 - d) * half, off, width).astype(jnp.bfloat16)
        pair_copy(n).start()
    for n, (off, width) in enumerate(tiles):
        arrived(1, off)
        mine = product(d * half, off, width)
        pair_copy(n).wait_recv()
        pair_copy(n).wait_send()
        got = precv[off : off + width, :].astype(jnp.float32)
        eg_out[off : off + width, :] = (mine + got).astype(jnp.bfloat16)

    for i in range(1, S):
        for n in range(3):
            small_copy(n, i, s).wait_send()
        for n in range(2):
            part_copy(n, i, s).wait_send()
        for c in range(len(pieces)):
            raw_copy(c, i, s).wait_send()

    @pl.loop(0, E)
    def _(z):
        for i in range(1, S):
            gs_copy(i, z, s).wait_send()

    @pl.loop(1, E)
    def _(j):
        if not spread:
            gz_copy(j, e).wait_send()
        for i in range(S):
            for c in range(len(pieces)):
                hz_copy(c, i, j, e).wait_send()

    if spread:
        for n in range(len(bits)):
            for m in masks(n):
                for copy in gz_pair(m, n, at_mask(m)):
                    copy.wait_send()


def on_device(grad_out, expert_ids, gate_weights, hidden, queries, keys, values):
    E = lax.axis_size("expert")
    S = lax.axis_size("seq")
    T = grad_out.shape[1]
    D = grad_out.shape[2]
    U = hidden.shape[3] // S
    C = -(-(7 * T // (2 * E)) // 16) * 16
    KD = keys.shape[2]
    rows = 2 * T
    bf, f32 = jnp.bfloat16, jnp.float32
    ids = expert_ids[0].astype(f32)
    ids_t = jnp.broadcast_to(ids.reshape(1, rows), (8, rows))
    ids_k = jnp.broadcast_to(ids.T.reshape(1, rows), (8, rows))
    gates_k = jnp.broadcast_to(gate_weights[0].T.reshape(1, rows), (8, rows))
    tiles = -(-(U // 2) // 256)
    info = jnp.concatenate([ids_k, gates_k], axis=0)
    sent = (E, T, D) if spreads(E) else (E * C, D)
    vm = pl.BlockSpec(memory_space=pltpu.VMEM)
    dma = pltpu.SemaphoreType.DMA
    eg, gq, gk, gv = pl.pallas_call(
        functools.partial(kernel, (E, S, T, C, U, D)),
        out_shape=(
            jax.ShapeDtypeStruct((U // 2, D), bf),
            jax.ShapeDtypeStruct((T, queries.shape[2]), bf),
            jax.ShapeDtypeStruct((T, KD), bf),
            jax.ShapeDtypeStruct((T, KD), bf),
        ),
        in_specs=[vm] * 6 + [pl.BlockSpec(memory_space=pl.ANY)],
        out_specs=(vm,) * 4,
        scratch_shapes=[
            pltpu.VMEM((S, T, KD), bf),
            pltpu.VMEM((S, T, KD), bf),
            pltpu.VMEM((S, 8, rows), f32),
            pltpu.VMEM((S, T, 2, U), bf),
            pltpu.VMEM((S, E * C, U), bf),
            pltpu.VMEM((S, E, C, U), bf),
            pltpu.VMEM(sent, bf),
            pltpu.VMEM((S, E, C, D), bf),
            pltpu.VMEM((E if spreads(E) else 1, 16, rows), f32),
            pltpu.VMEM((S, T, KD), bf),
            pltpu.VMEM((S, T, KD), bf),
            pltpu.VMEM((S, T, KD), f32),
            pltpu.VMEM((S, T, KD), f32),
            pltpu.VMEM((S, T, KD), bf),
            pltpu.VMEM((S, T, KD), bf),
            pltpu.VMEM((U // 2, D), bf),
            dma((3, S)), dma((3, S)), dma((1,)), dma((4, S)), dma((4, S)),
            dma((E,)), dma((E,)), dma((E,)), dma((E,)), dma((S, E)), dma((S, E)), dma((4, S, E)), dma((4, S, E)),
            dma((2, S)), dma((2, S)), dma((tiles,)), dma((tiles,)),
        ],
        compiler_params=pltpu.CompilerParams(
            collective_id=0, has_side_effects=True, vmem_limit_bytes=62 * 1024 * 1024
        ),
    )(ids_t, info, grad_out[0], queries[0], keys[0], values[0], hidden[0])
    return (eg[None], gq[None], gk[None], gv[None])


def flip(at, b):
    return at + b - 2 * b * lax.rem(at // b, 2)


def greet(peers):
    barrier = pltpu.get_barrier_semaphore()
    for peer in peers:
        pl.semaphore_signal(barrier, inc=1, device_id=peer, device_id_type=MESH)
    pl.semaphore_wait(barrier, len(peers))


def send(src, dst, ssem, rsem, where):
    return pltpu.make_async_remote_copy(
        src_ref=src, dst_ref=dst, send_sem=ssem, recv_sem=rsem,
        device_id=where, device_id_type=MESH,
    )


def routing_kernel(ids, gates, info, most, mine, theirs, ssem, rsem):
    e, s, d = (lax.axis_index(n) for n in ("expert", "seq", "dp"))
    seq_peers = [flip(s, 1), flip(s, 2), flip(flip(s, 1), 2)]
    z_peers = [flip(e, 1), flip(e, 2), flip(flip(e, 1), 2)]
    greet([{"seq": p} for p in seq_peers] + [{"expert": p} for p in z_peers] + [{"dp": 1 - d}])
    rows = info.shape[3]

    def line(ref):
        flat = jnp.concatenate([ref[0:1, :], ref[1:2, :]], axis=1).astype(jnp.float32)
        return jnp.broadcast_to(flat, (8, rows))

    info[e, s] = line(ids)
    info[e, 4] = line(gates)

    def seq_copy(i, slot):
        return send(info.at[e, s], info.at[e, slot], ssem.at[i], rsem.at[i], {"seq": seq_peers[i]})

    def z_copy(i, slot):
        return send(info.at[e], info.at[slot], ssem.at[3 + i], rsem.at[3 + i], {"expert": z_peers[i]})

    for i in range(3):
        seq_copy(i, s).start()
    for i in range(3):
        seq_copy(i, seq_peers[i]).wait_recv()
    for i in range(3):
        z_copy(i, e).start()
    for i in range(3):
        z_copy(i, z_peers[i]).wait_recv()
    top = jnp.zeros((1, 1), jnp.float32)
    for z in range(4):
        crossing = jnp.zeros((1, rows), jnp.float32)
        for b in range(4):
            high = (info[z, b, 0:1, :] >= 2.0).astype(jnp.float32)
            crossing = crossing + (high if z < 2 else 1.0 - high)
        top = jnp.maximum(top, jnp.sum(crossing, axis=1, keepdims=True))
    mine[...] = jnp.broadcast_to(top, (8, 128))
    last = send(mine, theirs, ssem.at[6], rsem.at[6], {"dp": 1 - d})
    last.start()
    last.wait()
    most[...] = jnp.maximum(mine[...], theirs[...])
    for i in range(3):
        seq_copy(i, s).wait_send()
        z_copy(i, e).wait_send()


def line_pieces(half):
    cut = min(384, half)
    return [(0, 0, cut), (0, cut, half - cut), (1, 0, half - 256), (1, half - 256, 256)]


def line_tiles(half):
    edges = sorted({0, half} | {p[1] for p in line_pieces(half)})
    return [
        (lo + t, min(256, hi - lo - t)) for lo, hi in zip(edges, edges[1:]) for t in range(0, hi - lo, 256)
    ]


def line_kernel(
    dims,
    info, go, q, k, v, hid,
    eg_out, gq_out, gk_out, gv_out,
    kbuf, vbuf, hraw, picks, hsend, hrecv, gsend, grecv,
    kpart, vpart, kown, vown, kin, vin, precv,
    kv_send, kv_recv, local_sem, raw_send, raw_recv, gz_send, gz_recv, gs_send, gs_recv,
    hz_send, hz_recv, relay_send, relay_recv, part_send, part_recv, pair_send, pair_recv,
):
    E, S, T, C, U, D, K = dims
    W = S * C
    half = U // 2
    rows = 2 * T
    packed = K < 2 * W
    both = 2 * W - K
    pieces = line_pieces(half)
    tiles = line_tiles(half)
    e, s, d = (lax.axis_index(n) for n in ("expert", "seq", "dp"))
    side = e // 2
    friend, across, corner = flip(e, 1), flip(e, 2), flip(flip(e, 1), 2)
    near, far = 2 - side, 3 - 3 * side
    inner = jnp.logical_or(e == 1, e == 2)
    outer = jnp.logical_not(inner)
    others = [2 - 2 * side, 3 - 2 * side]
    peers = [flip(s, 1), flip(s, 2), flip(flip(s, 1), 2)]
    bases = [pl.multiple_of((d if n else 1 - d) * half + o, 128) for n, o, _ in pieces]
    greet([{"seq": p} for p in peers] + [{"expert": p} for p in (friend, across, corner)] + [{"dp": 1 - d}])

    def cols(c):
        return pl.ds(bases[c], pieces[c][2])

    def kv_copy(n, i, slot):
        src, dst = ((k, kbuf), (v, vbuf))[n]
        return send(src, dst.at[slot], kv_send.at[n, i], kv_recv.at[n, i], {"seq": peers[i]})

    def raw_copy(c, i, slot):
        there = pl.ds(pl.multiple_of(peers[i] * U + bases[c], 128), pieces[c][2])
        return send(
            hid.at[:, :, there], hraw.at[slot, :, :, cols(c)],
            raw_send.at[c, i], raw_recv.at[c, i], {"seq": peers[i]},
        )

    def own_copy(c):
        here = pl.ds(pl.multiple_of(s * U + bases[c], 128), pieces[c][2])
        return pltpu.make_async_copy(hid.at[:, :, here], hraw.at[s, :, :, cols(c)], local_sem.at[c])

    def gz_copy(n, slot):
        src = go if n < 2 else gsend.at[across]
        dst = gsend.at[slot]
        to = across if n == 0 else friend
        return send(src, dst, gz_send.at[n], gz_recv.at[n], {"expert": to})

    gz_copy(0, e).start()
    gz_copy(1, e).start()
    for c in range(len(pieces)):
        own_copy(c).start()
        for i in range(3):
            raw_copy(c, i, s).start()
    for i in range(3):
        for n in range(2):
            kv_copy(n, i, s).start()
    kbuf[s] = k[...]
    vbuf[s] = v[...]

    col = lax.broadcasted_iota(jnp.int32, (rows, rows), 1)
    row = lax.broadcasted_iota(jnp.int32, (rows, rows), 0)
    f32, bf = jnp.float32, jnp.bfloat16
    experts = lax.broadcasted_iota(jnp.int32, (8, rows), 0).astype(f32)
    by_place = (col < row).astype(bf)
    interleave = (row == lax.rem(col, 2) * T + col // 2).astype(bf)
    in_order = (row < col).astype(bf)
    k_order = (2 * lax.rem(row, T) + row // T < 2 * lax.rem(col, T) + col // T).astype(bf)

    def ranked(ids, earlier):
        onehot = (experts == ids).astype(f32)
        return onehot, dot(onehot.astype(bf), earlier, ((1,), (0,)))

    total = 2 * W + K
    offsets = jnp.zeros((8, 1), f32)
    places = lax.broadcasted_iota(jnp.int32, (total, rows), 0).astype(f32)
    for b in range(S):
        ids = dot(info[e, b].astype(bf), interleave, ((1,), (0,)))[0:1, :]
        onehot, before = ranked(ids, in_order)
        start = offsets if packed else float(C * b)
        rank = jnp.sum(onehot * (before + start), axis=0, keepdims=True)
        offsets = offsets + jnp.sum(onehot, axis=1, keepdims=True)
        back = (W + K - 1) - rank if packed else K + rank
        code = jnp.where(
            ids == friend.astype(f32), rank,
            jnp.where(
                ids == e.astype(f32), W + K + rank,
                jnp.where(ids == near.astype(f32), W + rank, back),
            ),
        )
        picks[:, b * rows : (b + 1) * rows] = (places == code).astype(bf)

    def gs_copy(z, n):
        to = peers[0] if n in (0, 3) else peers[1]
        slot = (s, s, peers[0], peers[1])[n]
        lanes = (slice(0, D), slice(0, D), slice(0, D // 2), slice(D // 2, D))[n]
        block = grecv.at[z, slot, :, lanes]
        return send(block, block, gs_send.at[z, n], gs_recv.at[z, n], {"seq": to})

    def gs_wait(z, n):
        slot = (peers[0], peers[1], peers[2], peers[2])[n]
        lanes = (slice(0, D), slice(0, D), slice(0, D // 2), slice(D // 2, D))[n]
        block = grecv.at[z, slot, :, lanes]
        send(block, block, gs_send.at[z, n], gs_recv.at[z, n], {"seq": peers[0]}).wait_recv()

    wanted = lax.broadcasted_iota(jnp.int32, (C, rows), 0).astype(f32)

    def forward(z, grads):
        ids = info[z, pl.ds(s, 1)][0, 0:1, :]
        onehot, before = ranked(ids, k_order)
        rank = jnp.sum(before * onehot, axis=0, keepdims=True)
        code = jnp.where(ids == e.astype(f32), rank, -1.0)
        chosen = (wanted == code).astype(f32)
        gate = jnp.sum(chosen * info[z, 4, 0:1, :], axis=1, keepdims=True)
        token = (chosen[:, :T] + chosen[:, T:]).astype(bf)
        grecv[z, pl.ds(s, 1)] = (dot(token, grads, ((1,), (0,))) * gate).astype(bf)[None]
        for n in range(2):
            gs_copy(z, n).start()

    def pass_on(z):
        for n in range(2):
            gs_wait(z, n)
            gs_copy(z, 2 + n).start()

    def hz_parts(c):
        units = cols(c)
        return (
            (friend, hsend.at[0:W, units], hrecv.at[e, 0:W, units]),
            (near, hsend.at[W : 2 * W, units], hrecv.at[e, 0:W, units]),
            (far, hsend.at[2 * W : W + K, units], hrecv.at[e, both:W, units]),
        )

    def hz_copy(c, n):
        to, src, dst = hz_parts(c)[n]
        return send(src, dst, hz_send.at[c, n], hz_recv.at[c, e], {"expert": to})

    def hz_wait(c, z, low):
        block = hrecv.at[z, low:W, cols(c)]
        send(block, block, hz_send.at[c, 0], hz_recv.at[c, z], {"expert": friend}).wait_recv()

    def relay_copy(c, z):
        return send(
            hrecv.at[z, K - W : W, cols(c)], hrecv.at[z, 0:both, cols(c)],
            relay_send.at[c, z], relay_recv.at[c, z], {"expert": friend},
        )

    def pack(c):
        own_copy(c).wait()
        for i in range(3):
            raw_copy(c, i, peers[i]).wait_recv()
        width = pieces[c][2]
        for t in range(0, width, 256):
            units = pl.ds(pl.multiple_of(bases[c] + t, 128), min(256, width - t))
            block = hraw[:, :, :, units].reshape(S * rows, min(256, width - t))
            hsend[:, units] = dot(picks[0 : W + K, :], block, ((1,), (0,))).astype(bf)
            hrecv[pl.ds(e, 1), :, units] = dot(picks[W + K :, :], block, ((1,), (0,))).astype(bf)[None]
        for n in range(3):
            hz_copy(c, n).start()

    def relay(c):
        @pl.when(inner)
        def _():
            for z in others:
                hz_wait(c, z, 0)
                if packed:
                    relay_copy(c, z).start()

    def arrived(c):
        hz_wait(c, friend, 0)

        @pl.when(outer)
        def _():
            for z in others:
                hz_wait(c, z, both)
                if packed:
                    relay_copy(c, z).wait_recv()

    scale = HEAD_DIM ** (-0.5)
    length = S * T

    def attention(j):
        lanes = slice(j * HEAD_DIM, (j + 1) * HEAD_DIM)
        heads = [slice(h * HEAD_DIM, (h + 1) * HEAD_DIM) for h in range(j * GROUP, (j + 1) * GROUP)]
        qs = jnp.concatenate([q[:, h] for h in heads], axis=0)
        gs = jnp.concatenate([go[:, h] for h in heads], axis=0)
        kj = kbuf[:, :, lanes].reshape(length, HEAD_DIM)
        vj = vbuf[:, :, lanes].reshape(length, HEAD_DIM)
        scores = dot(qs, kj, ((1,), (1,))) * scale
        raised = jnp.exp(scores - jnp.max(scores, axis=-1, keepdims=True))
        probs = raised / jnp.sum(raised, axis=-1, keepdims=True)
        dprobs = dot(gs, vj, ((1,), (1,)))
        delta = jnp.sum(probs * dprobs, axis=-1, keepdims=True)
        ds = (probs * (dprobs - delta)).astype(jnp.bfloat16)
        dv = dot(probs.astype(jnp.bfloat16), gs, ((0,), (0,)))
        dk = dot(ds, qs, ((0,), (0,))) * scale
        dq = dot(ds, kj, ((1,), (0,))) * scale
        for n, h in enumerate(heads):
            gq_out[:, h] = dq[n * T : (n + 1) * T].astype(jnp.bfloat16)
        dk = dk.reshape(S, T, HEAD_DIM)
        dv = dv.reshape(S, T, HEAD_DIM)
        kown[:, :, lanes] = dk
        vown[:, :, lanes] = dv
        kpart[:, :, lanes] = dk.astype(jnp.bfloat16)
        vpart[:, :, lanes] = dv.astype(jnp.bfloat16)

    pack(0)
    forward(e, go[...])
    pack(1)
    gz_copy(0, across).wait_recv()
    gz_copy(2, across).start()
    forward(across, gsend[across])
    pack(2)
    gz_copy(1, friend).wait_recv()
    forward(friend, gsend[friend])
    pack(3)
    for i in range(3):
        for n in range(2):
            kv_copy(n, i, peers[i]).wait_recv()
    attention(0)
    relay(0)
    gz_copy(2, corner).wait_recv()
    forward(corner, gsend[corner])
    attention(1)
    pass_on(e)
    attention(2)
    relay(1)
    attention(3)

    def part_copy(n, i, slot):
        src, dst = ((kpart, kin), (vpart, vin))[n]
        return send(src.at[peers[i]], dst.at[slot], part_send.at[n, i], part_recv.at[n, i], {"seq": peers[i]})

    for i in range(3):
        for n in range(2):
            part_copy(n, i, s).start()
    pass_on(across)
    pass_on(friend)
    pass_on(corner)
    for n, (own, got, out) in enumerate(((kown, kin, gk_out), (vown, vin, gv_out))):
        summed = own[s]
        for i in range(3):
            part_copy(n, i, peers[i]).wait_recv()
            summed = summed + got[peers[i]].astype(jnp.float32)
        out[...] = summed.astype(jnp.bfloat16)

    def settle(z):
        for n in (2, 3):
            gs_wait(z, n)
        for n in range(4):
            gs_copy(z, n).wait_send()
        if not packed:
            return
        slots = lax.broadcasted_iota(jnp.int32, (1, W), 1).astype(f32)
        code = jnp.full((1, W), -1.0, f32)
        start = jnp.zeros((1, 1), f32)
        for b in range(S):
            named = (info[z, b, 0:1, :] == e.astype(f32)).astype(f32)
            count = jnp.sum(named, axis=1, keepdims=True)
            inside = jnp.logical_and(slots >= float(C * b), slots - float(C * b) < count)
            inside = jnp.logical_and(inside, slots < float(C * (b + 1)))
            code = jnp.where(inside, slots - float(C * b) + start, code)
            start = start + count
        turned = jnp.logical_and(z // 2 != side, outer).astype(f32)
        code = jnp.where(code >= 0.0, code + turned * (float(W - 1) - 2.0 * code), code)
        moves = (lax.broadcasted_iota(jnp.int32, (W, W), 0).astype(f32) == code).astype(bf)
        for t in range(0, D, 512):
            block = grecv[z, :, :, t : t + 512].reshape(W, 512)
            grecv[z, :, :, t : t + 512] = dot(moves, block, ((1,), (0,))).astype(bf).reshape(S, C, 512)

    for z in (e, across, friend, corner):
        settle(z)

    def product(base, off, width):
        units = pl.ds(pl.multiple_of(base + off, 128), width)
        h = hrecv[:, :, units].reshape(E * W, width)
        return dot(h, grecv[...].reshape(E * W, D), ((0,), (0,)))

    def pair_copy(n):
        off, width = tiles[n]
        return send(eg_out.at[off : off + width], precv.at[off : off + width], pair_send.at[n], pair_recv.at[n], {"dp": 1 - d})

    for c, (m, o, w) in enumerate(pieces):
        if c >= 2:
            relay(c)
        arrived(c)
        for n, (off, width) in enumerate(tiles):
            if off < o or off >= o + w:
                continue
            if m == 0:
                eg_out[off : off + width, :] = product((1 - d) * half, off, width).astype(jnp.bfloat16)
                pair_copy(n).start()
            else:
                mine = product(d * half, off, width)
                pair_copy(n).wait_recv()
                pair_copy(n).wait_send()
                got = precv[off : off + width, :].astype(jnp.float32)
                eg_out[off : off + width, :] = (mine + got).astype(jnp.bfloat16)

    for i in range(3):
        for n in range(2):
            kv_copy(n, i, s).wait_send()
            part_copy(n, i, s).wait_send()
        gz_copy(i, across if i == 2 else e).wait_send()
    for c in range(len(pieces)):
        for i in range(3):
            raw_copy(c, i, s).wait_send()
            hz_copy(c, i).wait_send()
    if packed:

        @pl.when(inner)
        def _():
            for c in range(len(pieces)):
                for z in others:
                    relay_copy(c, z).wait_send()


def line_call(K, number, info, grad_out, queries, keys, values, hidden):
    E, S = lax.axis_size("expert"), lax.axis_size("seq")
    T, D = grad_out.shape
    U = hidden.shape[2] // S
    C = -(-(7 * T // (2 * E)) // 16) * 16
    KD = keys.shape[1]
    W, rows, half = S * C, 2 * T, U // 2
    bf, f32 = jnp.bfloat16, jnp.float32
    vm = pl.BlockSpec(memory_space=pltpu.VMEM)
    dma = pltpu.SemaphoreType.DMA
    P_ = len(line_pieces(half))
    tiles = len(line_tiles(half))
    return pl.pallas_call(
        functools.partial(line_kernel, (E, S, T, C, U, D, K)),
        out_shape=(
            jax.ShapeDtypeStruct((half, D), bf),
            jax.ShapeDtypeStruct((T, D), bf),
            jax.ShapeDtypeStruct((T, KD), bf),
            jax.ShapeDtypeStruct((T, KD), bf),
        ),
        in_specs=[vm] * 5 + [pl.BlockSpec(memory_space=pl.ANY)],
        out_specs=(vm,) * 4,
        scratch_shapes=[
            pltpu.VMEM((S, T, KD), bf),
            pltpu.VMEM((S, T, KD), bf),
            pltpu.VMEM((S, T, 2, U), bf),
            pltpu.VMEM((2 * W + K, S * rows), bf),
            pltpu.VMEM((W + K, U), bf),
            pltpu.VMEM((E, W, U), bf),
            pltpu.VMEM((E, T, D), bf),
            pltpu.VMEM((E, S, C, D), bf),
            pltpu.VMEM((S, T, KD), bf),
            pltpu.VMEM((S, T, KD), bf),
            pltpu.VMEM((S, T, KD), f32),
            pltpu.VMEM((S, T, KD), f32),
            pltpu.VMEM((S, T, KD), bf),
            pltpu.VMEM((S, T, KD), bf),
            pltpu.VMEM((half, D), bf),
            dma((2, 3)), dma((2, 3)), dma((P_,)), dma((P_, 3)), dma((P_, 3)), dma((3,)), dma((3,)),
            dma((E, 4)), dma((E, 4)), dma((P_, 3)), dma((P_, E)), dma((P_, E)), dma((P_, E)),
            dma((2, 3)), dma((2, 3)), dma((tiles,)), dma((tiles,)),
        ],
        compiler_params=pltpu.CompilerParams(
            collective_id=number, has_side_effects=True, vmem_limit_bytes=62 * 1024 * 1024
        ),
    )(info, grad_out, queries, keys, values, hidden)


def on_line(grad_out, expert_ids, gate_weights, hidden, queries, keys, values):
    E, S = lax.axis_size("expert"), lax.axis_size("seq")
    T = grad_out.shape[1]
    C = -(-(7 * T // (2 * E)) // 16) * 16
    rows = 2 * T
    f32 = jnp.float32
    vm = pl.BlockSpec(memory_space=pltpu.VMEM)
    dma = pltpu.SemaphoreType.DMA
    info, most = pl.pallas_call(
        routing_kernel,
        out_shape=(
            jax.ShapeDtypeStruct((E, S + 1, 8, rows), f32),
            jax.ShapeDtypeStruct((8, 128), f32),
        ),
        in_specs=[vm] * 2,
        out_specs=(vm,) * 2,
        scratch_shapes=[pltpu.VMEM((8, 128), f32), pltpu.VMEM((8, 128), f32), dma((7,)), dma((7,))],
        compiler_params=pltpu.CompilerParams(collective_id=0, has_side_effects=True),
    )(expert_ids[0].T, gate_weights[0].T)
    operands = (info, grad_out[0], queries[0], keys[0], values[0], hidden[0])
    full = 2 * S * C
    tight = full * 6 // 7 // 16 * 16
    eg, gq, gk, gv = lax.cond(
        most[0, 0] <= float(tight),
        functools.partial(line_call, tight, 1),
        functools.partial(line_call, full, 2),
        *operands,
    )
    return (eg[None], gq[None], gk[None], gv[None])


def solution(mesh):
    split = P(("expert", "dp"), "seq", None)
    in_specs = (split, split, split, P(("expert", "dp"), "seq", None, None), split, split, split)
    out_specs = (P("expert", ("seq", "dp"), None), split, split, split)
    body = on_line if mesh.shape["expert"] == 4 and mesh.shape["seq"] == 4 else on_device
    return jax.shard_map(
        body, mesh=mesh, in_specs=in_specs, out_specs=out_specs, check_vma=False
    )
```

```python
import functools

import jax
import jax.numpy as jnp
from jax import lax
from jax.experimental import pallas as pl
from jax.experimental.pallas import tpu as pltpu
from jax.sharding import PartitionSpec as P

HEADS = 16
KV_HEADS = 4
HEAD_DIM = 128
GROUP = HEADS // KV_HEADS
MESH = pl.DeviceIdType.MESH


def dot(a, b, contract):
    return lax.dot_general(a, b, (contract, ((), ())), preferred_element_type=jnp.float32)


def routing_codes(ids, order_row, order_col, experts, capacity):
    count = max(8, experts)
    rows = ids.shape[1]
    expert_of = lax.broadcasted_iota(jnp.int32, (count, rows), 0).astype(jnp.float32)
    onehot = (expert_of == ids).astype(jnp.float32)
    earlier = (order_col < order_row).astype(jnp.float32)
    before = dot(onehot.astype(jnp.bfloat16), earlier.astype(jnp.bfloat16), ((1,), (0,)))
    slot = jnp.sum(before * onehot, axis=0, keepdims=True)
    return ids * float(capacity) + slot


def spreads(experts):
    return experts <= 8 and experts & (experts - 1) == 0


def kernel(
    dims,
    ids_t, info, go, q, k, v, hid,
    eg_out, gq_out, gk_out, gv_out,
    kbuf, vbuf, idbuf, hraw, hsend, hrecv, gsend, grecv, infos,
    kpart, vpart, kown, vown, kin, vin, precv,
    small_send, small_recv, local_sem, hraw_send, hraw_recv,
    gz_send, gz_recv, gi_send, gi_recv, gs_send, gs_recv, hz_send, hz_recv,
    part_send, part_recv, pair_send, pair_recv,
):
    E, S, T, C, U, D = dims
    half = U // 2
    first = -(-half // 256) * 128
    pieces = [(n, o, w) for n in range(2) for o, w in ((0, first), (first, half - first)) if w > 0]
    spread = spreads(E)
    e = lax.axis_index("expert")
    s = lax.axis_index("seq")
    d = lax.axis_index("dp")
    seq_peer = [lax.rem(s + i, S) for i in range(S)]
    bases = [
        pl.multiple_of((d if n else 1 - d) * half + o, 128) for n, o, _ in pieces
    ]

    def ex_peer(j):
        return lax.rem(e + j, E)

    barrier = pltpu.get_barrier_semaphore()
    for i in range(1, S):
        pl.semaphore_signal(barrier, inc=1, device_id={"seq": seq_peer[i]}, device_id_type=MESH)

    @pl.loop(1, E)
    def _(j):
        pl.semaphore_signal(barrier, inc=1, device_id={"expert": ex_peer(j)}, device_id_type=MESH)

    pl.semaphore_signal(barrier, inc=1, device_id={"dp": 1 - d}, device_id_type=MESH)
    pl.semaphore_wait(barrier, S + E - 1)

    def send(src, dst, ssem, rsem, where):
        return pltpu.make_async_remote_copy(
            src_ref=src, dst_ref=dst, send_sem=ssem, recv_sem=rsem,
            device_id=where, device_id_type=MESH,
        )

    def small_copy(n, i, slot):
        src, dst = ((ids_t, idbuf), (k, kbuf), (v, vbuf))[n]
        return send(src, dst.at[slot], small_send.at[n, i], small_recv.at[n, slot], {"seq": seq_peer[i]})

    def raw_copy(c, i, slot):
        width = pieces[c][2]
        cols = pl.ds(pl.multiple_of(seq_peer[i] * U + bases[c], 128), width)
        return send(
            hid.at[:, :, cols], hraw.at[slot, :, :, pl.ds(bases[c], width)],
            hraw_send.at[c, i], hraw_recv.at[c, slot], {"seq": seq_peer[i]},
        )

    own_cols = pl.ds(pl.multiple_of(s * U, 128), U)
    own_raw = pltpu.make_async_copy(hid.at[:, :, own_cols], hraw.at[s], local_sem.at[0])
    own_raw.start()
    for i in range(1, S):
        for n in range(3):
            small_copy(n, i, s).start()
    for c in range(len(pieces)):
        for i in range(1, S):
            raw_copy(c, i, s).start()
    kbuf[s] = k[...]
    vbuf[s] = v[...]
    idbuf[s] = ids_t[...]

    rows = 2 * T
    col = lax.broadcasted_iota(jnp.int32, (rows, rows), 1)
    row = lax.broadcasted_iota(jnp.int32, (rows, rows), 0)
    place = lax.broadcasted_iota(jnp.int32, (E * C, rows), 0).astype(jnp.float32)

    def expert_rows(p):
        return pl.ds(pl.multiple_of(p * C, 16), C)

    def gs_copy(i, z, slot):
        return send(grecv.at[s, z], grecv.at[slot, z], gs_send.at[i, z], gs_recv.at[slot, z], {"seq": seq_peer[i]})

    def gs_wait(i, z):
        slot = seq_peer[i]
        send(grecv.at[s, z], grecv.at[slot, z], gs_send.at[i, z], gs_recv.at[slot, z], {"seq": slot}).wait_recv()

    def packed_grads(ids, gates, grads, wanted):
        code = routing_codes(
            ids, 2 * lax.rem(col, T) + col // T, 2 * lax.rem(row, T) + row // T, E, C
        )
        picks = (wanted == code).astype(jnp.float32)
        gate = jnp.sum(picks * gates, axis=1, keepdims=True)
        token_picks = (picks[:, :T] + picks[:, T:]).astype(jnp.bfloat16)
        return (dot(token_picks, grads, ((1,), (0,))) * gate).astype(jnp.bfloat16)

    if spread:
        def flip(at, b):
            return at + b - 2 * b * lax.rem(at // b, 2)

        bits = []
        b = E // 2
        while b >= 1:
            bits.append(b)
            b //= 2

        def masks(n):
            held = [0]
            for bit in bits[:n]:
                held = held + [m + bit for m in held]
            return held

        def at_mask(m):
            at = e
            for bit in bits:
                if m & bit:
                    at = flip(at, bit)
            return at

        def gz_pair(m, n, slot):
            to = {"expert": flip(e, bits[n])}
            key = m + bits[n]
            return (
                send(gsend.at[slot], gsend.at[slot], gz_send.at[key], gz_recv.at[slot], to),
                send(infos.at[slot], infos.at[slot], gi_send.at[key], gi_recv.at[slot], to),
            )

        def forward(m):
            z = at_mask(m)
            wanted = (
                lax.broadcasted_iota(jnp.int32, (C, rows), 0) + e * C
            ).astype(jnp.float32)
            grecv[s, z] = packed_grads(infos[z, 0:1, :], infos[z, 8:9, :], gsend[z], wanted)
            for i in range(1, S):
                gs_copy(i, z, s).start()

        def arrive(m, n):
            for copy in gz_pair(m, n, at_mask(m + bits[n])):
                copy.wait_recv()
            for later in range(n + 1, len(bits)):
                for copy in gz_pair(m + bits[n], later, at_mask(m + bits[n])):
                    copy.start()

        gsend[e] = go[...]
        infos[e] = info[...]
        for n in range(len(bits)):
            for copy in gz_pair(0, n, e):
                copy.start()
    else:

        def gz_copy(j, slot):
            p = ex_peer(j)
            return send(gsend.at[expert_rows(p)], grecv.at[s, slot], gz_send.at[j], gz_recv.at[slot], {"expert": p})

        gsend[...] = packed_grads(info[0:1, :], info[8:9, :], go[...], place)

        @pl.loop(1, E)
        def _(j):
            gz_copy(j, e).start()

        grecv[s, e] = gsend[expert_rows(e)]
        for i in range(1, S):
            gs_copy(i, e, s).start()

    def hz_copy(c, i, j, slot):
        p = ex_peer(j)
        src = seq_peer[i]
        units = pl.ds(bases[c], pieces[c][2])
        return send(
            hsend.at[src, expert_rows(p), units], hrecv.at[src, slot, :, units],
            hz_send.at[c, src, j], hz_recv.at[c, src, slot], {"expert": p},
        )

    def pack_hidden(c, i):
        src = seq_peer[i]
        width = pieces[c][2]
        units = pl.ds(bases[c], width)
        hcode = routing_codes(idbuf[src, 0:1, :], col, row, E, C)
        hpicks = (place == hcode).astype(jnp.bfloat16)
        hsend[src, :, units] = dot(
            hpicks, hraw[src, :, :, units].reshape(rows, width), ((1,), (0,))
        ).astype(jnp.bfloat16)

        @pl.loop(1, E)
        def _(j):
            hz_copy(c, i, j, e).start()

        hrecv[src, e, :, units] = hsend[src, expert_rows(e), units]

    own_raw.wait()
    for c in range(len(pieces)):
        pack_hidden(c, 0)
    if spread:
        forward(0)

    scale = HEAD_DIM ** (-0.5)
    length = S * T

    def attention(j):
        lanes = slice(j * HEAD_DIM, (j + 1) * HEAD_DIM)
        heads = [slice(h * HEAD_DIM, (h + 1) * HEAD_DIM) for h in range(j * GROUP, (j + 1) * GROUP)]
        qs = jnp.concatenate([q[:, h] for h in heads], axis=0)
        gs = jnp.concatenate([go[:, h] for h in heads], axis=0)
        kj = kbuf[:, :, lanes].reshape(length, HEAD_DIM)
        vj = vbuf[:, :, lanes].reshape(length, HEAD_DIM)
        scores = dot(qs, kj, ((1,), (1,))) * scale
        raised = jnp.exp(scores - jnp.max(scores, axis=-1, keepdims=True))
        probs = raised / jnp.sum(raised, axis=-1, keepdims=True)
        dprobs = dot(gs, vj, ((1,), (1,)))
        delta = jnp.sum(probs * dprobs, axis=-1, keepdims=True)
        ds = (probs * (dprobs - delta)).astype(jnp.bfloat16)
        dv = dot(probs.astype(jnp.bfloat16), gs, ((0,), (0,)))
        dk = dot(ds, qs, ((0,), (0,))) * scale
        dq = dot(ds, kj, ((1,), (0,))) * scale
        for n, h in enumerate(heads):
            gq_out[:, h] = dq[n * T : (n + 1) * T].astype(jnp.bfloat16)
        dk = dk.reshape(S, T, HEAD_DIM)
        dv = dv.reshape(S, T, HEAD_DIM)
        kown[:, :, lanes] = dk
        vown[:, :, lanes] = dv
        kpart[:, :, lanes] = dk.astype(jnp.bfloat16)
        vpart[:, :, lanes] = dv.astype(jnp.bfloat16)

    for i in range(1, S):
        for n in range(3):
            small_copy(n, i, seq_peer[i]).wait_recv()

    attention(0)

    if spread:
        attention(1)
        for n in range(len(bits)):
            for m in masks(n):
                arrive(m, n)
                forward(m + bits[n])
    else:

        @pl.loop(1, E)
        def _(j):
            z = ex_peer(j)
            gz_copy(j, z).wait_recv()
            for i in range(1, S):
                gs_copy(i, z, s).start()

        attention(1)
    for c in range(len(pieces)):
        for i in range(1, S):
            raw_copy(c, i, seq_peer[i]).wait_recv()
            pack_hidden(c, i)
        if c + 2 < KV_HEADS:
            attention(c + 2)
    for j in range(len(pieces) + 2, KV_HEADS):
        attention(j)

    def part_copy(n, i, slot):
        src, dst = ((kpart, kin), (vpart, vin))[n]
        return send(src.at[seq_peer[i]], dst.at[slot], part_send.at[n, i], part_recv.at[n, slot], {"seq": seq_peer[i]})

    for i in range(1, S):
        for n in range(2):
            part_copy(n, i, s).start()
    for n, (own, got, out) in enumerate(((kown, kin, gk_out), (vown, vin, gv_out))):
        total = own[s]
        for i in range(1, S):
            part_copy(n, i, seq_peer[i]).wait_recv()
            total = total + got[seq_peer[i]].astype(jnp.float32)
        out[...] = total.astype(jnp.bfloat16)

    @pl.loop(0, E)
    def _(z):
        for i in range(1, S):
            gs_wait(i, z)

    wide = 256
    tiles = [
        (o + t, min(wide, w - t)) for n, o, w in pieces if n == 0 for t in range(0, w, wide)
    ]

    def arrived(n, off):
        for c, (m, o, _) in enumerate(pieces):
            if m == n and o == off:

                @pl.loop(1, E)
                def _(j):
                    for i in range(S):
                        hz_copy(c, i, j, ex_peer(j)).wait_recv()

    def product(base, off, width):
        units = pl.ds(pl.multiple_of(base + off, 128), width)
        h = hrecv[:, :, :, units].reshape(S * E * C, width)
        return dot(h, grecv[...].reshape(S * E * C, D), ((0,), (0,)))

    def pair_copy(n):
        off, width = tiles[n]
        return send(eg_out.at[off : off + width], precv.at[off : off + width], pair_send.at[n], pair_recv.at[n], {"dp": 1 - d})

    for n, (off, width) in enumerate(tiles):
        arrived(0, off)
        eg_out[off : off + width, :] = product((1 - d) * half, off, width).astype(jnp.bfloat16)
        pair_copy(n).start()
    for n, (off, width) in enumerate(tiles):
        arrived(1, off)
        mine = product(d * half, off, width)
        pair_copy(n).wait_recv()
        pair_copy(n).wait_send()
        got = precv[off : off + width, :].astype(jnp.float32)
        eg_out[off : off + width, :] = (mine + got).astype(jnp.bfloat16)

    for i in range(1, S):
        for n in range(3):
            small_copy(n, i, s).wait_send()
        for n in range(2):
            part_copy(n, i, s).wait_send()
        for c in range(len(pieces)):
            raw_copy(c, i, s).wait_send()

    @pl.loop(0, E)
    def _(z):
        for i in range(1, S):
            gs_copy(i, z, s).wait_send()

    @pl.loop(1, E)
    def _(j):
        if not spread:
            gz_copy(j, e).wait_send()
        for i in range(S):
            for c in range(len(pieces)):
                hz_copy(c, i, j, e).wait_send()

    if spread:
        for n in range(len(bits)):
            for m in masks(n):
                for copy in gz_pair(m, n, at_mask(m)):
                    copy.wait_send()


def on_device(grad_out, expert_ids, gate_weights, hidden, queries, keys, values):
    E = lax.axis_size("expert")
    S = lax.axis_size("seq")
    T = grad_out.shape[1]
    D = grad_out.shape[2]
    U = hidden.shape[3] // S
    C = -(-(7 * T // (2 * E)) // 16) * 16
    KD = keys.shape[2]
    rows = 2 * T
    bf, f32 = jnp.bfloat16, jnp.float32
    ids = expert_ids[0].astype(f32)
    ids_t = jnp.broadcast_to(ids.reshape(1, rows), (8, rows))
    ids_k = jnp.broadcast_to(ids.T.reshape(1, rows), (8, rows))
    gates_k = jnp.broadcast_to(gate_weights[0].T.reshape(1, rows), (8, rows))
    tiles = -(-(U // 2) // 256)
    info = jnp.concatenate([ids_k, gates_k], axis=0)
    sent = (E, T, D) if spreads(E) else (E * C, D)
    vm = pl.BlockSpec(memory_space=pltpu.VMEM)
    dma = pltpu.SemaphoreType.DMA
    eg, gq, gk, gv = pl.pallas_call(
        functools.partial(kernel, (E, S, T, C, U, D)),
        out_shape=(
            jax.ShapeDtypeStruct((U // 2, D), bf),
            jax.ShapeDtypeStruct((T, queries.shape[2]), bf),
            jax.ShapeDtypeStruct((T, KD), bf),
            jax.ShapeDtypeStruct((T, KD), bf),
        ),
        in_specs=[vm] * 6 + [pl.BlockSpec(memory_space=pl.ANY)],
        out_specs=(vm,) * 4,
        scratch_shapes=[
            pltpu.VMEM((S, T, KD), bf),
            pltpu.VMEM((S, T, KD), bf),
            pltpu.VMEM((S, 8, rows), f32),
            pltpu.VMEM((S, T, 2, U), bf),
            pltpu.VMEM((S, E * C, U), bf),
            pltpu.VMEM((S, E, C, U), bf),
            pltpu.VMEM(sent, bf),
            pltpu.VMEM((S, E, C, D), bf),
            pltpu.VMEM((E if spreads(E) else 1, 16, rows), f32),
            pltpu.VMEM((S, T, KD), bf),
            pltpu.VMEM((S, T, KD), bf),
            pltpu.VMEM((S, T, KD), f32),
            pltpu.VMEM((S, T, KD), f32),
            pltpu.VMEM((S, T, KD), bf),
            pltpu.VMEM((S, T, KD), bf),
            pltpu.VMEM((U // 2, D), bf),
            dma((3, S)), dma((3, S)), dma((1,)), dma((4, S)), dma((4, S)),
            dma((E,)), dma((E,)), dma((E,)), dma((E,)), dma((S, E)), dma((S, E)), dma((4, S, E)), dma((4, S, E)),
            dma((2, S)), dma((2, S)), dma((tiles,)), dma((tiles,)),
        ],
        compiler_params=pltpu.CompilerParams(
            collective_id=0, has_side_effects=True, vmem_limit_bytes=62 * 1024 * 1024
        ),
    )(ids_t, info, grad_out[0], queries[0], keys[0], values[0], hidden[0])
    return (eg[None], gq[None], gk[None], gv[None])


def flip(at, b):
    return at + b - 2 * b * lax.rem(at // b, 2)


def greet(peers):
    barrier = pltpu.get_barrier_semaphore()
    for peer in peers:
        pl.semaphore_signal(barrier, inc=1, device_id=peer, device_id_type=MESH)
    pl.semaphore_wait(barrier, len(peers))


def send(src, dst, ssem, rsem, where):
    return pltpu.make_async_remote_copy(
        src_ref=src, dst_ref=dst, send_sem=ssem, recv_sem=rsem,
        device_id=where, device_id_type=MESH,
    )


def line_pieces(half):
    cut = min(384, half)
    return [(0, 0, cut), (0, cut, half - cut), (1, 0, half - 256), (1, half - 256, 256)]


def line_tiles(half):
    edges = sorted({0, half} | {p[1] for p in line_pieces(half)})
    return [
        (lo + t, min(256, hi - lo - t)) for lo, hi in zip(edges, edges[1:]) for t in range(0, hi - lo, 256)
    ]


def line_kernel(
    dims,
    ids_in, gates_in, go, q, k, v, hid,
    eg_out, gq_out, gk_out, gv_out, most,
    info, peak, peak_in,
    kbuf, vbuf, hraw, picks, hsend, hrecv, gsend, grecv,
    kpart, vpart, kown, vown, kin, vin, precv,
    kv_send, kv_recv, local_sem, raw_send, raw_recv, gz_send, gz_recv, gs_send, gs_recv,
    hz_send, hz_recv, shared_recv, relay_send, relay_recv, part_send, part_recv, pair_send, pair_recv,
    info_send, info_recv,
):
    E, S, T, C, U, D, K = dims
    W = S * C
    half = U // 2
    rows = 2 * T
    packed = K < 2 * W
    parts = range(0 if packed else 1, 4)
    both = 2 * W - K
    pieces = line_pieces(half)
    tiles = line_tiles(half)
    e, s, d = (lax.axis_index(n) for n in ("expert", "seq", "dp"))
    side = e // 2
    friend, across, corner = flip(e, 1), flip(e, 2), flip(flip(e, 1), 2)
    near, far = 2 - side, 3 - 3 * side
    inner = jnp.logical_or(e == 1, e == 2)
    outer = jnp.logical_not(inner)
    others = [2 - 2 * side, 3 - 2 * side]
    peers = [flip(s, 1), flip(s, 2), flip(flip(s, 1), 2)]
    bases = [pl.multiple_of((d if n else 1 - d) * half + o, 128) for n, o, _ in pieces]
    greet([{"seq": p} for p in peers] + [{"expert": p} for p in (friend, across, corner)] + [{"dp": 1 - d}])

    def cols(c):
        return pl.ds(bases[c], pieces[c][2])

    def kv_copy(n, i, slot):
        src, dst = ((k, kbuf), (v, vbuf))[n]
        return send(src, dst.at[slot], kv_send.at[n, i], kv_recv.at[n, i], {"seq": peers[i]})

    def raw_copy(c, i, slot):
        there = pl.ds(pl.multiple_of(peers[i] * U + bases[c], 128), pieces[c][2])
        return send(
            hid.at[:, :, there], hraw.at[slot, :, :, cols(c)],
            raw_send.at[c, i], raw_recv.at[c, i], {"seq": peers[i]},
        )

    def own_copy(c):
        here = pl.ds(pl.multiple_of(s * U + bases[c], 128), pieces[c][2])
        return pltpu.make_async_copy(hid.at[:, :, here], hraw.at[s, :, :, cols(c)], local_sem.at[c])

    def gz_copy(n, slot):
        src = go if n < 2 else gsend.at[across]
        dst = gsend.at[slot]
        to = across if n == 0 else friend
        return send(src, dst, gz_send.at[n], gz_recv.at[n], {"expert": to})

    z_peers = [friend, across, corner]

    def line(ref):
        flat = jnp.concatenate([ref[0:1, :], ref[1:2, :]], axis=1).astype(jnp.float32)
        return jnp.broadcast_to(flat, (1, 8, rows))

    def info_copy(i, slot):
        if i < 3:
            return send(info.at[e, s], info.at[e, slot], info_send.at[i], info_recv.at[i], {"seq": peers[i]})
        return send(info.at[e], info.at[slot], info_send.at[i], info_recv.at[i], {"expert": z_peers[i - 3]})

    info[e, pl.ds(s, 1)] = line(ids_in)
    info[e, S : S + 1] = line(gates_in)
    for i in range(3):
        info_copy(i, s).start()
    gz_copy(0, e).start()
    gz_copy(1, e).start()
    for c in range(len(pieces)):
        own_copy(c).start()
        for i in range(3):
            raw_copy(c, i, s).start()
    for i in range(3):
        for n in range(2):
            kv_copy(n, i, s).start()
    kbuf[s] = k[...]
    vbuf[s] = v[...]

    col = lax.broadcasted_iota(jnp.int32, (rows, rows), 1)
    row = lax.broadcasted_iota(jnp.int32, (rows, rows), 0)
    f32, bf = jnp.float32, jnp.bfloat16
    experts = lax.broadcasted_iota(jnp.int32, (8, rows), 0).astype(f32)
    by_place = (col < row).astype(bf)
    interleave = (row == lax.rem(col, 2) * T + col // 2).astype(bf)
    in_order = (row < col).astype(bf)
    k_order = (2 * lax.rem(row, T) + row // T < 2 * lax.rem(col, T) + col // T).astype(bf)

    def ranked(ids, earlier):
        onehot = (experts == ids).astype(f32)
        return onehot, dot(onehot.astype(bf), earlier, ((1,), (0,)))

    for i in range(3):
        info_copy(i, peers[i]).wait_recv()
    for i in range(3):
        info_copy(3 + i, e).start()
    total = 2 * W + K
    offsets = jnp.zeros((8, 1), f32)
    places = lax.broadcasted_iota(jnp.int32, (total, rows), 0).astype(f32)
    for b in range(S):
        ids = dot(info[e, b].astype(bf), interleave, ((1,), (0,)))[0:1, :]
        onehot, before = ranked(ids, in_order)
        start = offsets if packed else float(C * b)
        rank = jnp.sum(onehot * (before + start), axis=0, keepdims=True)
        offsets = offsets + jnp.sum(onehot, axis=1, keepdims=True)
        back = (W + K - 1) - rank if packed else K + rank
        code = jnp.where(
            ids == friend.astype(f32), rank,
            jnp.where(
                ids == e.astype(f32), W + K + rank,
                jnp.where(ids == near.astype(f32), W + rank, back),
            ),
        )
        picks[:, b * rows : (b + 1) * rows] = (places == code).astype(bf)

    def gs_copy(z, n):
        to = peers[0] if n in (0, 3) else peers[1]
        slot = (s, s, peers[0], peers[1])[n]
        lanes = (slice(0, D), slice(0, D), slice(0, D // 2), slice(D // 2, D))[n]
        block = grecv.at[z, slot, :, lanes]
        return send(block, block, gs_send.at[z, n], gs_recv.at[z, n], {"seq": to})

    def gs_wait(z, n):
        slot = (peers[0], peers[1], peers[2], peers[2])[n]
        lanes = (slice(0, D), slice(0, D), slice(0, D // 2), slice(D // 2, D))[n]
        block = grecv.at[z, slot, :, lanes]
        send(block, block, gs_send.at[z, n], gs_recv.at[z, n], {"seq": peers[0]}).wait_recv()

    wanted = lax.broadcasted_iota(jnp.int32, (C, rows), 0).astype(f32)

    def forward(z, grads):
        ids = info[z, pl.ds(s, 1)][0, 0:1, :]
        onehot, before = ranked(ids, k_order)
        rank = jnp.sum(before * onehot, axis=0, keepdims=True)
        code = jnp.where(ids == e.astype(f32), rank, -1.0)
        chosen = (wanted == code).astype(f32)
        gate = jnp.sum(chosen * info[z, 4, 0:1, :], axis=1, keepdims=True)
        token = (chosen[:, :T] + chosen[:, T:]).astype(bf)
        grecv[z, pl.ds(s, 1)] = (dot(token, grads, ((1,), (0,))) * gate).astype(bf)[None]
        for n in range(2):
            gs_copy(z, n).start()

    def pass_on(z):
        for n in range(2):
            gs_wait(z, n)
            gs_copy(z, 2 + n).start()

    def hz_copy(c, n):
        units = cols(c)
        to = (near, far, near, friend)[n]
        first, low, high = ((K, K - W, W), (2 * W, both, W), (W, 0, K - W), (0, 0, W))[n]
        src = hsend.at[first : first + high - low, units]
        landed = shared_recv if n == 0 else hz_recv
        return send(src, hrecv.at[e, low:high, units], hz_send.at[c, n], landed.at[c, e], {"expert": to})

    def hz_wait(c, z, low, high, landed):
        block = hrecv.at[z, low:high, cols(c)]
        send(block, block, hz_send.at[c, 0], landed.at[c, z], {"expert": friend}).wait_recv()

    def relay_copy(c, z):
        return send(
            hrecv.at[z, K - W : W, cols(c)], hrecv.at[z, 0:both, cols(c)],
            relay_send.at[c, z], relay_recv.at[c, z], {"expert": friend},
        )

    def pack(c):
        own_copy(c).wait()
        for i in range(3):
            raw_copy(c, i, peers[i]).wait_recv()
        width = pieces[c][2]
        for t in range(0, width, 256):
            units = pl.ds(pl.multiple_of(bases[c] + t, 128), min(256, width - t))
            block = hraw[:, :, :, units].reshape(S * rows, min(256, width - t))
            hsend[:, units] = dot(picks[0 : W + K, :], block, ((1,), (0,))).astype(bf)
            hrecv[pl.ds(e, 1), :, units] = dot(picks[W + K :, :], block, ((1,), (0,))).astype(bf)[None]
        for n in parts:
            hz_copy(c, n).start()

    def relay(c):
        if packed:

            @pl.when(inner)
            def _():
                for z in others:
                    hz_wait(c, z, K - W, W, shared_recv)
                    relay_copy(c, z).start()

    def arrived(c):
        hz_wait(c, friend, 0, W, hz_recv)

        @pl.when(inner)
        def _():
            for z in others:
                hz_wait(c, z, 0, K - W, hz_recv)

        @pl.when(outer)
        def _():
            for z in others:
                hz_wait(c, z, both, W, hz_recv)
                if packed:
                    relay_copy(c, z).wait_recv()

    scale = HEAD_DIM ** (-0.5)
    length = S * T

    def attention(j):
        lanes = slice(j * HEAD_DIM, (j + 1) * HEAD_DIM)
        heads = [slice(h * HEAD_DIM, (h + 1) * HEAD_DIM) for h in range(j * GROUP, (j + 1) * GROUP)]
        qs = jnp.concatenate([q[:, h] for h in heads], axis=0)
        gs = jnp.concatenate([go[:, h] for h in heads], axis=0)
        kj = kbuf[:, :, lanes].reshape(length, HEAD_DIM)
        vj = vbuf[:, :, lanes].reshape(length, HEAD_DIM)
        scores = dot(qs, kj, ((1,), (1,))) * scale
        raised = jnp.exp(scores - jnp.max(scores, axis=-1, keepdims=True))
        probs = raised / jnp.sum(raised, axis=-1, keepdims=True)
        dprobs = dot(gs, vj, ((1,), (1,)))
        delta = jnp.sum(probs * dprobs, axis=-1, keepdims=True)
        ds = (probs * (dprobs - delta)).astype(jnp.bfloat16)
        dv = dot(probs.astype(jnp.bfloat16), gs, ((0,), (0,)))
        dk = dot(ds, qs, ((0,), (0,))) * scale
        dq = dot(ds, kj, ((1,), (0,))) * scale
        for n, h in enumerate(heads):
            gq_out[:, h] = dq[n * T : (n + 1) * T].astype(jnp.bfloat16)
        dk = dk.reshape(S, T, HEAD_DIM)
        dv = dv.reshape(S, T, HEAD_DIM)
        kown[:, :, lanes] = dk
        vown[:, :, lanes] = dv
        kpart[:, :, lanes] = dk.astype(jnp.bfloat16)
        vpart[:, :, lanes] = dv.astype(jnp.bfloat16)

    pack(0)
    forward(e, go[...])
    pack(1)
    for i in range(3):
        info_copy(3 + i, z_peers[i]).wait_recv()
    gz_copy(0, across).wait_recv()
    gz_copy(2, across).start()
    forward(across, gsend[across])
    pack(2)
    gz_copy(1, friend).wait_recv()
    forward(friend, gsend[friend])
    pack(3)
    relay(0)
    for i in range(3):
        for n in range(2):
            kv_copy(n, i, peers[i]).wait_recv()
    attention(0)
    pass_on(e)
    attention(1)
    relay(1)
    gz_copy(2, corner).wait_recv()
    forward(corner, gsend[corner])
    pass_on(across)
    attention(2)
    attention(3)
    pass_on(friend)

    top = jnp.zeros((1, 1), f32)
    for z in range(E):
        crossing = jnp.zeros((1, rows), f32)
        for b in range(S):
            high = (info[z, b, 0:1, :] >= float(E // 2)).astype(f32)
            crossing = crossing + (high if z < E // 2 else 1.0 - high)
        top = jnp.maximum(top, jnp.sum(crossing, axis=1, keepdims=True))
    peak[...] = jnp.broadcast_to(top, (8, 128))
    top_copy = send(peak, peak_in, info_send.at[6], info_recv.at[6], {"dp": 1 - d})
    top_copy.start()

    def part_copy(n, i, slot):
        src, dst = ((kpart, kin), (vpart, vin))[n]
        return send(src.at[peers[i]], dst.at[slot], part_send.at[n, i], part_recv.at[n, i], {"seq": peers[i]})

    for i in range(3):
        for n in range(2):
            part_copy(n, i, s).start()
    relay(2)
    pass_on(corner)
    for n, (own, got, out) in enumerate(((kown, kin, gk_out), (vown, vin, gv_out))):
        summed = own[s]
        for i in range(3):
            part_copy(n, i, peers[i]).wait_recv()
            summed = summed + got[peers[i]].astype(jnp.float32)
        out[...] = summed.astype(jnp.bfloat16)

    def settle(z):
        for n in (2, 3):
            gs_wait(z, n)
        for n in range(4):
            gs_copy(z, n).wait_send()
        if not packed:
            return
        slots = lax.broadcasted_iota(jnp.int32, (1, W), 1).astype(f32)
        code = jnp.full((1, W), -1.0, f32)
        start = jnp.zeros((1, 1), f32)
        for b in range(S):
            named = (info[z, b, 0:1, :] == e.astype(f32)).astype(f32)
            count = jnp.sum(named, axis=1, keepdims=True)
            inside = jnp.logical_and(slots >= float(C * b), slots - float(C * b) < count)
            inside = jnp.logical_and(inside, slots < float(C * (b + 1)))
            code = jnp.where(inside, slots - float(C * b) + start, code)
            start = start + count
        turned = jnp.logical_and(z // 2 != side, outer).astype(f32)
        code = jnp.where(code >= 0.0, code + turned * (float(W - 1) - 2.0 * code), code)
        moves = (lax.broadcasted_iota(jnp.int32, (W, W), 0).astype(f32) == code).astype(bf)
        for t in range(0, D, 512):
            block = grecv[z, :, :, t : t + 512].reshape(W, 512)
            grecv[z, :, :, t : t + 512] = dot(moves, block, ((1,), (0,))).astype(bf).reshape(S, C, 512)

    for z in (e, across, friend, corner):
        settle(z)

    def product(base, off, width):
        units = pl.ds(pl.multiple_of(base + off, 128), width)
        h = hrecv[:, :, units].reshape(E * W, width)
        return dot(h, grecv[...].reshape(E * W, D), ((0,), (0,)))

    def pair_copy(n):
        off, width = tiles[n]
        return send(eg_out.at[off : off + width], precv.at[off : off + width], pair_send.at[n], pair_recv.at[n], {"dp": 1 - d})

    for c, (m, o, w) in enumerate(pieces):
        if c == 3:
            relay(c)
        arrived(c)
        for n, (off, width) in enumerate(tiles):
            if off < o or off >= o + w:
                continue
            if m == 0:
                eg_out[off : off + width, :] = product((1 - d) * half, off, width).astype(jnp.bfloat16)
                pair_copy(n).start()
            else:
                mine = product(d * half, off, width)
                pair_copy(n).wait_recv()
                pair_copy(n).wait_send()
                got = precv[off : off + width, :].astype(jnp.float32)
                eg_out[off : off + width, :] = (mine + got).astype(jnp.bfloat16)

    top_copy.wait()
    most[...] = jnp.maximum(peak[...], peak_in[...])
    for i in range(6):
        info_copy(i, s if i < 3 else e).wait_send()
    for i in range(3):
        for n in range(2):
            kv_copy(n, i, s).wait_send()
            part_copy(n, i, s).wait_send()
        gz_copy(i, across if i == 2 else e).wait_send()
    for c in range(len(pieces)):
        for i in range(3):
            raw_copy(c, i, s).wait_send()
        for n in parts:
            hz_copy(c, n).wait_send()
    if packed:

        @pl.when(inner)
        def _():
            for c in range(len(pieces)):
                for z in others:
                    relay_copy(c, z).wait_send()


def line_call(K, number, ids, gates, grad_out, queries, keys, values, hidden):
    E, S = lax.axis_size("expert"), lax.axis_size("seq")
    T, D = grad_out.shape
    U = hidden.shape[2] // S
    C = -(-(7 * T // (2 * E)) // 16) * 16
    KD = keys.shape[1]
    W, rows, half = S * C, 2 * T, U // 2
    bf, f32 = jnp.bfloat16, jnp.float32
    vm = pl.BlockSpec(memory_space=pltpu.VMEM)
    dma = pltpu.SemaphoreType.DMA
    P_ = len(line_pieces(half))
    tiles = len(line_tiles(half))
    return pl.pallas_call(
        functools.partial(line_kernel, (E, S, T, C, U, D, K)),
        out_shape=(
            pltpu.VMEM((half, D), bf),
            pltpu.VMEM((T, D), bf),
            pltpu.VMEM((T, KD), bf),
            pltpu.VMEM((T, KD), bf),
            jax.ShapeDtypeStruct((8, 128), f32),
        ),
        in_specs=[vm] * 6 + [pl.BlockSpec(memory_space=pl.ANY)],
        out_specs=(vm,) * 5,
        scratch_shapes=[
            pltpu.VMEM((E, S + 1, 8, rows), f32),
            pltpu.VMEM((8, 128), f32),
            pltpu.VMEM((8, 128), f32),
            pltpu.VMEM((S, T, KD), bf),
            pltpu.VMEM((S, T, KD), bf),
            pltpu.VMEM((S, T, 2, U), bf),
            pltpu.VMEM((2 * W + K, S * rows), bf),
            pltpu.VMEM((W + K, U), bf),
            pltpu.VMEM((E, W, U), bf),
            pltpu.VMEM((E, T, D), bf),
            pltpu.VMEM((E, S, C, D), bf),
            pltpu.VMEM((S, T, KD), bf),
            pltpu.VMEM((S, T, KD), bf),
            pltpu.VMEM((S, T, KD), f32),
            pltpu.VMEM((S, T, KD), f32),
            pltpu.VMEM((S, T, KD), bf),
            pltpu.VMEM((S, T, KD), bf),
            pltpu.VMEM((half, D), bf),
            dma((2, 3)), dma((2, 3)), dma((P_,)), dma((P_, 3)), dma((P_, 3)), dma((3,)), dma((3,)),
            dma((E, 4)), dma((E, 4)), dma((P_, 4)), dma((P_, E)), dma((P_, E)), dma((P_, E)), dma((P_, E)),
            dma((2, 3)), dma((2, 3)), dma((tiles,)), dma((tiles,)), dma((7,)), dma((7,)),
        ],
        compiler_params=pltpu.CompilerParams(
            collective_id=number, has_side_effects=True, vmem_limit_bytes=50 * 1024 * 1024
        ),
    )(ids, gates, grad_out, queries, keys, values, hidden)


def publish_kernel(*refs):
    n = (len(refs) - 1) // 2
    copies = []
    for a in range(n):
        count = 8 if a == 0 else 1
        size = refs[a].shape[0] // count
        for c in range(count):
            part = pl.ds(c * size, size)
            copies.append(
                pltpu.make_async_copy(refs[a].at[part], refs[n + a].at[part], refs[-1].at[len(copies)])
            )
    for copy in copies:
        copy.start()
    for copy in copies:
        copy.wait()


def publish(*grads):
    hbm = pl.BlockSpec(memory_space=pl.ANY)
    return pl.pallas_call(
        publish_kernel,
        out_shape=tuple(jax.ShapeDtypeStruct(g.shape, g.dtype) for g in grads),
        in_specs=[hbm] * len(grads),
        out_specs=(hbm,) * len(grads),
        scratch_shapes=[pltpu.SemaphoreType.DMA((8 + len(grads) - 1,))],
        compiler_params=pltpu.CompilerParams(vmem_limit_bytes=1024 * 1024),
    )(*grads)


def on_line(grad_out, expert_ids, gate_weights, hidden, queries, keys, values):
    E, S = lax.axis_size("expert"), lax.axis_size("seq")
    C = -(-(7 * grad_out.shape[1] // (2 * E)) // 16) * 16
    operands = (expert_ids[0].T, gate_weights[0].T, grad_out[0], queries[0], keys[0], values[0], hidden[0])
    full = 2 * S * C
    tight = full * 6 // 7 // 16 * 16
    *grads, most = line_call(tight, 0, *operands)
    grads = publish(*grads)

    def kept(grads, operands):
        return tuple(grads)

    def again(grads, operands):
        return tuple(publish(*line_call(full, 1, *operands)[:4]))

    eg, gq, gk, gv = lax.cond(most[0, 0] <= float(tight), kept, again, grads, operands)
    return (eg[None], gq[None], gk[None], gv[None])


def solution(mesh):
    split = P(("expert", "dp"), "seq", None)
    in_specs = (split, split, split, P(("expert", "dp"), "seq", None, None), split, split, split)
    out_specs = (P("expert", ("seq", "dp"), None), split, split, split)
    body = on_line if mesh.shape["expert"] == 4 and mesh.shape["seq"] == 4 else on_device
    return jax.shard_map(
        body, mesh=mesh, in_specs=in_specs, out_specs=out_specs, check_vma=False
    )
```

```python
import functools

import jax
import jax.numpy as jnp
from jax import lax
from jax.experimental import pallas as pl
from jax.experimental.pallas import tpu as pltpu
from jax.sharding import PartitionSpec as P

HEADS = 16
KV_HEADS = 4
HEAD_DIM = 128
GROUP = HEADS // KV_HEADS
MESH = pl.DeviceIdType.MESH


def dot(a, b, contract):
    return lax.dot_general(a, b, (contract, ((), ())), preferred_element_type=jnp.float32)


def routing_codes(ids, order_row, order_col, experts, capacity):
    count = max(8, experts)
    rows = ids.shape[1]
    expert_of = lax.broadcasted_iota(jnp.int32, (count, rows), 0).astype(jnp.float32)
    onehot = (expert_of == ids).astype(jnp.float32)
    earlier = (order_col < order_row).astype(jnp.float32)
    before = dot(onehot.astype(jnp.bfloat16), earlier.astype(jnp.bfloat16), ((1,), (0,)))
    slot = jnp.sum(before * onehot, axis=0, keepdims=True)
    return ids * float(capacity) + slot


def spreads(experts):
    return experts <= 8 and experts & (experts - 1) == 0


def kernel(
    dims,
    ids_t, info, go, q, k, v, hid,
    eg_out, gq_out, gk_out, gv_out,
    kbuf, vbuf, idbuf, hraw, hsend, hrecv, gsend, grecv, infos,
    kpart, vpart, kown, vown, kin, vin, precv,
    small_send, small_recv, local_sem, hraw_send, hraw_recv,
    gz_send, gz_recv, gi_send, gi_recv, gs_send, gs_recv, hz_send, hz_recv,
    part_send, part_recv, pair_send, pair_recv,
):
    E, S, T, C, U, D = dims
    half = U // 2
    first = -(-half // 256) * 128
    pieces = [(n, o, w) for n in range(2) for o, w in ((0, first), (first, half - first)) if w > 0]
    spread = spreads(E)
    e = lax.axis_index("expert")
    s = lax.axis_index("seq")
    d = lax.axis_index("dp")
    seq_peer = [lax.rem(s + i, S) for i in range(S)]
    bases = [
        pl.multiple_of((d if n else 1 - d) * half + o, 128) for n, o, _ in pieces
    ]

    def ex_peer(j):
        return lax.rem(e + j, E)

    barrier = pltpu.get_barrier_semaphore()
    for i in range(1, S):
        pl.semaphore_signal(barrier, inc=1, device_id={"seq": seq_peer[i]}, device_id_type=MESH)

    @pl.loop(1, E)
    def _(j):
        pl.semaphore_signal(barrier, inc=1, device_id={"expert": ex_peer(j)}, device_id_type=MESH)

    pl.semaphore_signal(barrier, inc=1, device_id={"dp": 1 - d}, device_id_type=MESH)
    pl.semaphore_wait(barrier, S + E - 1)

    def send(src, dst, ssem, rsem, where):
        return pltpu.make_async_remote_copy(
            src_ref=src, dst_ref=dst, send_sem=ssem, recv_sem=rsem,
            device_id=where, device_id_type=MESH,
        )

    def small_copy(n, i, slot):
        src, dst = ((ids_t, idbuf), (k, kbuf), (v, vbuf))[n]
        return send(src, dst.at[slot], small_send.at[n, i], small_recv.at[n, slot], {"seq": seq_peer[i]})

    def raw_copy(c, i, slot):
        width = pieces[c][2]
        cols = pl.ds(pl.multiple_of(seq_peer[i] * U + bases[c], 128), width)
        return send(
            hid.at[:, :, cols], hraw.at[slot, :, :, pl.ds(bases[c], width)],
            hraw_send.at[c, i], hraw_recv.at[c, slot], {"seq": seq_peer[i]},
        )

    own_cols = pl.ds(pl.multiple_of(s * U, 128), U)
    own_raw = pltpu.make_async_copy(hid.at[:, :, own_cols], hraw.at[s], local_sem.at[0])
    own_raw.start()
    for i in range(1, S):
        for n in range(3):
            small_copy(n, i, s).start()
    for c in range(len(pieces)):
        for i in range(1, S):
            raw_copy(c, i, s).start()
    kbuf[s] = k[...]
    vbuf[s] = v[...]
    idbuf[s] = ids_t[...]

    rows = 2 * T
    col = lax.broadcasted_iota(jnp.int32, (rows, rows), 1)
    row = lax.broadcasted_iota(jnp.int32, (rows, rows), 0)
    place = lax.broadcasted_iota(jnp.int32, (E * C, rows), 0).astype(jnp.float32)

    def expert_rows(p):
        return pl.ds(pl.multiple_of(p * C, 16), C)

    def gs_copy(i, z, slot):
        return send(grecv.at[s, z], grecv.at[slot, z], gs_send.at[i, z], gs_recv.at[slot, z], {"seq": seq_peer[i]})

    def gs_wait(i, z):
        slot = seq_peer[i]
        send(grecv.at[s, z], grecv.at[slot, z], gs_send.at[i, z], gs_recv.at[slot, z], {"seq": slot}).wait_recv()

    def packed_grads(ids, gates, grads, wanted):
        code = routing_codes(
            ids, 2 * lax.rem(col, T) + col // T, 2 * lax.rem(row, T) + row // T, E, C
        )
        picks = (wanted == code).astype(jnp.float32)
        gate = jnp.sum(picks * gates, axis=1, keepdims=True)
        token_picks = (picks[:, :T] + picks[:, T:]).astype(jnp.bfloat16)
        return (dot(token_picks, grads, ((1,), (0,))) * gate).astype(jnp.bfloat16)

    if spread:
        def flip(at, b):
            return at + b - 2 * b * lax.rem(at // b, 2)

        bits = []
        b = E // 2
        while b >= 1:
            bits.append(b)
            b //= 2

        def masks(n):
            held = [0]
            for bit in bits[:n]:
                held = held + [m + bit for m in held]
            return held

        def at_mask(m):
            at = e
            for bit in bits:
                if m & bit:
                    at = flip(at, bit)
            return at

        def gz_pair(m, n, slot):
            to = {"expert": flip(e, bits[n])}
            key = m + bits[n]
            return (
                send(gsend.at[slot], gsend.at[slot], gz_send.at[key], gz_recv.at[slot], to),
                send(infos.at[slot], infos.at[slot], gi_send.at[key], gi_recv.at[slot], to),
            )

        def forward(m):
            z = at_mask(m)
            wanted = (
                lax.broadcasted_iota(jnp.int32, (C, rows), 0) + e * C
            ).astype(jnp.float32)
            grecv[s, z] = packed_grads(infos[z, 0:1, :], infos[z, 8:9, :], gsend[z], wanted)
            for i in range(1, S):
                gs_copy(i, z, s).start()

        def arrive(m, n):
            for copy in gz_pair(m, n, at_mask(m + bits[n])):
                copy.wait_recv()
            for later in range(n + 1, len(bits)):
                for copy in gz_pair(m + bits[n], later, at_mask(m + bits[n])):
                    copy.start()

        gsend[e] = go[...]
        infos[e] = info[...]
        for n in range(len(bits)):
            for copy in gz_pair(0, n, e):
                copy.start()
    else:

        def gz_copy(j, slot):
            p = ex_peer(j)
            return send(gsend.at[expert_rows(p)], grecv.at[s, slot], gz_send.at[j], gz_recv.at[slot], {"expert": p})

        gsend[...] = packed_grads(info[0:1, :], info[8:9, :], go[...], place)

        @pl.loop(1, E)
        def _(j):
            gz_copy(j, e).start()

        grecv[s, e] = gsend[expert_rows(e)]
        for i in range(1, S):
            gs_copy(i, e, s).start()

    def hz_copy(c, i, j, slot):
        p = ex_peer(j)
        src = seq_peer[i]
        units = pl.ds(bases[c], pieces[c][2])
        return send(
            hsend.at[src, expert_rows(p), units], hrecv.at[src, slot, :, units],
            hz_send.at[c, src, j], hz_recv.at[c, src, slot], {"expert": p},
        )

    def pack_hidden(c, i):
        src = seq_peer[i]
        width = pieces[c][2]
        units = pl.ds(bases[c], width)
        hcode = routing_codes(idbuf[src, 0:1, :], col, row, E, C)
        hpicks = (place == hcode).astype(jnp.bfloat16)
        hsend[src, :, units] = dot(
            hpicks, hraw[src, :, :, units].reshape(rows, width), ((1,), (0,))
        ).astype(jnp.bfloat16)

        @pl.loop(1, E)
        def _(j):
            hz_copy(c, i, j, e).start()

        hrecv[src, e, :, units] = hsend[src, expert_rows(e), units]

    own_raw.wait()
    for c in range(len(pieces)):
        pack_hidden(c, 0)
    if spread:
        forward(0)

    scale = HEAD_DIM ** (-0.5)
    length = S * T

    def attention(j):
        lanes = slice(j * HEAD_DIM, (j + 1) * HEAD_DIM)
        heads = [slice(h * HEAD_DIM, (h + 1) * HEAD_DIM) for h in range(j * GROUP, (j + 1) * GROUP)]
        qs = jnp.concatenate([q[:, h] for h in heads], axis=0)
        gs = jnp.concatenate([go[:, h] for h in heads], axis=0)
        kj = kbuf[:, :, lanes].reshape(length, HEAD_DIM)
        vj = vbuf[:, :, lanes].reshape(length, HEAD_DIM)
        scores = dot(qs, kj, ((1,), (1,))) * scale
        raised = jnp.exp(scores - jnp.max(scores, axis=-1, keepdims=True))
        probs = raised / jnp.sum(raised, axis=-1, keepdims=True)
        dprobs = dot(gs, vj, ((1,), (1,)))
        delta = jnp.sum(probs * dprobs, axis=-1, keepdims=True)
        ds = (probs * (dprobs - delta)).astype(jnp.bfloat16)
        dv = dot(probs.astype(jnp.bfloat16), gs, ((0,), (0,)))
        dk = dot(ds, qs, ((0,), (0,))) * scale
        dq = dot(ds, kj, ((1,), (0,))) * scale
        for n, h in enumerate(heads):
            gq_out[:, h] = dq[n * T : (n + 1) * T].astype(jnp.bfloat16)
        dk = dk.reshape(S, T, HEAD_DIM)
        dv = dv.reshape(S, T, HEAD_DIM)
        kown[:, :, lanes] = dk
        vown[:, :, lanes] = dv
        kpart[:, :, lanes] = dk.astype(jnp.bfloat16)
        vpart[:, :, lanes] = dv.astype(jnp.bfloat16)

    for i in range(1, S):
        for n in range(3):
            small_copy(n, i, seq_peer[i]).wait_recv()

    attention(0)

    if spread:
        attention(1)
        for n in range(len(bits)):
            for m in masks(n):
                arrive(m, n)
                forward(m + bits[n])
    else:

        @pl.loop(1, E)
        def _(j):
            z = ex_peer(j)
            gz_copy(j, z).wait_recv()
            for i in range(1, S):
                gs_copy(i, z, s).start()

        attention(1)
    for c in range(len(pieces)):
        for i in range(1, S):
            raw_copy(c, i, seq_peer[i]).wait_recv()
            pack_hidden(c, i)
        if c + 2 < KV_HEADS:
            attention(c + 2)
    for j in range(len(pieces) + 2, KV_HEADS):
        attention(j)

    def part_copy(n, i, slot):
        src, dst = ((kpart, kin), (vpart, vin))[n]
        return send(src.at[seq_peer[i]], dst.at[slot], part_send.at[n, i], part_recv.at[n, slot], {"seq": seq_peer[i]})

    for i in range(1, S):
        for n in range(2):
            part_copy(n, i, s).start()
    for n, (own, got, out) in enumerate(((kown, kin, gk_out), (vown, vin, gv_out))):
        total = own[s]
        for i in range(1, S):
            part_copy(n, i, seq_peer[i]).wait_recv()
            total = total + got[seq_peer[i]].astype(jnp.float32)
        out[...] = total.astype(jnp.bfloat16)

    @pl.loop(0, E)
    def _(z):
        for i in range(1, S):
            gs_wait(i, z)

    wide = 256
    tiles = [
        (o + t, min(wide, w - t)) for n, o, w in pieces if n == 0 for t in range(0, w, wide)
    ]

    def arrived(n, off):
        for c, (m, o, _) in enumerate(pieces):
            if m == n and o == off:

                @pl.loop(1, E)
                def _(j):
                    for i in range(S):
                        hz_copy(c, i, j, ex_peer(j)).wait_recv()

    def product(base, off, width):
        units = pl.ds(pl.multiple_of(base + off, 128), width)
        h = hrecv[:, :, :, units].reshape(S * E * C, width)
        return dot(h, grecv[...].reshape(S * E * C, D), ((0,), (0,)))

    def pair_copy(n):
        off, width = tiles[n]
        return send(eg_out.at[off : off + width], precv.at[off : off + width], pair_send.at[n], pair_recv.at[n], {"dp": 1 - d})

    for n, (off, width) in enumerate(tiles):
        arrived(0, off)
        eg_out[off : off + width, :] = product((1 - d) * half, off, width).astype(jnp.bfloat16)
        pair_copy(n).start()
    for n, (off, width) in enumerate(tiles):
        arrived(1, off)
        mine = product(d * half, off, width)
        pair_copy(n).wait_recv()
        pair_copy(n).wait_send()
        got = precv[off : off + width, :].astype(jnp.float32)
        eg_out[off : off + width, :] = (mine + got).astype(jnp.bfloat16)

    for i in range(1, S):
        for n in range(3):
            small_copy(n, i, s).wait_send()
        for n in range(2):
            part_copy(n, i, s).wait_send()
        for c in range(len(pieces)):
            raw_copy(c, i, s).wait_send()

    @pl.loop(0, E)
    def _(z):
        for i in range(1, S):
            gs_copy(i, z, s).wait_send()

    @pl.loop(1, E)
    def _(j):
        if not spread:
            gz_copy(j, e).wait_send()
        for i in range(S):
            for c in range(len(pieces)):
                hz_copy(c, i, j, e).wait_send()

    if spread:
        for n in range(len(bits)):
            for m in masks(n):
                for copy in gz_pair(m, n, at_mask(m)):
                    copy.wait_send()


def on_device(grad_out, expert_ids, gate_weights, hidden, queries, keys, values):
    E = lax.axis_size("expert")
    S = lax.axis_size("seq")
    T = grad_out.shape[1]
    D = grad_out.shape[2]
    U = hidden.shape[3] // S
    C = -(-(7 * T // (2 * E)) // 16) * 16
    KD = keys.shape[2]
    rows = 2 * T
    bf, f32 = jnp.bfloat16, jnp.float32
    ids = expert_ids[0].astype(f32)
    ids_t = jnp.broadcast_to(ids.reshape(1, rows), (8, rows))
    ids_k = jnp.broadcast_to(ids.T.reshape(1, rows), (8, rows))
    gates_k = jnp.broadcast_to(gate_weights[0].T.reshape(1, rows), (8, rows))
    tiles = -(-(U // 2) // 256)
    info = jnp.concatenate([ids_k, gates_k], axis=0)
    sent = (E, T, D) if spreads(E) else (E * C, D)
    vm = pl.BlockSpec(memory_space=pltpu.VMEM)
    dma = pltpu.SemaphoreType.DMA
    eg, gq, gk, gv = pl.pallas_call(
        functools.partial(kernel, (E, S, T, C, U, D)),
        out_shape=(
            jax.ShapeDtypeStruct((U // 2, D), bf),
            jax.ShapeDtypeStruct((T, queries.shape[2]), bf),
            jax.ShapeDtypeStruct((T, KD), bf),
            jax.ShapeDtypeStruct((T, KD), bf),
        ),
        in_specs=[vm] * 6 + [pl.BlockSpec(memory_space=pl.ANY)],
        out_specs=(vm,) * 4,
        scratch_shapes=[
            pltpu.VMEM((S, T, KD), bf),
            pltpu.VMEM((S, T, KD), bf),
            pltpu.VMEM((S, 8, rows), f32),
            pltpu.VMEM((S, T, 2, U), bf),
            pltpu.VMEM((S, E * C, U), bf),
            pltpu.VMEM((S, E, C, U), bf),
            pltpu.VMEM(sent, bf),
            pltpu.VMEM((S, E, C, D), bf),
            pltpu.VMEM((E if spreads(E) else 1, 16, rows), f32),
            pltpu.VMEM((S, T, KD), bf),
            pltpu.VMEM((S, T, KD), bf),
            pltpu.VMEM((S, T, KD), f32),
            pltpu.VMEM((S, T, KD), f32),
            pltpu.VMEM((S, T, KD), bf),
            pltpu.VMEM((S, T, KD), bf),
            pltpu.VMEM((U // 2, D), bf),
            dma((3, S)), dma((3, S)), dma((1,)), dma((4, S)), dma((4, S)),
            dma((E,)), dma((E,)), dma((E,)), dma((E,)), dma((S, E)), dma((S, E)), dma((4, S, E)), dma((4, S, E)),
            dma((2, S)), dma((2, S)), dma((tiles,)), dma((tiles,)),
        ],
        compiler_params=pltpu.CompilerParams(
            collective_id=0, has_side_effects=True, vmem_limit_bytes=62 * 1024 * 1024
        ),
    )(ids_t, info, grad_out[0], queries[0], keys[0], values[0], hidden[0])
    return (eg[None], gq[None], gk[None], gv[None])


def flip(at, b):
    return at + b - 2 * b * lax.rem(at // b, 2)


def greet(peers):
    barrier = pltpu.get_barrier_semaphore()
    for peer in peers:
        pl.semaphore_signal(barrier, inc=1, device_id=peer, device_id_type=MESH)
    pl.semaphore_wait(barrier, len(peers))


def send(src, dst, ssem, rsem, where):
    return pltpu.make_async_remote_copy(
        src_ref=src, dst_ref=dst, send_sem=ssem, recv_sem=rsem,
        device_id=where, device_id_type=MESH,
    )


def line_pieces(half):
    cut = min(384, half)
    return [(0, 0, cut), (0, cut, half - cut), (1, 0, half - 256), (1, half - 256, 256)]


def line_tiles(half):
    edges = sorted({0, half} | {p[1] for p in line_pieces(half)})
    return [
        (lo + t, min(256, hi - lo - t)) for lo, hi in zip(edges, edges[1:]) for t in range(0, hi - lo, 256)
    ]


def line_kernel(
    dims,
    ids_in, gates_in, go, q, k, v, hid,
    eg_out, gq_out, gk_out, gv_out, most,
    info, peak, peak_in,
    kbuf, vbuf, hraw, picks, hsend, hrecv, gsend, grecv,
    kpart, vpart, kown, vown, kin, vin, precv,
    kv_send, kv_recv, local_sem, raw_send, raw_recv, gz_send, gz_recv, gs_send, gs_recv,
    hz_send, hz_recv, shared_recv, relay_send, relay_recv, part_send, part_recv, pair_send, pair_recv,
    info_send, info_recv,
):
    E, S, T, C, U, D, K = dims
    W = S * C
    half = U // 2
    rows = 2 * T
    packed = K < 2 * W
    parts = range(0 if packed else 1, 4)
    both = 2 * W - K
    pieces = line_pieces(half)
    tiles = line_tiles(half)
    e, s, d = (lax.axis_index(n) for n in ("expert", "seq", "dp"))
    side = e // 2
    friend, across, corner = flip(e, 1), flip(e, 2), flip(flip(e, 1), 2)
    near, far = 2 - side, 3 - 3 * side
    inner = jnp.logical_or(e == 1, e == 2)
    outer = jnp.logical_not(inner)
    others = [2 - 2 * side, 3 - 2 * side]
    peers = [flip(s, 1), flip(s, 2), flip(flip(s, 1), 2)]
    bases = [pl.multiple_of((d if n else 1 - d) * half + o, 128) for n, o, _ in pieces]
    greet([{"seq": p} for p in peers] + [{"expert": p} for p in (friend, across, corner)] + [{"dp": 1 - d}])

    def cols(c):
        return pl.ds(bases[c], pieces[c][2])

    def kv_copy(n, i, slot):
        src, dst = ((k, kbuf), (v, vbuf))[n]
        return send(src, dst.at[slot], kv_send.at[n, i], kv_recv.at[n, i], {"seq": peers[i]})

    def raw_copy(c, i, slot):
        there = pl.ds(pl.multiple_of(peers[i] * U + bases[c], 128), pieces[c][2])
        return send(
            hid.at[:, :, there], hraw.at[slot, :, :, cols(c)],
            raw_send.at[c, i], raw_recv.at[c, i], {"seq": peers[i]},
        )

    def own_copy(c):
        here = pl.ds(pl.multiple_of(s * U + bases[c], 128), pieces[c][2])
        return pltpu.make_async_copy(hid.at[:, :, here], hraw.at[s, :, :, cols(c)], local_sem.at[c])

    def gz_copy(n, slot):
        src = go if n < 2 else gsend.at[across]
        dst = gsend.at[slot]
        to = across if n == 0 else friend
        return send(src, dst, gz_send.at[n], gz_recv.at[n], {"expert": to})

    z_peers = [friend, across, corner]

    def line(ref):
        flat = jnp.concatenate([ref[0:1, :], ref[1:2, :]], axis=1).astype(jnp.float32)
        return jnp.broadcast_to(flat, (1, 8, rows))

    def info_copy(i, slot):
        if i < 3:
            return send(info.at[e, s], info.at[e, slot], info_send.at[i], info_recv.at[i], {"seq": peers[i]})
        return send(info.at[e], info.at[slot], info_send.at[i], info_recv.at[i], {"expert": z_peers[i - 3]})

    info[e, pl.ds(s, 1)] = line(ids_in)
    info[e, S : S + 1] = line(gates_in)
    for i in range(3):
        info_copy(i, s).start()
    gz_copy(0, e).start()
    gz_copy(1, e).start()
    for c in range(len(pieces)):
        own_copy(c).start()
        for i in range(3):
            raw_copy(c, i, s).start()
    for i in range(3):
        for n in range(2):
            kv_copy(n, i, s).start()
    kbuf[s] = k[...]
    vbuf[s] = v[...]

    col = lax.broadcasted_iota(jnp.int32, (rows, rows), 1)
    row = lax.broadcasted_iota(jnp.int32, (rows, rows), 0)
    f32, bf = jnp.float32, jnp.bfloat16
    experts = lax.broadcasted_iota(jnp.int32, (8, rows), 0).astype(f32)
    by_place = (col < row).astype(bf)
    interleave = (row == lax.rem(col, 2) * T + col // 2).astype(bf)
    in_order = (row < col).astype(bf)
    k_order = (2 * lax.rem(row, T) + row // T < 2 * lax.rem(col, T) + col // T).astype(bf)

    def ranked(ids, earlier):
        onehot = (experts == ids).astype(f32)
        return onehot, dot(onehot.astype(bf), earlier, ((1,), (0,)))

    for i in range(3):
        info_copy(i, peers[i]).wait_recv()
    for i in range(3):
        info_copy(3 + i, e).start()
    total = 2 * W + K
    offsets = jnp.zeros((8, 1), f32)
    places = lax.broadcasted_iota(jnp.int32, (128, rows), 0).astype(f32)

    def mark(b, start):
        ids = dot(info[e, b].astype(bf), interleave, ((1,), (0,)))[0:1, :]
        onehot, before = ranked(ids, in_order)
        rank = jnp.sum(onehot * (before + start), axis=0, keepdims=True)
        back = (W + K - 1) - rank if packed else K + rank
        code = jnp.where(
            ids == friend.astype(f32), rank,
            jnp.where(
                ids == e.astype(f32), W + K + rank,
                jnp.where(ids == near.astype(f32), W + rank, back),
            ),
        )

        @pl.loop(0, total // 128)
        def _(r):
            at = places + (128 * r).astype(f32)
            picks[pl.ds(pl.multiple_of(128 * r, 128), 128), b * rows : (b + 1) * rows] = (at == code).astype(bf)

        return start + jnp.sum(onehot, axis=1, keepdims=True)

    for b in range(S):
        offsets = mark(b, offsets if packed else float(C * b))

    def gs_copy(z, n):
        to = peers[0] if n in (0, 3) else peers[1]
        slot = (s, s, peers[0], peers[1])[n]
        lanes = (slice(0, D), slice(0, D), slice(0, D // 2), slice(D // 2, D))[n]
        block = grecv.at[z, slot, :, lanes]
        return send(block, block, gs_send.at[z, n], gs_recv.at[z, n], {"seq": to})

    def gs_wait(z, n):
        slot = (peers[0], peers[1], peers[2], peers[2])[n]
        lanes = (slice(0, D), slice(0, D), slice(0, D // 2), slice(D // 2, D))[n]
        block = grecv.at[z, slot, :, lanes]
        send(block, block, gs_send.at[z, n], gs_recv.at[z, n], {"seq": peers[0]}).wait_recv()

    wanted = lax.broadcasted_iota(jnp.int32, (C, rows), 0).astype(f32)

    def forward(z, grads):
        ids = info[z, pl.ds(s, 1)][0, 0:1, :]
        onehot, before = ranked(ids, k_order)
        rank = jnp.sum(before * onehot, axis=0, keepdims=True)
        code = jnp.where(ids == e.astype(f32), rank, -1.0)
        chosen = (wanted == code).astype(f32)
        gate = jnp.sum(chosen * info[z, 4, 0:1, :], axis=1, keepdims=True)
        token = (chosen[:, :T] + chosen[:, T:]).astype(bf)
        grecv[z, pl.ds(s, 1)] = (dot(token, grads, ((1,), (0,))) * gate).astype(bf)[None]
        for n in range(2):
            gs_copy(z, n).start()

    def pass_on(z):
        for n in range(2):
            gs_wait(z, n)
            gs_copy(z, 2 + n).start()

    def hz_copy(c, n):
        units = cols(c)
        to = (near, far, near, friend)[n]
        first, low, high = ((K, K - W, W), (2 * W, both, W), (W, 0, K - W), (0, 0, W))[n]
        src = hsend.at[first : first + high - low, units]
        landed = shared_recv if n == 0 else hz_recv
        return send(src, hrecv.at[e, low:high, units], hz_send.at[c, n], landed.at[c, e], {"expert": to})

    def hz_wait(c, z, low, high, landed):
        block = hrecv.at[z, low:high, cols(c)]
        send(block, block, hz_send.at[c, 0], landed.at[c, z], {"expert": friend}).wait_recv()

    def relay_copy(c, z):
        return send(
            hrecv.at[z, K - W : W, cols(c)], hrecv.at[z, 0:both, cols(c)],
            relay_send.at[c, z], relay_recv.at[c, z], {"expert": friend},
        )

    def pack(c):
        own_copy(c).wait()
        for i in range(3):
            raw_copy(c, i, peers[i]).wait_recv()
        width = pieces[c][2]
        sent = (W + K) // 4

        def gather(t, size):
            units = pl.ds(pl.multiple_of(bases[c] + t, 128), size)
            block = hraw[:, :, :, units].reshape(S * rows, size)

            @pl.loop(0, 4)
            def _(r):
                some = pl.ds(pl.multiple_of(r * sent, 16), sent)
                hsend[some, units] = dot(picks[some, :], block, ((1,), (0,))).astype(bf)

            hrecv[pl.ds(e, 1), :, units] = dot(picks[W + K :, :], block, ((1,), (0,))).astype(bf)[None]

        if width >= 256:

            @pl.loop(0, width // 256)
            def _(t):
                gather(t * 256, 256)

        if width % 256:
            gather(width - 128, 128)
        for n in parts:
            hz_copy(c, n).start()

    def relay(c):
        if packed:

            @pl.when(inner)
            def _():
                for z in others:
                    hz_wait(c, z, K - W, W, shared_recv)
                    relay_copy(c, z).start()

    def arrived(c):
        hz_wait(c, friend, 0, W, hz_recv)

        @pl.when(inner)
        def _():
            for z in others:
                hz_wait(c, z, 0, K - W, hz_recv)

        @pl.when(outer)
        def _():
            for z in others:
                hz_wait(c, z, both, W, hz_recv)
                if packed:
                    relay_copy(c, z).wait_recv()

    scale = HEAD_DIM ** (-0.5)
    length = S * T

    def attention(j):
        def lanes_of(h):
            return pl.ds(pl.multiple_of(h * HEAD_DIM, HEAD_DIM), HEAD_DIM)

        lanes = lanes_of(j)
        heads = [lanes_of(j * GROUP + n) for n in range(GROUP)]
        qs = jnp.concatenate([q[:, h] for h in heads], axis=0)
        gs = jnp.concatenate([go[:, h] for h in heads], axis=0)
        kj = kbuf[:, :, lanes].reshape(length, HEAD_DIM)
        vj = vbuf[:, :, lanes].reshape(length, HEAD_DIM)
        scores = dot(qs, kj, ((1,), (1,))) * scale
        raised = jnp.exp(scores - jnp.max(scores, axis=-1, keepdims=True))
        probs = raised / jnp.sum(raised, axis=-1, keepdims=True)
        dprobs = dot(gs, vj, ((1,), (1,)))
        delta = jnp.sum(probs * dprobs, axis=-1, keepdims=True)
        ds = (probs * (dprobs - delta)).astype(jnp.bfloat16)
        dv = dot(probs.astype(jnp.bfloat16), gs, ((0,), (0,)))
        dk = dot(ds, qs, ((0,), (0,))) * scale
        dq = dot(ds, kj, ((1,), (0,))) * scale
        for n, h in enumerate(heads):
            gq_out[:, h] = dq[n * T : (n + 1) * T].astype(jnp.bfloat16)
        dk = dk.reshape(S, T, HEAD_DIM)
        dv = dv.reshape(S, T, HEAD_DIM)
        kown[:, :, lanes] = dk
        vown[:, :, lanes] = dv
        kpart[:, :, lanes] = dk.astype(jnp.bfloat16)
        vpart[:, :, lanes] = dv.astype(jnp.bfloat16)

    pack(0)
    forward(e, go[...])
    pack(1)
    for i in range(3):
        info_copy(3 + i, z_peers[i]).wait_recv()
    gz_copy(0, across).wait_recv()
    gz_copy(2, across).start()
    forward(across, gsend[across])
    pack(2)
    gz_copy(1, friend).wait_recv()
    forward(friend, gsend[friend])
    pack(3)
    relay(0)
    for i in range(3):
        for n in range(2):
            kv_copy(n, i, peers[i]).wait_recv()
    pl.loop(0, KV_HEADS)(attention)
    relay(1)
    pass_on(e)
    gz_copy(2, corner).wait_recv()
    forward(corner, gsend[corner])
    pass_on(across)
    pass_on(friend)

    top = jnp.zeros((1, 1), f32)
    for z in range(E):
        crossing = jnp.zeros((1, rows), f32)
        for b in range(S):
            high = (info[z, b, 0:1, :] >= float(E // 2)).astype(f32)
            crossing = crossing + (high if z < E // 2 else 1.0 - high)
        top = jnp.maximum(top, jnp.sum(crossing, axis=1, keepdims=True))
    peak[...] = jnp.broadcast_to(top, (8, 128))
    top_copy = send(peak, peak_in, info_send.at[6], info_recv.at[6], {"dp": 1 - d})
    top_copy.start()

    def part_copy(n, i, slot):
        src, dst = ((kpart, kin), (vpart, vin))[n]
        return send(src.at[peers[i]], dst.at[slot], part_send.at[n, i], part_recv.at[n, i], {"seq": peers[i]})

    for i in range(3):
        for n in range(2):
            part_copy(n, i, s).start()
    relay(2)
    pass_on(corner)
    for n, (own, got, out) in enumerate(((kown, kin, gk_out), (vown, vin, gv_out))):
        summed = own[s]
        for i in range(3):
            part_copy(n, i, peers[i]).wait_recv()
            summed = summed + got[peers[i]].astype(jnp.float32)
        out[...] = summed.astype(jnp.bfloat16)

    def settle(z):
        for n in (2, 3):
            gs_wait(z, n)
        for n in range(4):
            gs_copy(z, n).wait_send()
        if not packed:
            return
        slots = lax.broadcasted_iota(jnp.int32, (1, W), 1).astype(f32)
        code = jnp.full((1, W), -1.0, f32)
        start = jnp.zeros((1, 1), f32)
        for b in range(S):
            named = (info[z, b, 0:1, :] == e.astype(f32)).astype(f32)
            count = jnp.sum(named, axis=1, keepdims=True)
            inside = jnp.logical_and(slots >= float(C * b), slots - float(C * b) < count)
            inside = jnp.logical_and(inside, slots < float(C * (b + 1)))
            code = jnp.where(inside, slots - float(C * b) + start, code)
            start = start + count
        turned = jnp.logical_and(z // 2 != side, outer).astype(f32)
        code = jnp.where(code >= 0.0, code + turned * (float(W - 1) - 2.0 * code), code)
        moves = (lax.broadcasted_iota(jnp.int32, (W, W), 0).astype(f32) == code).astype(bf)

        @pl.loop(0, D // 512)
        def _(t):
            lanes = pl.ds(pl.multiple_of(t * 512, 512), 512)
            block = grecv[z, :, :, lanes].reshape(W, 512)
            grecv[z, :, :, lanes] = dot(moves, block, ((1,), (0,))).astype(bf).reshape(S, C, 512)

    pl.loop(0, E)(settle)

    def product(base, off, width, use):
        units = pl.ds(pl.multiple_of(base + off, 128), width)
        here = pl.ds(off, width)

        @pl.loop(0, D // 1024)
        def _(t):
            lanes = pl.ds(pl.multiple_of(t * 1024, 1024), 1024)
            h = hrecv[:, :, units].reshape(E * W, width)
            use(here, lanes, dot(h, grecv[:, :, :, lanes].reshape(E * W, 1024), ((0,), (0,))))

    def give(here, lanes, value):
        eg_out[here, lanes] = value.astype(jnp.bfloat16)

    def take(here, lanes, value):
        eg_out[here, lanes] = (value + precv[here, lanes].astype(jnp.float32)).astype(jnp.bfloat16)

    def pair_copy(n):
        off, width = tiles[n]
        return send(eg_out.at[off : off + width], precv.at[off : off + width], pair_send.at[n], pair_recv.at[n], {"dp": 1 - d})

    for c, (m, o, w) in enumerate(pieces):
        if c == 3:
            relay(c)
        arrived(c)
        for n, (off, width) in enumerate(tiles):
            if off < o or off >= o + w:
                continue
            if m == 0:
                product((1 - d) * half, off, width, give)
                pair_copy(n).start()
            else:
                pair_copy(n).wait_recv()
                pair_copy(n).wait_send()
                product(d * half, off, width, take)

    top_copy.wait()
    most[...] = jnp.maximum(peak[...], peak_in[...])
    for i in range(6):
        info_copy(i, s if i < 3 else e).wait_send()
    for i in range(3):
        for n in range(2):
            kv_copy(n, i, s).wait_send()
            part_copy(n, i, s).wait_send()
        gz_copy(i, across if i == 2 else e).wait_send()
    for c in range(len(pieces)):
        for i in range(3):
            raw_copy(c, i, s).wait_send()
        for n in parts:
            hz_copy(c, n).wait_send()
    if packed:

        @pl.when(inner)
        def _():
            for c in range(len(pieces)):
                for z in others:
                    relay_copy(c, z).wait_send()


def line_call(K, number, ids, gates, grad_out, queries, keys, values, hidden):
    E, S = lax.axis_size("expert"), lax.axis_size("seq")
    T, D = grad_out.shape
    U = hidden.shape[2] // S
    C = -(-(7 * T // (2 * E)) // 16) * 16
    KD = keys.shape[1]
    W, rows, half = S * C, 2 * T, U // 2
    bf, f32 = jnp.bfloat16, jnp.float32
    vm = pl.BlockSpec(memory_space=pltpu.VMEM)
    dma = pltpu.SemaphoreType.DMA
    P_ = len(line_pieces(half))
    tiles = len(line_tiles(half))
    return pl.pallas_call(
        functools.partial(line_kernel, (E, S, T, C, U, D, K)),
        out_shape=(
            pltpu.VMEM((half, D), bf),
            pltpu.VMEM((T, D), bf),
            pltpu.VMEM((T, KD), bf),
            pltpu.VMEM((T, KD), bf),
            jax.ShapeDtypeStruct((8, 128), f32),
        ),
        in_specs=[vm] * 6 + [pl.BlockSpec(memory_space=pl.ANY)],
        out_specs=(vm,) * 5,
        scratch_shapes=[
            pltpu.VMEM((E, S + 1, 8, rows), f32),
            pltpu.VMEM((8, 128), f32),
            pltpu.VMEM((8, 128), f32),
            pltpu.VMEM((S, T, KD), bf),
            pltpu.VMEM((S, T, KD), bf),
            pltpu.VMEM((S, T, 2, U), bf),
            pltpu.VMEM((2 * W + K, S * rows), bf),
            pltpu.VMEM((W + K, U), bf),
            pltpu.VMEM((E, W, U), bf),
            pltpu.VMEM((E, T, D), bf),
            pltpu.VMEM((E, S, C, D), bf),
            pltpu.VMEM((S, T, KD), bf),
            pltpu.VMEM((S, T, KD), bf),
            pltpu.VMEM((S, T, KD), f32),
            pltpu.VMEM((S, T, KD), f32),
            pltpu.VMEM((S, T, KD), bf),
            pltpu.VMEM((S, T, KD), bf),
            pltpu.VMEM((half, D), bf),
            dma((2, 3)), dma((2, 3)), dma((P_,)), dma((P_, 3)), dma((P_, 3)), dma((3,)), dma((3,)),
            dma((E, 4)), dma((E, 4)), dma((P_, 4)), dma((P_, E)), dma((P_, E)), dma((P_, E)), dma((P_, E)),
            dma((2, 3)), dma((2, 3)), dma((tiles,)), dma((tiles,)), dma((7,)), dma((7,)),
        ],
        compiler_params=pltpu.CompilerParams(
            collective_id=number, has_side_effects=True, vmem_limit_bytes=50 * 1024 * 1024
        ),
    )(ids, gates, grad_out, queries, keys, values, hidden)


def publish_kernel(*refs):
    n = (len(refs) - 1) // 2
    copies = []
    for a in range(n):
        count = 8 if a == 0 else 1
        size = refs[a].shape[0] // count
        for c in range(count):
            part = pl.ds(c * size, size)
            copies.append(
                pltpu.make_async_copy(refs[a].at[part], refs[n + a].at[part], refs[-1].at[len(copies)])
            )
    for copy in copies:
        copy.start()
    for copy in copies:
        copy.wait()


def publish(*grads):
    hbm = pl.BlockSpec(memory_space=pl.ANY)
    return pl.pallas_call(
        publish_kernel,
        out_shape=tuple(jax.ShapeDtypeStruct(g.shape, g.dtype) for g in grads),
        in_specs=[hbm] * len(grads),
        out_specs=(hbm,) * len(grads),
        scratch_shapes=[pltpu.SemaphoreType.DMA((8 + len(grads) - 1,))],
        compiler_params=pltpu.CompilerParams(vmem_limit_bytes=1024 * 1024),
    )(*grads)


def on_line(grad_out, expert_ids, gate_weights, hidden, queries, keys, values):
    E, S = lax.axis_size("expert"), lax.axis_size("seq")
    C = -(-(7 * grad_out.shape[1] // (2 * E)) // 16) * 16
    operands = (expert_ids[0].T, gate_weights[0].T, grad_out[0], queries[0], keys[0], values[0], hidden[0])
    full = 2 * S * C
    tight = full * 6 // 7 // 16 * 16
    *grads, most = line_call(tight, 0, *operands)
    grads = publish(*grads)

    def kept(grads, operands):
        return tuple(grads)

    def again(grads, operands):
        return tuple(publish(*line_call(full, 1, *operands)[:4]))

    eg, gq, gk, gv = lax.cond(most[0, 0] <= float(tight), kept, again, grads, operands)
    return (eg[None], gq[None], gk[None], gv[None])


def solution(mesh):
    split = P(("expert", "dp"), "seq", None)
    in_specs = (split, split, split, P(("expert", "dp"), "seq", None, None), split, split, split)
    out_specs = (P("expert", ("seq", "dp"), None), split, split, split)
    body = on_line if mesh.shape["expert"] == 4 and mesh.shape["seq"] == 4 else on_device
    return jax.shard_map(
        body, mesh=mesh, in_specs=in_specs, out_specs=out_specs, check_vma=False
    )
```

```python
import functools

import jax
import jax.numpy as jnp
from jax import lax
from jax.experimental import pallas as pl
from jax.experimental.pallas import tpu as pltpu
from jax.sharding import PartitionSpec as P

HEADS = 16
KV_HEADS = 4
HEAD_DIM = 128
GROUP = HEADS // KV_HEADS
MESH = pl.DeviceIdType.MESH


def dot(a, b, contract):
    return lax.dot_general(a, b, (contract, ((), ())), preferred_element_type=jnp.float32)


def routing_codes(ids, order_row, order_col, experts, capacity):
    count = max(8, experts)
    rows = ids.shape[1]
    expert_of = lax.broadcasted_iota(jnp.int32, (count, rows), 0).astype(jnp.float32)
    onehot = (expert_of == ids).astype(jnp.float32)
    earlier = (order_col < order_row).astype(jnp.float32)
    before = dot(onehot.astype(jnp.bfloat16), earlier.astype(jnp.bfloat16), ((1,), (0,)))
    slot = jnp.sum(before * onehot, axis=0, keepdims=True)
    return ids * float(capacity) + slot


def spreads(experts):
    return experts <= 8 and experts & (experts - 1) == 0


def kernel(
    dims,
    ids_t, info, go, q, k, v, hid,
    eg_out, gq_out, gk_out, gv_out,
    kbuf, vbuf, idbuf, hraw, hsend, hrecv, gsend, grecv, infos,
    kpart, vpart, kown, vown, kin, vin, precv,
    small_send, small_recv, local_sem, hraw_send, hraw_recv,
    gz_send, gz_recv, gi_send, gi_recv, gs_send, gs_recv, hz_send, hz_recv,
    part_send, part_recv, pair_send, pair_recv,
):
    E, S, T, C, U, D = dims
    half = U // 2
    first = -(-half // 256) * 128
    pieces = [(n, o, w) for n in range(2) for o, w in ((0, first), (first, half - first)) if w > 0]
    spread = spreads(E)
    e = lax.axis_index("expert")
    s = lax.axis_index("seq")
    d = lax.axis_index("dp")
    seq_peer = [lax.rem(s + i, S) for i in range(S)]
    bases = [
        pl.multiple_of((d if n else 1 - d) * half + o, 128) for n, o, _ in pieces
    ]

    def ex_peer(j):
        return lax.rem(e + j, E)

    barrier = pltpu.get_barrier_semaphore()
    for i in range(1, S):
        pl.semaphore_signal(barrier, inc=1, device_id={"seq": seq_peer[i]}, device_id_type=MESH)

    @pl.loop(1, E)
    def _(j):
        pl.semaphore_signal(barrier, inc=1, device_id={"expert": ex_peer(j)}, device_id_type=MESH)

    pl.semaphore_signal(barrier, inc=1, device_id={"dp": 1 - d}, device_id_type=MESH)
    pl.semaphore_wait(barrier, S + E - 1)

    def send(src, dst, ssem, rsem, where):
        return pltpu.make_async_remote_copy(
            src_ref=src, dst_ref=dst, send_sem=ssem, recv_sem=rsem,
            device_id=where, device_id_type=MESH,
        )

    def small_copy(n, i, slot):
        src, dst = ((ids_t, idbuf), (k, kbuf), (v, vbuf))[n]
        return send(src, dst.at[slot], small_send.at[n, i], small_recv.at[n, slot], {"seq": seq_peer[i]})

    def raw_copy(c, i, slot):
        width = pieces[c][2]
        cols = pl.ds(pl.multiple_of(seq_peer[i] * U + bases[c], 128), width)
        return send(
            hid.at[:, :, cols], hraw.at[slot, :, :, pl.ds(bases[c], width)],
            hraw_send.at[c, i], hraw_recv.at[c, slot], {"seq": seq_peer[i]},
        )

    own_cols = pl.ds(pl.multiple_of(s * U, 128), U)
    own_raw = pltpu.make_async_copy(hid.at[:, :, own_cols], hraw.at[s], local_sem.at[0])
    own_raw.start()
    for i in range(1, S):
        for n in range(3):
            small_copy(n, i, s).start()
    for c in range(len(pieces)):
        for i in range(1, S):
            raw_copy(c, i, s).start()
    kbuf[s] = k[...]
    vbuf[s] = v[...]
    idbuf[s] = ids_t[...]

    rows = 2 * T
    col = lax.broadcasted_iota(jnp.int32, (rows, rows), 1)
    row = lax.broadcasted_iota(jnp.int32, (rows, rows), 0)
    place = lax.broadcasted_iota(jnp.int32, (E * C, rows), 0).astype(jnp.float32)

    def expert_rows(p):
        return pl.ds(pl.multiple_of(p * C, 16), C)

    def gs_copy(i, z, slot):
        return send(grecv.at[s, z], grecv.at[slot, z], gs_send.at[i, z], gs_recv.at[slot, z], {"seq": seq_peer[i]})

    def gs_wait(i, z):
        slot = seq_peer[i]
        send(grecv.at[s, z], grecv.at[slot, z], gs_send.at[i, z], gs_recv.at[slot, z], {"seq": slot}).wait_recv()

    def packed_grads(ids, gates, grads, wanted):
        code = routing_codes(
            ids, 2 * lax.rem(col, T) + col // T, 2 * lax.rem(row, T) + row // T, E, C
        )
        picks = (wanted == code).astype(jnp.float32)
        gate = jnp.sum(picks * gates, axis=1, keepdims=True)
        token_picks = (picks[:, :T] + picks[:, T:]).astype(jnp.bfloat16)
        return (dot(token_picks, grads, ((1,), (0,))) * gate).astype(jnp.bfloat16)

    if spread:
        def flip(at, b):
            return at + b - 2 * b * lax.rem(at // b, 2)

        bits = []
        b = E // 2
        while b >= 1:
            bits.append(b)
            b //= 2

        def masks(n):
            held = [0]
            for bit in bits[:n]:
                held = held + [m + bit for m in held]
            return held

        def at_mask(m):
            at = e
            for bit in bits:
                if m & bit:
                    at = flip(at, bit)
            return at

        def gz_pair(m, n, slot):
            to = {"expert": flip(e, bits[n])}
            key = m + bits[n]
            return (
                send(gsend.at[slot], gsend.at[slot], gz_send.at[key], gz_recv.at[slot], to),
                send(infos.at[slot], infos.at[slot], gi_send.at[key], gi_recv.at[slot], to),
            )

        def forward(m):
            z = at_mask(m)
            wanted = (
                lax.broadcasted_iota(jnp.int32, (C, rows), 0) + e * C
            ).astype(jnp.float32)
            grecv[s, z] = packed_grads(infos[z, 0:1, :], infos[z, 8:9, :], gsend[z], wanted)
            for i in range(1, S):
                gs_copy(i, z, s).start()

        def arrive(m, n):
            for copy in gz_pair(m, n, at_mask(m + bits[n])):
                copy.wait_recv()
            for later in range(n + 1, len(bits)):
                for copy in gz_pair(m + bits[n], later, at_mask(m + bits[n])):
                    copy.start()

        gsend[e] = go[...]
        infos[e] = info[...]
        for n in range(len(bits)):
            for copy in gz_pair(0, n, e):
                copy.start()
    else:

        def gz_copy(j, slot):
            p = ex_peer(j)
            return send(gsend.at[expert_rows(p)], grecv.at[s, slot], gz_send.at[j], gz_recv.at[slot], {"expert": p})

        gsend[...] = packed_grads(info[0:1, :], info[8:9, :], go[...], place)

        @pl.loop(1, E)
        def _(j):
            gz_copy(j, e).start()

        grecv[s, e] = gsend[expert_rows(e)]
        for i in range(1, S):
            gs_copy(i, e, s).start()

    def hz_copy(c, i, j, slot):
        p = ex_peer(j)
        src = seq_peer[i]
        units = pl.ds(bases[c], pieces[c][2])
        return send(
            hsend.at[src, expert_rows(p), units], hrecv.at[src, slot, :, units],
            hz_send.at[c, src, j], hz_recv.at[c, src, slot], {"expert": p},
        )

    def pack_hidden(c, i):
        src = seq_peer[i]
        width = pieces[c][2]
        units = pl.ds(bases[c], width)
        hcode = routing_codes(idbuf[src, 0:1, :], col, row, E, C)
        hpicks = (place == hcode).astype(jnp.bfloat16)
        hsend[src, :, units] = dot(
            hpicks, hraw[src, :, :, units].reshape(rows, width), ((1,), (0,))
        ).astype(jnp.bfloat16)

        @pl.loop(1, E)
        def _(j):
            hz_copy(c, i, j, e).start()

        hrecv[src, e, :, units] = hsend[src, expert_rows(e), units]

    own_raw.wait()
    for c in range(len(pieces)):
        pack_hidden(c, 0)
    if spread:
        forward(0)

    scale = HEAD_DIM ** (-0.5)
    length = S * T

    def attention(j):
        lanes = slice(j * HEAD_DIM, (j + 1) * HEAD_DIM)
        heads = [slice(h * HEAD_DIM, (h + 1) * HEAD_DIM) for h in range(j * GROUP, (j + 1) * GROUP)]
        qs = jnp.concatenate([q[:, h] for h in heads], axis=0)
        gs = jnp.concatenate([go[:, h] for h in heads], axis=0)
        kj = kbuf[:, :, lanes].reshape(length, HEAD_DIM)
        vj = vbuf[:, :, lanes].reshape(length, HEAD_DIM)
        scores = dot(qs, kj, ((1,), (1,))) * scale
        raised = jnp.exp(scores - jnp.max(scores, axis=-1, keepdims=True))
        probs = raised / jnp.sum(raised, axis=-1, keepdims=True)
        dprobs = dot(gs, vj, ((1,), (1,)))
        delta = jnp.sum(probs * dprobs, axis=-1, keepdims=True)
        ds = (probs * (dprobs - delta)).astype(jnp.bfloat16)
        dv = dot(probs.astype(jnp.bfloat16), gs, ((0,), (0,)))
        dk = dot(ds, qs, ((0,), (0,))) * scale
        dq = dot(ds, kj, ((1,), (0,))) * scale
        for n, h in enumerate(heads):
            gq_out[:, h] = dq[n * T : (n + 1) * T].astype(jnp.bfloat16)
        dk = dk.reshape(S, T, HEAD_DIM)
        dv = dv.reshape(S, T, HEAD_DIM)
        kown[:, :, lanes] = dk
        vown[:, :, lanes] = dv
        kpart[:, :, lanes] = dk.astype(jnp.bfloat16)
        vpart[:, :, lanes] = dv.astype(jnp.bfloat16)

    for i in range(1, S):
        for n in range(3):
            small_copy(n, i, seq_peer[i]).wait_recv()

    attention(0)

    if spread:
        attention(1)
        for n in range(len(bits)):
            for m in masks(n):
                arrive(m, n)
                forward(m + bits[n])
    else:

        @pl.loop(1, E)
        def _(j):
            z = ex_peer(j)
            gz_copy(j, z).wait_recv()
            for i in range(1, S):
                gs_copy(i, z, s).start()

        attention(1)
    for c in range(len(pieces)):
        for i in range(1, S):
            raw_copy(c, i, seq_peer[i]).wait_recv()
            pack_hidden(c, i)
        if c + 2 < KV_HEADS:
            attention(c + 2)
    for j in range(len(pieces) + 2, KV_HEADS):
        attention(j)

    def part_copy(n, i, slot):
        src, dst = ((kpart, kin), (vpart, vin))[n]
        return send(src.at[seq_peer[i]], dst.at[slot], part_send.at[n, i], part_recv.at[n, slot], {"seq": seq_peer[i]})

    for i in range(1, S):
        for n in range(2):
            part_copy(n, i, s).start()
    for n, (own, got, out) in enumerate(((kown, kin, gk_out), (vown, vin, gv_out))):
        total = own[s]
        for i in range(1, S):
            part_copy(n, i, seq_peer[i]).wait_recv()
            total = total + got[seq_peer[i]].astype(jnp.float32)
        out[...] = total.astype(jnp.bfloat16)

    @pl.loop(0, E)
    def _(z):
        for i in range(1, S):
            gs_wait(i, z)

    wide = 256
    tiles = [
        (o + t, min(wide, w - t)) for n, o, w in pieces if n == 0 for t in range(0, w, wide)
    ]

    def arrived(n, off):
        for c, (m, o, _) in enumerate(pieces):
            if m == n and o == off:

                @pl.loop(1, E)
                def _(j):
                    for i in range(S):
                        hz_copy(c, i, j, ex_peer(j)).wait_recv()

    def product(base, off, width):
        units = pl.ds(pl.multiple_of(base + off, 128), width)
        h = hrecv[:, :, :, units].reshape(S * E * C, width)
        return dot(h, grecv[...].reshape(S * E * C, D), ((0,), (0,)))

    def pair_copy(n):
        off, width = tiles[n]
        return send(eg_out.at[off : off + width], precv.at[off : off + width], pair_send.at[n], pair_recv.at[n], {"dp": 1 - d})

    for n, (off, width) in enumerate(tiles):
        arrived(0, off)
        eg_out[off : off + width, :] = product((1 - d) * half, off, width).astype(jnp.bfloat16)
        pair_copy(n).start()
    for n, (off, width) in enumerate(tiles):
        arrived(1, off)
        mine = product(d * half, off, width)
        pair_copy(n).wait_recv()
        pair_copy(n).wait_send()
        got = precv[off : off + width, :].astype(jnp.float32)
        eg_out[off : off + width, :] = (mine + got).astype(jnp.bfloat16)

    for i in range(1, S):
        for n in range(3):
            small_copy(n, i, s).wait_send()
        for n in range(2):
            part_copy(n, i, s).wait_send()
        for c in range(len(pieces)):
            raw_copy(c, i, s).wait_send()

    @pl.loop(0, E)
    def _(z):
        for i in range(1, S):
            gs_copy(i, z, s).wait_send()

    @pl.loop(1, E)
    def _(j):
        if not spread:
            gz_copy(j, e).wait_send()
        for i in range(S):
            for c in range(len(pieces)):
                hz_copy(c, i, j, e).wait_send()

    if spread:
        for n in range(len(bits)):
            for m in masks(n):
                for copy in gz_pair(m, n, at_mask(m)):
                    copy.wait_send()


def on_device(grad_out, expert_ids, gate_weights, hidden, queries, keys, values):
    E = lax.axis_size("expert")
    S = lax.axis_size("seq")
    T = grad_out.shape[1]
    D = grad_out.shape[2]
    U = hidden.shape[3] // S
    C = -(-(7 * T // (2 * E)) // 16) * 16
    KD = keys.shape[2]
    rows = 2 * T
    bf, f32 = jnp.bfloat16, jnp.float32
    ids = expert_ids[0].astype(f32)
    ids_t = jnp.broadcast_to(ids.reshape(1, rows), (8, rows))
    ids_k = jnp.broadcast_to(ids.T.reshape(1, rows), (8, rows))
    gates_k = jnp.broadcast_to(gate_weights[0].T.reshape(1, rows), (8, rows))
    tiles = -(-(U // 2) // 256)
    info = jnp.concatenate([ids_k, gates_k], axis=0)
    sent = (E, T, D) if spreads(E) else (E * C, D)
    vm = pl.BlockSpec(memory_space=pltpu.VMEM)
    dma = pltpu.SemaphoreType.DMA
    eg, gq, gk, gv = pl.pallas_call(
        functools.partial(kernel, (E, S, T, C, U, D)),
        out_shape=(
            jax.ShapeDtypeStruct((U // 2, D), bf),
            jax.ShapeDtypeStruct((T, queries.shape[2]), bf),
            jax.ShapeDtypeStruct((T, KD), bf),
            jax.ShapeDtypeStruct((T, KD), bf),
        ),
        in_specs=[vm] * 6 + [pl.BlockSpec(memory_space=pl.ANY)],
        out_specs=(vm,) * 4,
        scratch_shapes=[
            pltpu.VMEM((S, T, KD), bf),
            pltpu.VMEM((S, T, KD), bf),
            pltpu.VMEM((S, 8, rows), f32),
            pltpu.VMEM((S, T, 2, U), bf),
            pltpu.VMEM((S, E * C, U), bf),
            pltpu.VMEM((S, E, C, U), bf),
            pltpu.VMEM(sent, bf),
            pltpu.VMEM((S, E, C, D), bf),
            pltpu.VMEM((E if spreads(E) else 1, 16, rows), f32),
            pltpu.VMEM((S, T, KD), bf),
            pltpu.VMEM((S, T, KD), bf),
            pltpu.VMEM((S, T, KD), f32),
            pltpu.VMEM((S, T, KD), f32),
            pltpu.VMEM((S, T, KD), bf),
            pltpu.VMEM((S, T, KD), bf),
            pltpu.VMEM((U // 2, D), bf),
            dma((3, S)), dma((3, S)), dma((1,)), dma((4, S)), dma((4, S)),
            dma((E,)), dma((E,)), dma((E,)), dma((E,)), dma((S, E)), dma((S, E)), dma((4, S, E)), dma((4, S, E)),
            dma((2, S)), dma((2, S)), dma((tiles,)), dma((tiles,)),
        ],
        compiler_params=pltpu.CompilerParams(
            collective_id=0, has_side_effects=True, vmem_limit_bytes=62 * 1024 * 1024
        ),
    )(ids_t, info, grad_out[0], queries[0], keys[0], values[0], hidden[0])
    return (eg[None], gq[None], gk[None], gv[None])


def flip(at, b):
    return at + b - 2 * b * lax.rem(at // b, 2)


def greet(peers):
    barrier = pltpu.get_barrier_semaphore()
    for peer in peers:
        pl.semaphore_signal(barrier, inc=1, device_id=peer, device_id_type=MESH)
    pl.semaphore_wait(barrier, len(peers))


def send(src, dst, ssem, rsem, where):
    return pltpu.make_async_remote_copy(
        src_ref=src, dst_ref=dst, send_sem=ssem, recv_sem=rsem,
        device_id=where, device_id_type=MESH,
    )


def line_pieces(half):
    cut = min(384, half)
    return [(0, 0, cut), (0, cut, half - cut), (1, 0, half - 256), (1, half - 256, 256)]


def line_tiles(half):
    edges = sorted({0, half} | {p[1] for p in line_pieces(half)})
    return [
        (lo + t, min(256, hi - lo - t)) for lo, hi in zip(edges, edges[1:]) for t in range(0, hi - lo, 256)
    ]


def line_kernel(
    dims,
    ids_in, gates_in, go, q, k, v, hid,
    eg_out, gq_out, gk_out, gv_out, most,
    info, peak, peak_in,
    kbuf, vbuf, hraw, picks, hsend, hrecv, gsend, grecv,
    kpart, vpart, kown, vown, kin, vin, precv,
    kv_send, kv_recv, local_sem, raw_send, raw_recv, gz_send, gz_recv, gs_send, gs_recv,
    hz_send, hz_recv, shared_recv, relay_send, relay_recv, part_send, part_recv, pair_send, pair_recv,
    info_send, info_recv,
):
    E, S, T, C, U, D, K = dims
    W = S * C
    half = U // 2
    rows = 2 * T
    packed = K < 2 * W
    parts = range(0 if packed else 1, 4)
    both = 2 * W - K
    pieces = line_pieces(half)
    tiles = line_tiles(half)
    e, s, d = (lax.axis_index(n) for n in ("expert", "seq", "dp"))
    side = e // 2
    friend, across, corner = flip(e, 1), flip(e, 2), flip(flip(e, 1), 2)
    near, far = 2 - side, 3 - 3 * side
    inner = jnp.logical_or(e == 1, e == 2)
    outer = jnp.logical_not(inner)
    others = [2 - 2 * side, 3 - 2 * side]
    peers = [flip(s, 1), flip(s, 2), flip(flip(s, 1), 2)]
    bases = [pl.multiple_of((d if n else 1 - d) * half + o, 128) for n, o, _ in pieces]
    greet([{"seq": p} for p in peers] + [{"expert": p} for p in (friend, across, corner)] + [{"dp": 1 - d}])

    def cols(c):
        return pl.ds(bases[c], pieces[c][2])

    def kv_copy(n, i, slot):
        src, dst = ((k, kbuf), (v, vbuf))[n]
        return send(src, dst.at[slot], kv_send.at[n, i], kv_recv.at[n, i], {"seq": peers[i]})

    def raw_copy(c, i, slot):
        there = pl.ds(pl.multiple_of(peers[i] * U + bases[c], 128), pieces[c][2])
        return send(
            hid.at[:, :, there], hraw.at[slot, :, :, cols(c)],
            raw_send.at[c, i], raw_recv.at[c, i], {"seq": peers[i]},
        )

    def own_copy(c):
        here = pl.ds(pl.multiple_of(s * U + bases[c], 128), pieces[c][2])
        return pltpu.make_async_copy(hid.at[:, :, here], hraw.at[s, :, :, cols(c)], local_sem.at[c])

    def gz_copy(n, slot):
        src = go if n < 2 else gsend.at[across]
        dst = gsend.at[slot]
        to = across if n == 0 else friend
        return send(src, dst, gz_send.at[n], gz_recv.at[n], {"expert": to})

    z_peers = [friend, across, corner]

    def line(ref):
        flat = jnp.concatenate([ref[0:1, :], ref[1:2, :]], axis=1).astype(jnp.float32)
        return jnp.broadcast_to(flat, (1, 8, rows))

    def info_copy(i, slot):
        if i < 3:
            return send(info.at[e, s], info.at[e, slot], info_send.at[i], info_recv.at[i], {"seq": peers[i]})
        return send(info.at[e], info.at[slot], info_send.at[i], info_recv.at[i], {"expert": z_peers[i - 3]})

    info[e, pl.ds(s, 1)] = line(ids_in)
    info[e, S : S + 1] = line(gates_in)
    for i in range(3):
        info_copy(i, s).start()
    gz_copy(0, e).start()
    gz_copy(1, e).start()
    for c in range(len(pieces)):
        own_copy(c).start()
        for i in range(3):
            raw_copy(c, i, s).start()
    for i in range(3):
        for n in range(2):
            kv_copy(n, i, s).start()
    kbuf[s] = k[...]
    vbuf[s] = v[...]

    col = lax.broadcasted_iota(jnp.int32, (rows, rows), 1)
    row = lax.broadcasted_iota(jnp.int32, (rows, rows), 0)
    f32, bf = jnp.float32, jnp.bfloat16
    experts = lax.broadcasted_iota(jnp.int32, (8, rows), 0).astype(f32)
    by_place = (col < row).astype(bf)
    interleave = (row == lax.rem(col, 2) * T + col // 2).astype(bf)
    in_order = (row < col).astype(bf)
    k_order = (2 * lax.rem(row, T) + row // T < 2 * lax.rem(col, T) + col // T).astype(bf)

    def ranked(ids, earlier):
        onehot = (experts == ids).astype(f32)
        return onehot, dot(onehot.astype(bf), earlier, ((1,), (0,)))

    for i in range(3):
        info_copy(i, peers[i]).wait_recv()
    for i in range(3):
        info_copy(3 + i, e).start()
    total = 2 * W + K
    offsets = jnp.zeros((8, 1), f32)
    places = lax.broadcasted_iota(jnp.int32, (128, rows), 0).astype(f32)

    def mark(b, start):
        ids = dot(info[e, b].astype(bf), interleave, ((1,), (0,)))[0:1, :]
        onehot, before = ranked(ids, in_order)
        rank = jnp.sum(onehot * (before + start), axis=0, keepdims=True)
        back = (W + K - 1) - rank if packed else K + rank
        code = jnp.where(
            ids == friend.astype(f32), rank,
            jnp.where(
                ids == e.astype(f32), W + K + rank,
                jnp.where(ids == near.astype(f32), W + rank, back),
            ),
        )

        @pl.loop(0, total // 128)
        def _(r):
            at = places + (128 * r).astype(f32)
            picks[pl.ds(pl.multiple_of(128 * r, 128), 128), b * rows : (b + 1) * rows] = (at == code).astype(bf)

        return start + jnp.sum(onehot, axis=1, keepdims=True)

    for b in range(S):
        offsets = mark(b, offsets if packed else float(C * b))

    def gs_copy(z, n):
        to = peers[0] if n in (0, 3) else peers[1]
        slot = (s, s, peers[0], peers[1])[n]
        lanes = (slice(0, D), slice(0, D), slice(0, D // 2), slice(D // 2, D))[n]
        block = grecv.at[z, slot, :, lanes]
        return send(block, block, gs_send.at[z, n], gs_recv.at[z, n], {"seq": to})

    def gs_wait(z, n):
        slot = (peers[0], peers[1], peers[2], peers[2])[n]
        lanes = (slice(0, D), slice(0, D), slice(0, D // 2), slice(D // 2, D))[n]
        block = grecv.at[z, slot, :, lanes]
        send(block, block, gs_send.at[z, n], gs_recv.at[z, n], {"seq": peers[0]}).wait_recv()

    wanted = lax.broadcasted_iota(jnp.int32, (C, rows), 0).astype(f32)

    def forward(z, grads):
        ids = info[z, pl.ds(s, 1)][0, 0:1, :]
        onehot, before = ranked(ids, k_order)
        rank = jnp.sum(before * onehot, axis=0, keepdims=True)
        code = jnp.where(ids == e.astype(f32), rank, -1.0)
        chosen = (wanted == code).astype(f32)
        gate = jnp.sum(chosen * info[z, 4, 0:1, :], axis=1, keepdims=True)
        token = (chosen[:, :T] + chosen[:, T:]).astype(bf)
        grecv[z, pl.ds(s, 1)] = (dot(token, grads, ((1,), (0,))) * gate).astype(bf)[None]
        for n in range(2):
            gs_copy(z, n).start()

    def pass_on(z):
        for n in range(2):
            gs_wait(z, n)
            gs_copy(z, 2 + n).start()

    def hz_copy(c, n):
        units = cols(c)
        to = (near, far, near, friend)[n]
        first, low, high = ((K, K - W, W), (2 * W, both, W), (W, 0, K - W), (0, 0, W))[n]
        src = hsend.at[first : first + high - low, units]
        landed = shared_recv if n == 0 else hz_recv
        return send(src, hrecv.at[e, low:high, units], hz_send.at[c, n], landed.at[c, e], {"expert": to})

    def hz_wait(c, z, low, high, landed):
        block = hrecv.at[z, low:high, cols(c)]
        send(block, block, hz_send.at[c, 0], landed.at[c, z], {"expert": friend}).wait_recv()

    def relay_copy(c, z):
        return send(
            hrecv.at[z, K - W : W, cols(c)], hrecv.at[z, 0:both, cols(c)],
            relay_send.at[c, z], relay_recv.at[c, z], {"expert": friend},
        )

    def pack(c):
        own_copy(c).wait()
        for i in range(3):
            raw_copy(c, i, peers[i]).wait_recv()
        width = pieces[c][2]
        sent = (W + K) // 4

        def gather(t, size):
            units = pl.ds(pl.multiple_of(bases[c] + t, 128), size)
            block = hraw[:, :, :, units].reshape(S * rows, size)

            @pl.loop(0, 4)
            def _(r):
                some = pl.ds(pl.multiple_of(r * sent, 16), sent)
                hsend[some, units] = dot(picks[some, :], block, ((1,), (0,))).astype(bf)

            hrecv[pl.ds(e, 1), :, units] = dot(picks[W + K :, :], block, ((1,), (0,))).astype(bf)[None]

        if width >= 256:

            @pl.loop(0, width // 256)
            def _(t):
                gather(t * 256, 256)

        if width % 256:
            gather(width - 128, 128)
        for n in parts:
            hz_copy(c, n).start()

    def relay(c):
        if packed:

            @pl.when(inner)
            def _():
                for z in others:
                    hz_wait(c, z, K - W, W, shared_recv)
                    relay_copy(c, z).start()

    def arrived(c):
        hz_wait(c, friend, 0, W, hz_recv)

        @pl.when(inner)
        def _():
            for z in others:
                hz_wait(c, z, 0, K - W, hz_recv)

        @pl.when(outer)
        def _():
            for z in others:
                hz_wait(c, z, both, W, hz_recv)
                if packed:
                    relay_copy(c, z).wait_recv()

    scale = HEAD_DIM ** (-0.5)
    length = S * T

    def attention(j):
        def lanes_of(h):
            return pl.ds(pl.multiple_of(h * HEAD_DIM, HEAD_DIM), HEAD_DIM)

        lanes = lanes_of(j)
        heads = [lanes_of(j * GROUP + n) for n in range(GROUP)]
        qs = jnp.concatenate([q[:, h] for h in heads], axis=0)
        gs = jnp.concatenate([go[:, h] for h in heads], axis=0)
        kj = kbuf[:, :, lanes].reshape(length, HEAD_DIM)
        vj = vbuf[:, :, lanes].reshape(length, HEAD_DIM)
        scores = dot(qs, kj, ((1,), (1,))) * scale
        raised = jnp.exp(scores - jnp.max(scores, axis=-1, keepdims=True))
        probs = raised / jnp.sum(raised, axis=-1, keepdims=True)
        dprobs = dot(gs, vj, ((1,), (1,)))
        delta = jnp.sum(probs * dprobs, axis=-1, keepdims=True)
        ds = (probs * (dprobs - delta)).astype(jnp.bfloat16)
        dv = dot(probs.astype(jnp.bfloat16), gs, ((0,), (0,)))
        dk = dot(ds, qs, ((0,), (0,))) * scale
        dq = dot(ds, kj, ((1,), (0,))) * scale
        for n, h in enumerate(heads):
            gq_out[:, h] = dq[n * T : (n + 1) * T].astype(jnp.bfloat16)
        dk = dk.reshape(S, T, HEAD_DIM)
        dv = dv.reshape(S, T, HEAD_DIM)
        kown[:, :, lanes] = dk
        vown[:, :, lanes] = dv
        kpart[:, :, lanes] = dk.astype(jnp.bfloat16)
        vpart[:, :, lanes] = dv.astype(jnp.bfloat16)

    pack(0)
    forward(e, go[...])
    pack(1)
    for i in range(3):
        info_copy(3 + i, z_peers[i]).wait_recv()
    gz_copy(0, across).wait_recv()
    gz_copy(2, across).start()
    forward(across, gsend[across])
    pack(2)
    gz_copy(1, friend).wait_recv()
    forward(friend, gsend[friend])
    pack(3)
    relay(0)
    for i in range(3):
        for n in range(2):
            kv_copy(n, i, peers[i]).wait_recv()
    pl.loop(0, KV_HEADS)(attention)
    relay(1)
    pass_on(e)
    gz_copy(2, corner).wait_recv()
    forward(corner, gsend[corner])
    pass_on(across)
    pass_on(friend)

    top = jnp.zeros((1, 1), f32)
    for z in range(E):
        crossing = jnp.zeros((1, rows), f32)
        for b in range(S):
            high = (info[z, b, 0:1, :] >= float(E // 2)).astype(f32)
            crossing = crossing + (high if z < E // 2 else 1.0 - high)
        top = jnp.maximum(top, jnp.sum(crossing, axis=1, keepdims=True))
    peak[...] = jnp.broadcast_to(top, (8, 128))
    top_copy = send(peak, peak_in, info_send.at[6], info_recv.at[6], {"dp": 1 - d})
    top_copy.start()

    def part_copy(n, i, slot):
        src, dst = ((kpart, kin), (vpart, vin))[n]
        return send(src.at[peers[i]], dst.at[slot], part_send.at[n, i], part_recv.at[n, i], {"seq": peers[i]})

    for i in range(3):
        for n in range(2):
            part_copy(n, i, s).start()
    relay(2)
    pass_on(corner)
    for n, (own, got, out) in enumerate(((kown, kin, gk_out), (vown, vin, gv_out))):
        summed = own[s]
        for i in range(3):
            part_copy(n, i, peers[i]).wait_recv()
            summed = summed + got[peers[i]].astype(jnp.float32)
        out[...] = summed.astype(jnp.bfloat16)

    def settle(z):
        for n in (2, 3):
            gs_wait(z, n)
        for n in range(4):
            gs_copy(z, n).wait_send()
        if not packed:
            return
        slots = lax.broadcasted_iota(jnp.int32, (1, W), 1).astype(f32)
        code = jnp.full((1, W), -1.0, f32)
        start = jnp.zeros((1, 1), f32)
        for b in range(S):
            named = (info[z, b, 0:1, :] == e.astype(f32)).astype(f32)
            count = jnp.sum(named, axis=1, keepdims=True)
            inside = jnp.logical_and(slots >= float(C * b), slots - float(C * b) < count)
            inside = jnp.logical_and(inside, slots < float(C * (b + 1)))
            code = jnp.where(inside, slots - float(C * b) + start, code)
            start = start + count
        turned = jnp.logical_and(z // 2 != side, outer).astype(f32)
        code = jnp.where(code >= 0.0, code + turned * (float(W - 1) - 2.0 * code), code)
        moves = (lax.broadcasted_iota(jnp.int32, (W, W), 0).astype(f32) == code).astype(bf)

        @pl.loop(0, D // 512)
        def _(t):
            lanes = pl.ds(pl.multiple_of(t * 512, 512), 512)
            block = grecv[z, :, :, lanes].reshape(W, 512)
            grecv[z, :, :, lanes] = dot(moves, block, ((1,), (0,))).astype(bf).reshape(S, C, 512)

    pl.loop(0, E)(settle)

    def product(base, off, width, use):
        units = pl.ds(pl.multiple_of(base + off, 128), width)
        here = pl.ds(off, width)

        @pl.loop(0, D // 1024)
        def _(t):
            lanes = pl.ds(pl.multiple_of(t * 1024, 1024), 1024)
            h = hrecv[:, :, units].reshape(E * W, width)
            use(here, lanes, dot(h, grecv[:, :, :, lanes].reshape(E * W, 1024), ((0,), (0,))))

    def give(here, lanes, value):
        eg_out[here, lanes] = value.astype(jnp.bfloat16)

    def take(here, lanes, value):
        eg_out[here, lanes] = (value + precv[here, lanes].astype(jnp.float32)).astype(jnp.bfloat16)

    def pair_copy(n):
        off, width = tiles[n]
        return send(eg_out.at[off : off + width], precv.at[off : off + width], pair_send.at[n], pair_recv.at[n], {"dp": 1 - d})

    for c, (m, o, w) in enumerate(pieces):
        if c == 2:
            relay(3)
        arrived(c)
        for n, (off, width) in enumerate(tiles):
            if off < o or off >= o + w:
                continue
            if m == 0:
                product((1 - d) * half, off, width, give)
                pair_copy(n).start()
            else:
                pair_copy(n).wait_recv()
                pair_copy(n).wait_send()
                product(d * half, off, width, take)

    top_copy.wait()
    most[0, 0] = jnp.max(jnp.maximum(peak[...], peak_in[...]))
    for i in range(6):
        info_copy(i, s if i < 3 else e).wait_send()
    for i in range(3):
        for n in range(2):
            kv_copy(n, i, s).wait_send()
            part_copy(n, i, s).wait_send()
        gz_copy(i, across if i == 2 else e).wait_send()
    for c in range(len(pieces)):
        for i in range(3):
            raw_copy(c, i, s).wait_send()
        for n in parts:
            hz_copy(c, n).wait_send()
    if packed:

        @pl.when(inner)
        def _():
            for c in range(len(pieces)):
                for z in others:
                    relay_copy(c, z).wait_send()


def line_call(K, number, ids, gates, grad_out, queries, keys, values, hidden):
    E, S = lax.axis_size("expert"), lax.axis_size("seq")
    T, D = grad_out.shape
    U = hidden.shape[2] // S
    C = -(-(7 * T // (2 * E)) // 16) * 16
    KD = keys.shape[1]
    W, rows, half = S * C, 2 * T, U // 2
    bf, f32 = jnp.bfloat16, jnp.float32
    vm = pl.BlockSpec(memory_space=pltpu.VMEM)
    dma = pltpu.SemaphoreType.DMA
    P_ = len(line_pieces(half))
    tiles = len(line_tiles(half))
    return pl.pallas_call(
        functools.partial(line_kernel, (E, S, T, C, U, D, K)),
        out_shape=(
            pltpu.VMEM((half, D), bf),
            pltpu.VMEM((T, D), bf),
            pltpu.VMEM((T, KD), bf),
            pltpu.VMEM((T, KD), bf),
            jax.ShapeDtypeStruct((1, 1), f32),
        ),
        in_specs=[vm] * 6 + [pl.BlockSpec(memory_space=pl.ANY)],
        out_specs=(vm,) * 4 + (pl.BlockSpec(memory_space=pltpu.SMEM),),
        scratch_shapes=[
            pltpu.VMEM((E, S + 1, 8, rows), f32),
            pltpu.VMEM((8, 128), f32),
            pltpu.VMEM((8, 128), f32),
            pltpu.VMEM((S, T, KD), bf),
            pltpu.VMEM((S, T, KD), bf),
            pltpu.VMEM((S, T, 2, U), bf),
            pltpu.VMEM((2 * W + K, S * rows), bf),
            pltpu.VMEM((W + K, U), bf),
            pltpu.VMEM((E, W, U), bf),
            pltpu.VMEM((E, T, D), bf),
            pltpu.VMEM((E, S, C, D), bf),
            pltpu.VMEM((S, T, KD), bf),
            pltpu.VMEM((S, T, KD), bf),
            pltpu.VMEM((S, T, KD), f32),
            pltpu.VMEM((S, T, KD), f32),
            pltpu.VMEM((S, T, KD), bf),
            pltpu.VMEM((S, T, KD), bf),
            pltpu.VMEM((half, D), bf),
            dma((2, 3)), dma((2, 3)), dma((P_,)), dma((P_, 3)), dma((P_, 3)), dma((3,)), dma((3,)),
            dma((E, 4)), dma((E, 4)), dma((P_, 4)), dma((P_, E)), dma((P_, E)), dma((P_, E)), dma((P_, E)),
            dma((2, 3)), dma((2, 3)), dma((tiles,)), dma((tiles,)), dma((7,)), dma((7,)),
        ],
        compiler_params=pltpu.CompilerParams(
            collective_id=number, has_side_effects=True, vmem_limit_bytes=50 * 1024 * 1024
        ),
    )(ids, gates, grad_out, queries, keys, values, hidden)


def publish_kernel(*refs):
    n = (len(refs) - 1) // 2
    copies = []
    for a in range(n):
        count = 8 if a == 0 else 1
        size = refs[a].shape[0] // count
        for c in range(count):
            part = pl.ds(c * size, size)
            copies.append(
                pltpu.make_async_copy(refs[a].at[part], refs[n + a].at[part], refs[-1].at[len(copies)])
            )
    for copy in copies:
        copy.start()
    for copy in copies:
        copy.wait()


def publish(*grads):
    hbm = pl.BlockSpec(memory_space=pl.ANY)
    return pl.pallas_call(
        publish_kernel,
        out_shape=tuple(jax.ShapeDtypeStruct(g.shape, g.dtype) for g in grads),
        in_specs=[hbm] * len(grads),
        out_specs=(hbm,) * len(grads),
        scratch_shapes=[pltpu.SemaphoreType.DMA((8 + len(grads) - 1,))],
        compiler_params=pltpu.CompilerParams(vmem_limit_bytes=1024 * 1024),
    )(*grads)


def on_line(grad_out, expert_ids, gate_weights, hidden, queries, keys, values):
    E, S = lax.axis_size("expert"), lax.axis_size("seq")
    C = -(-(7 * grad_out.shape[1] // (2 * E)) // 16) * 16
    operands = (expert_ids[0].T, gate_weights[0].T, grad_out[0], queries[0], keys[0], values[0], hidden[0])
    full = 2 * S * C
    tight = full * 6 // 7 // 16 * 16
    *grads, most = line_call(tight, 0, *operands)
    grads = publish(*grads)

    def kept(grads, operands):
        return tuple(grads)

    def again(grads, operands):
        return tuple(publish(*line_call(full, 1, *operands)[:4]))

    eg, gq, gk, gv = lax.cond(most[0, 0] <= float(tight), kept, again, grads, operands)
    return (eg[None], gq[None], gk[None], gv[None])


def solution(mesh):
    split = P(("expert", "dp"), "seq", None)
    in_specs = (split, split, split, P(("expert", "dp"), "seq", None, None), split, split, split)
    out_specs = (P("expert", ("seq", "dp"), None), split, split, split)
    body = on_line if mesh.shape["expert"] == 4 and mesh.shape["seq"] == 4 else on_device
    return jax.shard_map(
        body, mesh=mesh, in_specs=in_specs, out_specs=out_specs, check_vma=False
    )
```

```python
import functools

import jax
import jax.numpy as jnp
from jax import lax
from jax.experimental import pallas as pl
from jax.experimental.pallas import tpu as pltpu
from jax.sharding import PartitionSpec as P

HEADS = 16
KV_HEADS = 4
HEAD_DIM = 128
GROUP = HEADS // KV_HEADS
MESH = pl.DeviceIdType.MESH


def dot(a, b, contract):
    return lax.dot_general(a, b, (contract, ((), ())), preferred_element_type=jnp.float32)


def routing_codes(ids, order_row, order_col, experts, capacity):
    count = max(8, experts)
    rows = ids.shape[1]
    expert_of = lax.broadcasted_iota(jnp.int32, (count, rows), 0).astype(jnp.float32)
    onehot = (expert_of == ids).astype(jnp.float32)
    earlier = (order_col < order_row).astype(jnp.float32)
    before = dot(onehot.astype(jnp.bfloat16), earlier.astype(jnp.bfloat16), ((1,), (0,)))
    slot = jnp.sum(before * onehot, axis=0, keepdims=True)
    return ids * float(capacity) + slot


def spreads(experts):
    return experts <= 8 and experts & (experts - 1) == 0


def kernel(
    dims,
    ids_t, info, go, q, k, v, hid,
    eg_out, gq_out, gk_out, gv_out,
    kbuf, vbuf, idbuf, hraw, hsend, hrecv, gsend, grecv, infos,
    kpart, vpart, kown, vown, kin, vin, precv,
    small_send, small_recv, local_sem, hraw_send, hraw_recv,
    gz_send, gz_recv, gi_send, gi_recv, gs_send, gs_recv, hz_send, hz_recv,
    part_send, part_recv, pair_send, pair_recv,
):
    E, S, T, C, U, D = dims
    half = U // 2
    first = -(-half // 256) * 128
    pieces = [(n, o, w) for n in range(2) for o, w in ((0, first), (first, half - first)) if w > 0]
    spread = spreads(E)
    e = lax.axis_index("expert")
    s = lax.axis_index("seq")
    d = lax.axis_index("dp")
    seq_peer = [lax.rem(s + i, S) for i in range(S)]
    bases = [
        pl.multiple_of((d if n else 1 - d) * half + o, 128) for n, o, _ in pieces
    ]

    def ex_peer(j):
        return lax.rem(e + j, E)

    barrier = pltpu.get_barrier_semaphore()
    for i in range(1, S):
        pl.semaphore_signal(barrier, inc=1, device_id={"seq": seq_peer[i]}, device_id_type=MESH)

    @pl.loop(1, E)
    def _(j):
        pl.semaphore_signal(barrier, inc=1, device_id={"expert": ex_peer(j)}, device_id_type=MESH)

    pl.semaphore_signal(barrier, inc=1, device_id={"dp": 1 - d}, device_id_type=MESH)
    pl.semaphore_wait(barrier, S + E - 1)

    def send(src, dst, ssem, rsem, where):
        return pltpu.make_async_remote_copy(
            src_ref=src, dst_ref=dst, send_sem=ssem, recv_sem=rsem,
            device_id=where, device_id_type=MESH,
        )

    def small_copy(n, i, slot):
        src, dst = ((ids_t, idbuf), (k, kbuf), (v, vbuf))[n]
        return send(src, dst.at[slot], small_send.at[n, i], small_recv.at[n, slot], {"seq": seq_peer[i]})

    def raw_copy(c, i, slot):
        width = pieces[c][2]
        cols = pl.ds(pl.multiple_of(seq_peer[i] * U + bases[c], 128), width)
        return send(
            hid.at[:, :, cols], hraw.at[slot, :, :, pl.ds(bases[c], width)],
            hraw_send.at[c, i], hraw_recv.at[c, slot], {"seq": seq_peer[i]},
        )

    own_cols = pl.ds(pl.multiple_of(s * U, 128), U)
    own_raw = pltpu.make_async_copy(hid.at[:, :, own_cols], hraw.at[s], local_sem.at[0])
    own_raw.start()
    for i in range(1, S):
        for n in range(3):
            small_copy(n, i, s).start()
    for c in range(len(pieces)):
        for i in range(1, S):
            raw_copy(c, i, s).start()
    kbuf[s] = k[...]
    vbuf[s] = v[...]
    idbuf[s] = ids_t[...]

    rows = 2 * T
    col = lax.broadcasted_iota(jnp.int32, (rows, rows), 1)
    row = lax.broadcasted_iota(jnp.int32, (rows, rows), 0)
    place = lax.broadcasted_iota(jnp.int32, (E * C, rows), 0).astype(jnp.float32)

    def expert_rows(p):
        return pl.ds(pl.multiple_of(p * C, 16), C)

    def gs_copy(i, z, slot):
        return send(grecv.at[s, z], grecv.at[slot, z], gs_send.at[i, z], gs_recv.at[slot, z], {"seq": seq_peer[i]})

    def gs_wait(i, z):
        slot = seq_peer[i]
        send(grecv.at[s, z], grecv.at[slot, z], gs_send.at[i, z], gs_recv.at[slot, z], {"seq": slot}).wait_recv()

    def packed_grads(ids, gates, grads, wanted):
        code = routing_codes(
            ids, 2 * lax.rem(col, T) + col // T, 2 * lax.rem(row, T) + row // T, E, C
        )
        picks = (wanted == code).astype(jnp.float32)
        gate = jnp.sum(picks * gates, axis=1, keepdims=True)
        token_picks = (picks[:, :T] + picks[:, T:]).astype(jnp.bfloat16)
        return (dot(token_picks, grads, ((1,), (0,))) * gate).astype(jnp.bfloat16)

    if spread:
        def flip(at, b):
            return at + b - 2 * b * lax.rem(at // b, 2)

        bits = []
        b = E // 2
        while b >= 1:
            bits.append(b)
            b //= 2

        def masks(n):
            held = [0]
            for bit in bits[:n]:
                held = held + [m + bit for m in held]
            return held

        def at_mask(m):
            at = e
            for bit in bits:
                if m & bit:
                    at = flip(at, bit)
            return at

        def gz_pair(m, n, slot):
            to = {"expert": flip(e, bits[n])}
            key = m + bits[n]
            return (
                send(gsend.at[slot], gsend.at[slot], gz_send.at[key], gz_recv.at[slot], to),
                send(infos.at[slot], infos.at[slot], gi_send.at[key], gi_recv.at[slot], to),
            )

        def forward(m):
            z = at_mask(m)
            wanted = (
                lax.broadcasted_iota(jnp.int32, (C, rows), 0) + e * C
            ).astype(jnp.float32)
            grecv[s, z] = packed_grads(infos[z, 0:1, :], infos[z, 8:9, :], gsend[z], wanted)
            for i in range(1, S):
                gs_copy(i, z, s).start()

        def arrive(m, n):
            for copy in gz_pair(m, n, at_mask(m + bits[n])):
                copy.wait_recv()
            for later in range(n + 1, len(bits)):
                for copy in gz_pair(m + bits[n], later, at_mask(m + bits[n])):
                    copy.start()

        gsend[e] = go[...]
        infos[e] = info[...]
        for n in range(len(bits)):
            for copy in gz_pair(0, n, e):
                copy.start()
    else:

        def gz_copy(j, slot):
            p = ex_peer(j)
            return send(gsend.at[expert_rows(p)], grecv.at[s, slot], gz_send.at[j], gz_recv.at[slot], {"expert": p})

        gsend[...] = packed_grads(info[0:1, :], info[8:9, :], go[...], place)

        @pl.loop(1, E)
        def _(j):
            gz_copy(j, e).start()

        grecv[s, e] = gsend[expert_rows(e)]
        for i in range(1, S):
            gs_copy(i, e, s).start()

    def hz_copy(c, i, j, slot):
        p = ex_peer(j)
        src = seq_peer[i]
        units = pl.ds(bases[c], pieces[c][2])
        return send(
            hsend.at[src, expert_rows(p), units], hrecv.at[src, slot, :, units],
            hz_send.at[c, src, j], hz_recv.at[c, src, slot], {"expert": p},
        )

    def pack_hidden(c, i):
        src = seq_peer[i]
        width = pieces[c][2]
        units = pl.ds(bases[c], width)
        hcode = routing_codes(idbuf[src, 0:1, :], col, row, E, C)
        hpicks = (place == hcode).astype(jnp.bfloat16)
        hsend[src, :, units] = dot(
            hpicks, hraw[src, :, :, units].reshape(rows, width), ((1,), (0,))
        ).astype(jnp.bfloat16)

        @pl.loop(1, E)
        def _(j):
            hz_copy(c, i, j, e).start()

        hrecv[src, e, :, units] = hsend[src, expert_rows(e), units]

    own_raw.wait()
    for c in range(len(pieces)):
        pack_hidden(c, 0)
    if spread:
        forward(0)

    scale = HEAD_DIM ** (-0.5)
    length = S * T

    def attention(j):
        lanes = slice(j * HEAD_DIM, (j + 1) * HEAD_DIM)
        heads = [slice(h * HEAD_DIM, (h + 1) * HEAD_DIM) for h in range(j * GROUP, (j + 1) * GROUP)]
        qs = jnp.concatenate([q[:, h] for h in heads], axis=0)
        gs = jnp.concatenate([go[:, h] for h in heads], axis=0)
        kj = kbuf[:, :, lanes].reshape(length, HEAD_DIM)
        vj = vbuf[:, :, lanes].reshape(length, HEAD_DIM)
        scores = dot(qs, kj, ((1,), (1,))) * scale
        raised = jnp.exp(scores - jnp.max(scores, axis=-1, keepdims=True))
        probs = raised / jnp.sum(raised, axis=-1, keepdims=True)
        dprobs = dot(gs, vj, ((1,), (1,)))
        delta = jnp.sum(probs * dprobs, axis=-1, keepdims=True)
        ds = (probs * (dprobs - delta)).astype(jnp.bfloat16)
        dv = dot(probs.astype(jnp.bfloat16), gs, ((0,), (0,)))
        dk = dot(ds, qs, ((0,), (0,))) * scale
        dq = dot(ds, kj, ((1,), (0,))) * scale
        for n, h in enumerate(heads):
            gq_out[:, h] = dq[n * T : (n + 1) * T].astype(jnp.bfloat16)
        dk = dk.reshape(S, T, HEAD_DIM)
        dv = dv.reshape(S, T, HEAD_DIM)
        kown[:, :, lanes] = dk
        vown[:, :, lanes] = dv
        kpart[:, :, lanes] = dk.astype(jnp.bfloat16)
        vpart[:, :, lanes] = dv.astype(jnp.bfloat16)

    for i in range(1, S):
        for n in range(3):
            small_copy(n, i, seq_peer[i]).wait_recv()

    attention(0)

    if spread:
        attention(1)
        for n in range(len(bits)):
            for m in masks(n):
                arrive(m, n)
                forward(m + bits[n])
    else:

        @pl.loop(1, E)
        def _(j):
            z = ex_peer(j)
            gz_copy(j, z).wait_recv()
            for i in range(1, S):
                gs_copy(i, z, s).start()

        attention(1)
    for c in range(len(pieces)):
        for i in range(1, S):
            raw_copy(c, i, seq_peer[i]).wait_recv()
            pack_hidden(c, i)
        if c + 2 < KV_HEADS:
            attention(c + 2)
    for j in range(len(pieces) + 2, KV_HEADS):
        attention(j)

    def part_copy(n, i, slot):
        src, dst = ((kpart, kin), (vpart, vin))[n]
        return send(src.at[seq_peer[i]], dst.at[slot], part_send.at[n, i], part_recv.at[n, slot], {"seq": seq_peer[i]})

    for i in range(1, S):
        for n in range(2):
            part_copy(n, i, s).start()
    for n, (own, got, out) in enumerate(((kown, kin, gk_out), (vown, vin, gv_out))):
        total = own[s]
        for i in range(1, S):
            part_copy(n, i, seq_peer[i]).wait_recv()
            total = total + got[seq_peer[i]].astype(jnp.float32)
        out[...] = total.astype(jnp.bfloat16)

    @pl.loop(0, E)
    def _(z):
        for i in range(1, S):
            gs_wait(i, z)

    wide = 256
    tiles = [
        (o + t, min(wide, w - t)) for n, o, w in pieces if n == 0 for t in range(0, w, wide)
    ]

    def arrived(n, off):
        for c, (m, o, _) in enumerate(pieces):
            if m == n and o == off:

                @pl.loop(1, E)
                def _(j):
                    for i in range(S):
                        hz_copy(c, i, j, ex_peer(j)).wait_recv()

    def product(base, off, width):
        units = pl.ds(pl.multiple_of(base + off, 128), width)
        h = hrecv[:, :, :, units].reshape(S * E * C, width)
        return dot(h, grecv[...].reshape(S * E * C, D), ((0,), (0,)))

    def pair_copy(n):
        off, width = tiles[n]
        return send(eg_out.at[off : off + width], precv.at[off : off + width], pair_send.at[n], pair_recv.at[n], {"dp": 1 - d})

    for n, (off, width) in enumerate(tiles):
        arrived(0, off)
        eg_out[off : off + width, :] = product((1 - d) * half, off, width).astype(jnp.bfloat16)
        pair_copy(n).start()
    for n, (off, width) in enumerate(tiles):
        arrived(1, off)
        mine = product(d * half, off, width)
        pair_copy(n).wait_recv()
        pair_copy(n).wait_send()
        got = precv[off : off + width, :].astype(jnp.float32)
        eg_out[off : off + width, :] = (mine + got).astype(jnp.bfloat16)

    for i in range(1, S):
        for n in range(3):
            small_copy(n, i, s).wait_send()
        for n in range(2):
            part_copy(n, i, s).wait_send()
        for c in range(len(pieces)):
            raw_copy(c, i, s).wait_send()

    @pl.loop(0, E)
    def _(z):
        for i in range(1, S):
            gs_copy(i, z, s).wait_send()

    @pl.loop(1, E)
    def _(j):
        if not spread:
            gz_copy(j, e).wait_send()
        for i in range(S):
            for c in range(len(pieces)):
                hz_copy(c, i, j, e).wait_send()

    if spread:
        for n in range(len(bits)):
            for m in masks(n):
                for copy in gz_pair(m, n, at_mask(m)):
                    copy.wait_send()


def on_device(grad_out, expert_ids, gate_weights, hidden, queries, keys, values):
    E = lax.axis_size("expert")
    S = lax.axis_size("seq")
    T = grad_out.shape[1]
    D = grad_out.shape[2]
    U = hidden.shape[3] // S
    C = -(-(7 * T // (2 * E)) // 16) * 16
    KD = keys.shape[2]
    rows = 2 * T
    bf, f32 = jnp.bfloat16, jnp.float32
    ids = expert_ids[0].astype(f32)
    ids_t = jnp.broadcast_to(ids.reshape(1, rows), (8, rows))
    ids_k = jnp.broadcast_to(ids.T.reshape(1, rows), (8, rows))
    gates_k = jnp.broadcast_to(gate_weights[0].T.reshape(1, rows), (8, rows))
    tiles = -(-(U // 2) // 256)
    info = jnp.concatenate([ids_k, gates_k], axis=0)
    sent = (E, T, D) if spreads(E) else (E * C, D)
    vm = pl.BlockSpec(memory_space=pltpu.VMEM)
    dma = pltpu.SemaphoreType.DMA
    eg, gq, gk, gv = pl.pallas_call(
        functools.partial(kernel, (E, S, T, C, U, D)),
        out_shape=(
            jax.ShapeDtypeStruct((U // 2, D), bf),
            jax.ShapeDtypeStruct((T, queries.shape[2]), bf),
            jax.ShapeDtypeStruct((T, KD), bf),
            jax.ShapeDtypeStruct((T, KD), bf),
        ),
        in_specs=[vm] * 6 + [pl.BlockSpec(memory_space=pl.ANY)],
        out_specs=(vm,) * 4,
        scratch_shapes=[
            pltpu.VMEM((S, T, KD), bf),
            pltpu.VMEM((S, T, KD), bf),
            pltpu.VMEM((S, 8, rows), f32),
            pltpu.VMEM((S, T, 2, U), bf),
            pltpu.VMEM((S, E * C, U), bf),
            pltpu.VMEM((S, E, C, U), bf),
            pltpu.VMEM(sent, bf),
            pltpu.VMEM((S, E, C, D), bf),
            pltpu.VMEM((E if spreads(E) else 1, 16, rows), f32),
            pltpu.VMEM((S, T, KD), bf),
            pltpu.VMEM((S, T, KD), bf),
            pltpu.VMEM((S, T, KD), f32),
            pltpu.VMEM((S, T, KD), f32),
            pltpu.VMEM((S, T, KD), bf),
            pltpu.VMEM((S, T, KD), bf),
            pltpu.VMEM((U // 2, D), bf),
            dma((3, S)), dma((3, S)), dma((1,)), dma((4, S)), dma((4, S)),
            dma((E,)), dma((E,)), dma((E,)), dma((E,)), dma((S, E)), dma((S, E)), dma((4, S, E)), dma((4, S, E)),
            dma((2, S)), dma((2, S)), dma((tiles,)), dma((tiles,)),
        ],
        compiler_params=pltpu.CompilerParams(
            collective_id=0, has_side_effects=True, vmem_limit_bytes=62 * 1024 * 1024
        ),
    )(ids_t, info, grad_out[0], queries[0], keys[0], values[0], hidden[0])
    return (eg[None], gq[None], gk[None], gv[None])


def flip(at, b):
    return at + b - 2 * b * lax.rem(at // b, 2)


def greet(peers):
    barrier = pltpu.get_barrier_semaphore()
    for peer in peers:
        pl.semaphore_signal(barrier, inc=1, device_id=peer, device_id_type=MESH)
    pl.semaphore_wait(barrier, len(peers))


def send(src, dst, ssem, rsem, where):
    return pltpu.make_async_remote_copy(
        src_ref=src, dst_ref=dst, send_sem=ssem, recv_sem=rsem,
        device_id=where, device_id_type=MESH,
    )


def line_pieces(half):
    cut = min(384, half)
    return [(0, 0, cut), (0, cut, half - cut), (1, 0, half - 256), (1, half - 256, 256)]


def line_tiles(half):
    edges = sorted({0, half} | {p[1] for p in line_pieces(half)})
    return [
        (lo + t, min(256, hi - lo - t)) for lo, hi in zip(edges, edges[1:]) for t in range(0, hi - lo, 256)
    ]


def line_kernel(
    dims,
    ids_in, gates_in, go, q, k, v, hid,
    eg_out, gq_out, gk_out, gv_out, most,
    info, peak, peak_in,
    kbuf, vbuf, hraw, picks, hsend, hrecv, gsend, grecv,
    kpart, vpart, kown, vown, kin, vin, precv,
    kv_send, kv_recv, local_sem, raw_send, raw_recv, gz_send, gz_recv, gs_send, gs_recv,
    hz_send, hz_recv, shared_recv, relay_send, relay_recv, part_send, part_recv, pair_send, pair_recv,
    info_send, info_recv,
):
    E, S, T, C, U, D, K = dims
    W = S * C
    half = U // 2
    rows = 2 * T
    packed = K < 2 * W
    parts = range(0 if packed else 1, 4)
    both = 2 * W - K
    pieces = line_pieces(half)
    tiles = line_tiles(half)
    e, s, d = (lax.axis_index(n) for n in ("expert", "seq", "dp"))
    side = e // 2
    friend, across, corner = flip(e, 1), flip(e, 2), flip(flip(e, 1), 2)
    near, far = 2 - side, 3 - 3 * side
    inner = jnp.logical_or(e == 1, e == 2)
    outer = jnp.logical_not(inner)
    others = [2 - 2 * side, 3 - 2 * side]
    peers = [flip(s, 1), flip(s, 2), flip(flip(s, 1), 2)]
    bases = [pl.multiple_of((d if n else 1 - d) * half + o, 128) for n, o, _ in pieces]
    greet([{"seq": p} for p in peers] + [{"expert": p} for p in (friend, across, corner)] + [{"dp": 1 - d}])

    def cols(c):
        return pl.ds(bases[c], pieces[c][2])

    def kv_copy(n, i, slot):
        src, dst = ((k, kbuf), (v, vbuf))[n]
        return send(src, dst.at[slot], kv_send.at[n, i], kv_recv.at[n, i], {"seq": peers[i]})

    def raw_copy(c, i, slot):
        there = pl.ds(pl.multiple_of(peers[i] * U + bases[c], 128), pieces[c][2])
        return send(
            hid.at[:, :, there], hraw.at[slot, :, :, cols(c)],
            raw_send.at[c, i], raw_recv.at[c, i], {"seq": peers[i]},
        )

    def own_copy(c):
        here = pl.ds(pl.multiple_of(s * U + bases[c], 128), pieces[c][2])
        return pltpu.make_async_copy(hid.at[:, :, here], hraw.at[s, :, :, cols(c)], local_sem.at[c])

    def gz_copy(n, slot):
        src = go if n < 2 else gsend.at[across]
        dst = gsend.at[slot]
        to = across if n == 0 else friend
        return send(src, dst, gz_send.at[n], gz_recv.at[n], {"expert": to})

    z_peers = [friend, across, corner]

    def line(ref):
        flat = jnp.concatenate([ref[0:1, :], ref[1:2, :]], axis=1).astype(jnp.float32)
        return jnp.broadcast_to(flat, (1, 8, rows))

    def info_copy(i, slot):
        if i < 3:
            return send(info.at[e, s], info.at[e, slot], info_send.at[i], info_recv.at[i], {"seq": peers[i]})
        return send(info.at[e], info.at[slot], info_send.at[i], info_recv.at[i], {"expert": z_peers[i - 3]})

    info[e, pl.ds(s, 1)] = line(ids_in)
    info[e, S : S + 1] = line(gates_in)
    for i in range(3):
        info_copy(i, s).start()
    gz_copy(0, e).start()
    gz_copy(1, e).start()
    for c in range(len(pieces)):
        own_copy(c).start()
        for i in range(3):
            raw_copy(c, i, s).start()
    for i in range(3):
        for n in range(2):
            kv_copy(n, i, s).start()
    kbuf[s] = k[...]
    vbuf[s] = v[...]

    col = lax.broadcasted_iota(jnp.int32, (rows, rows), 1)
    row = lax.broadcasted_iota(jnp.int32, (rows, rows), 0)
    f32, bf = jnp.float32, jnp.bfloat16
    experts = lax.broadcasted_iota(jnp.int32, (8, rows), 0).astype(f32)
    by_place = (col < row).astype(bf)
    interleave = (row == lax.rem(col, 2) * T + col // 2).astype(bf)
    in_order = (row < col).astype(bf)
    k_order = (2 * lax.rem(row, T) + row // T < 2 * lax.rem(col, T) + col // T).astype(bf)

    def ranked(ids, earlier):
        onehot = (experts == ids).astype(f32)
        return onehot, dot(onehot.astype(bf), earlier, ((1,), (0,)))

    for i in range(3):
        info_copy(i, peers[i]).wait_recv()
    for i in range(3):
        info_copy(3 + i, e).start()
    total = 2 * W + K
    offsets = jnp.zeros((8, 1), f32)
    places = lax.broadcasted_iota(jnp.int32, (128, rows), 0).astype(f32)

    def mark(b, start):
        ids = dot(info[e, b].astype(bf), interleave, ((1,), (0,)))[0:1, :]
        onehot, before = ranked(ids, in_order)
        rank = jnp.sum(onehot * (before + start), axis=0, keepdims=True)
        back = (W + K - 1) - rank if packed else K + rank
        code = jnp.where(
            ids == friend.astype(f32), rank,
            jnp.where(
                ids == e.astype(f32), W + K + rank,
                jnp.where(ids == near.astype(f32), W + rank, back),
            ),
        )

        @pl.loop(0, total // 128)
        def _(r):
            at = places + (128 * r).astype(f32)
            picks[pl.ds(pl.multiple_of(128 * r, 128), 128), b * rows : (b + 1) * rows] = (at == code).astype(bf)

        return start + jnp.sum(onehot, axis=1, keepdims=True)

    for b in range(S):
        offsets = mark(b, offsets if packed else float(C * b))

    def gs_copy(z, n):
        to = peers[0] if n in (0, 3) else peers[1]
        slot = (s, s, peers[0], peers[1])[n]
        lanes = (slice(0, D), slice(0, D), slice(0, D // 2), slice(D // 2, D))[n]
        block = grecv.at[z, slot, :, lanes]
        return send(block, block, gs_send.at[z, n], gs_recv.at[z, n], {"seq": to})

    def gs_wait(z, n):
        slot = (peers[0], peers[1], peers[2], peers[2])[n]
        lanes = (slice(0, D), slice(0, D), slice(0, D // 2), slice(D // 2, D))[n]
        block = grecv.at[z, slot, :, lanes]
        send(block, block, gs_send.at[z, n], gs_recv.at[z, n], {"seq": peers[0]}).wait_recv()

    wanted = lax.broadcasted_iota(jnp.int32, (C, rows), 0).astype(f32)

    def forward(z, grads):
        ids = info[z, pl.ds(s, 1)][0, 0:1, :]
        onehot, before = ranked(ids, k_order)
        rank = jnp.sum(before * onehot, axis=0, keepdims=True)
        code = jnp.where(ids == e.astype(f32), rank, -1.0)
        chosen = (wanted == code).astype(f32)
        gate = jnp.sum(chosen * info[z, 4, 0:1, :], axis=1, keepdims=True)
        token = (chosen[:, :T] + chosen[:, T:]).astype(bf)
        grecv[z, pl.ds(s, 1)] = (dot(token, grads, ((1,), (0,))) * gate).astype(bf)[None]
        for n in range(2):
            gs_copy(z, n).start()

    def pass_on(z):
        for n in range(2):
            gs_wait(z, n)
            gs_copy(z, 2 + n).start()

    def hz_copy(c, n):
        units = cols(c)
        to = (near, far, near, friend)[n]
        first, low, high = ((K, K - W, W), (2 * W, both, W), (W, 0, K - W), (0, 0, W))[n]
        src = hsend.at[first : first + high - low, units]
        landed = shared_recv if n == 0 else hz_recv
        return send(src, hrecv.at[e, low:high, units], hz_send.at[c, n], landed.at[c, e], {"expert": to})

    def hz_wait(c, z, low, high, landed):
        block = hrecv.at[z, low:high, cols(c)]
        send(block, block, hz_send.at[c, 0], landed.at[c, z], {"expert": friend}).wait_recv()

    def relay_copy(c, z):
        return send(
            hrecv.at[z, K - W : W, cols(c)], hrecv.at[z, 0:both, cols(c)],
            relay_send.at[c, z], relay_recv.at[c, z], {"expert": friend},
        )

    def pack(c):
        own_copy(c).wait()
        for i in range(3):
            raw_copy(c, i, peers[i]).wait_recv()
        width = pieces[c][2]
        sent = (W + K) // 4

        def gather(t, size):
            units = pl.ds(pl.multiple_of(bases[c] + t, 128), size)
            block = hraw[:, :, :, units].reshape(S * rows, size)

            @pl.loop(0, 4)
            def _(r):
                some = pl.ds(pl.multiple_of(r * sent, 16), sent)
                hsend[some, units] = dot(picks[some, :], block, ((1,), (0,))).astype(bf)

            hrecv[pl.ds(e, 1), :, units] = dot(picks[W + K :, :], block, ((1,), (0,))).astype(bf)[None]

        if width >= 256:

            @pl.loop(0, width // 256)
            def _(t):
                gather(t * 256, 256)

        if width % 256:
            gather(width - 128, 128)
        for n in parts:
            hz_copy(c, n).start()

    def relay(c):
        if packed:

            @pl.when(inner)
            def _():
                for z in others:
                    hz_wait(c, z, K - W, W, shared_recv)
                    relay_copy(c, z).start()

    def arrived(c):
        hz_wait(c, friend, 0, W, hz_recv)

        @pl.when(inner)
        def _():
            for z in others:
                hz_wait(c, z, 0, K - W, hz_recv)

        @pl.when(outer)
        def _():
            for z in others:
                hz_wait(c, z, both, W, hz_recv)
                if packed:
                    relay_copy(c, z).wait_recv()

    scale = HEAD_DIM ** (-0.5)
    length = S * T

    def attention(j):
        def lanes_of(h):
            return pl.ds(pl.multiple_of(h * HEAD_DIM, HEAD_DIM), HEAD_DIM)

        lanes = lanes_of(j)
        heads = [lanes_of(j * GROUP + n) for n in range(GROUP)]
        qs = jnp.concatenate([q[:, h] for h in heads], axis=0)
        gs = jnp.concatenate([go[:, h] for h in heads], axis=0)
        kj = kbuf[:, :, lanes].reshape(length, HEAD_DIM)
        vj = vbuf[:, :, lanes].reshape(length, HEAD_DIM)
        scores = dot(qs, kj, ((1,), (1,))) * scale
        raised = jnp.exp(scores - jnp.max(scores, axis=-1, keepdims=True))
        probs = raised / jnp.sum(raised, axis=-1, keepdims=True)
        dprobs = dot(gs, vj, ((1,), (1,)))
        delta = jnp.sum(probs * dprobs, axis=-1, keepdims=True)
        ds = (probs * (dprobs - delta)).astype(jnp.bfloat16)
        dv = dot(probs.astype(jnp.bfloat16), gs, ((0,), (0,)))
        dk = dot(ds, qs, ((0,), (0,))) * scale
        dq = dot(ds, kj, ((1,), (0,))) * scale
        for n, h in enumerate(heads):
            gq_out[:, h] = dq[n * T : (n + 1) * T].astype(jnp.bfloat16)
        dk = dk.reshape(S, T, HEAD_DIM)
        dv = dv.reshape(S, T, HEAD_DIM)
        kown[:, :, lanes] = dk
        vown[:, :, lanes] = dv
        kpart[:, :, lanes] = dk.astype(jnp.bfloat16)
        vpart[:, :, lanes] = dv.astype(jnp.bfloat16)

    pack(0)
    forward(e, go[...])
    pack(1)
    for i in range(3):
        info_copy(3 + i, z_peers[i]).wait_recv()
    gz_copy(0, across).wait_recv()
    gz_copy(2, across).start()
    forward(across, gsend[across])
    pack(2)
    gz_copy(1, friend).wait_recv()
    forward(friend, gsend[friend])
    pack(3)
    relay(0)
    for i in range(3):
        for n in range(2):
            kv_copy(n, i, peers[i]).wait_recv()
    pl.loop(0, KV_HEADS)(attention)
    relay(1)
    pass_on(e)
    gz_copy(2, corner).wait_recv()
    forward(corner, gsend[corner])
    pass_on(across)
    pass_on(friend)

    top = jnp.zeros((1, 1), f32)
    for z in range(E):
        crossing = jnp.zeros((1, rows), f32)
        for b in range(S):
            high = (info[z, b, 0:1, :] >= float(E // 2)).astype(f32)
            crossing = crossing + (high if z < E // 2 else 1.0 - high)
        top = jnp.maximum(top, jnp.sum(crossing, axis=1, keepdims=True))
    peak[...] = jnp.broadcast_to(top, (8, 128))
    top_copy = send(peak, peak_in, info_send.at[6], info_recv.at[6], {"dp": 1 - d})
    top_copy.start()

    def part_copy(n, i, slot):
        src, dst = ((kpart, kin), (vpart, vin))[n]
        return send(src.at[peers[i]], dst.at[slot], part_send.at[n, i], part_recv.at[n, i], {"seq": peers[i]})

    for i in range(3):
        for n in range(2):
            part_copy(n, i, s).start()
    relay(2)
    pass_on(corner)
    for n, (own, got, out) in enumerate(((kown, kin, gk_out), (vown, vin, gv_out))):
        summed = own[s]
        for i in range(3):
            part_copy(n, i, peers[i]).wait_recv()
            summed = summed + got[peers[i]].astype(jnp.float32)
        out[...] = summed.astype(jnp.bfloat16)

    def settle(z):
        for n in (2, 3):
            gs_wait(z, n)
        for n in range(4):
            gs_copy(z, n).wait_send()
        if not packed:
            return
        slots = lax.broadcasted_iota(jnp.int32, (1, W), 1).astype(f32)
        code = jnp.full((1, W), -1.0, f32)
        start = jnp.zeros((1, 1), f32)
        for b in range(S):
            named = (info[z, b, 0:1, :] == e.astype(f32)).astype(f32)
            count = jnp.sum(named, axis=1, keepdims=True)
            inside = jnp.logical_and(slots >= float(C * b), slots - float(C * b) < count)
            inside = jnp.logical_and(inside, slots < float(C * (b + 1)))
            code = jnp.where(inside, slots - float(C * b) + start, code)
            start = start + count
        turned = jnp.logical_and(z // 2 != side, outer).astype(f32)
        code = jnp.where(code >= 0.0, code + turned * (float(W - 1) - 2.0 * code), code)
        moves = (lax.broadcasted_iota(jnp.int32, (W, W), 0).astype(f32) == code).astype(bf)

        @pl.loop(0, D // 512)
        def _(t):
            lanes = pl.ds(pl.multiple_of(t * 512, 512), 512)
            block = grecv[z, :, :, lanes].reshape(W, 512)
            grecv[z, :, :, lanes] = dot(moves, block, ((1,), (0,))).astype(bf).reshape(S, C, 512)

    pl.loop(0, E)(settle)

    def product(base, off, width, use):
        units = pl.ds(pl.multiple_of(base + off, 128), width)
        here = pl.ds(off, width)

        @pl.loop(0, D // 1024)
        def _(t):
            lanes = pl.ds(pl.multiple_of(t * 1024, 1024), 1024)
            h = hrecv[:, :, units].reshape(E * W, width)
            use(here, lanes, dot(h, grecv[:, :, :, lanes].reshape(E * W, 1024), ((0,), (0,))))

    def give(here, lanes, value):
        eg_out[here, lanes] = value.astype(jnp.bfloat16)

    def take(here, lanes, value):
        eg_out[here, lanes] = (value + precv[here, lanes].astype(jnp.float32)).astype(jnp.bfloat16)

    def pair_copy(n):
        off, width = tiles[n]
        return send(eg_out.at[off : off + width], precv.at[off : off + width], pair_send.at[n], pair_recv.at[n], {"dp": 1 - d})

    for c, (m, o, w) in enumerate(pieces):
        if c == 1:
            relay(3)
        arrived(c)
        for n, (off, width) in enumerate(tiles):
            if off < o or off >= o + w:
                continue
            if m == 0:
                product((1 - d) * half, off, width, give)
                pair_copy(n).start()
            else:
                pair_copy(n).wait_recv()
                pair_copy(n).wait_send()
                product(d * half, off, width, take)

    top_copy.wait()
    most[0, 0] = jnp.max(jnp.maximum(peak[...], peak_in[...]))
    for i in range(6):
        info_copy(i, s if i < 3 else e).wait_send()
    for i in range(3):
        for n in range(2):
            kv_copy(n, i, s).wait_send()
            part_copy(n, i, s).wait_send()
        gz_copy(i, across if i == 2 else e).wait_send()
    for c in range(len(pieces)):
        for i in range(3):
            raw_copy(c, i, s).wait_send()
        for n in parts:
            hz_copy(c, n).wait_send()
    if packed:

        @pl.when(inner)
        def _():
            for c in range(len(pieces)):
                for z in others:
                    relay_copy(c, z).wait_send()


def line_call(K, number, ids, gates, grad_out, queries, keys, values, hidden):
    E, S = lax.axis_size("expert"), lax.axis_size("seq")
    T, D = grad_out.shape
    U = hidden.shape[2] // S
    C = -(-(7 * T // (2 * E)) // 16) * 16
    KD = keys.shape[1]
    W, rows, half = S * C, 2 * T, U // 2
    bf, f32 = jnp.bfloat16, jnp.float32
    vm = pl.BlockSpec(memory_space=pltpu.VMEM)
    dma = pltpu.SemaphoreType.DMA
    P_ = len(line_pieces(half))
    tiles = len(line_tiles(half))
    return pl.pallas_call(
        functools.partial(line_kernel, (E, S, T, C, U, D, K)),
        out_shape=(
            pltpu.VMEM((half, D), bf),
            pltpu.VMEM((T, D), bf),
            pltpu.VMEM((T, KD), bf),
            pltpu.VMEM((T, KD), bf),
            jax.ShapeDtypeStruct((1, 1), f32),
        ),
        in_specs=[vm] * 6 + [pl.BlockSpec(memory_space=pl.ANY)],
        out_specs=(vm,) * 4 + (pl.BlockSpec(memory_space=pltpu.SMEM),),
        scratch_shapes=[
            pltpu.VMEM((E, S + 1, 8, rows), f32),
            pltpu.VMEM((8, 128), f32),
            pltpu.VMEM((8, 128), f32),
            pltpu.VMEM((S, T, KD), bf),
            pltpu.VMEM((S, T, KD), bf),
            pltpu.VMEM((S, T, 2, U), bf),
            pltpu.VMEM((2 * W + K, S * rows), bf),
            pltpu.VMEM((W + K, U), bf),
            pltpu.VMEM((E, W, U), bf),
            pltpu.VMEM((E, T, D), bf),
            pltpu.VMEM((E, S, C, D), bf),
            pltpu.VMEM((S, T, KD), bf),
            pltpu.VMEM((S, T, KD), bf),
            pltpu.VMEM((S, T, KD), f32),
            pltpu.VMEM((S, T, KD), f32),
            pltpu.VMEM((S, T, KD), bf),
            pltpu.VMEM((S, T, KD), bf),
            pltpu.VMEM((half, D), bf),
            dma((2, 3)), dma((2, 3)), dma((P_,)), dma((P_, 3)), dma((P_, 3)), dma((3,)), dma((3,)),
            dma((E, 4)), dma((E, 4)), dma((P_, 4)), dma((P_, E)), dma((P_, E)), dma((P_, E)), dma((P_, E)),
            dma((2, 3)), dma((2, 3)), dma((tiles,)), dma((tiles,)), dma((7,)), dma((7,)),
        ],
        compiler_params=pltpu.CompilerParams(
            collective_id=number, has_side_effects=True, vmem_limit_bytes=50 * 1024 * 1024
        ),
    )(ids, gates, grad_out, queries, keys, values, hidden)


def publish_kernel(*refs):
    n = (len(refs) - 1) // 2
    copies = []
    for a in range(n):
        count = 8 if a == 0 else 1
        size = refs[a].shape[0] // count
        for c in range(count):
            part = pl.ds(c * size, size)
            copies.append(
                pltpu.make_async_copy(refs[a].at[part], refs[n + a].at[part], refs[-1].at[len(copies)])
            )
    for copy in copies:
        copy.start()
    for copy in copies:
        copy.wait()


def publish(*grads):
    hbm = pl.BlockSpec(memory_space=pl.ANY)
    return pl.pallas_call(
        publish_kernel,
        out_shape=tuple(jax.ShapeDtypeStruct(g.shape, g.dtype) for g in grads),
        in_specs=[hbm] * len(grads),
        out_specs=(hbm,) * len(grads),
        scratch_shapes=[pltpu.SemaphoreType.DMA((8 + len(grads) - 1,))],
        compiler_params=pltpu.CompilerParams(vmem_limit_bytes=1024 * 1024),
    )(*grads)


def on_line(grad_out, expert_ids, gate_weights, hidden, queries, keys, values):
    E, S = lax.axis_size("expert"), lax.axis_size("seq")
    C = -(-(7 * grad_out.shape[1] // (2 * E)) // 16) * 16
    operands = (expert_ids[0].T, gate_weights[0].T, grad_out[0], queries[0], keys[0], values[0], hidden[0])
    full = 2 * S * C
    tight = full * 6 // 7 // 16 * 16
    *grads, most = line_call(tight, 0, *operands)
    grads = publish(*grads)

    def kept(grads, operands):
        return tuple(grads)

    def again(grads, operands):
        return tuple(publish(*line_call(full, 1, *operands)[:4]))

    eg, gq, gk, gv = lax.cond(most[0, 0] <= float(tight), kept, again, grads, operands)
    return (eg[None], gq[None], gk[None], gv[None])


def solution(mesh):
    split = P(("expert", "dp"), "seq", None)
    in_specs = (split, split, split, P(("expert", "dp"), "seq", None, None), split, split, split)
    out_specs = (P("expert", ("seq", "dp"), None), split, split, split)
    body = on_line if mesh.shape["expert"] == 4 and mesh.shape["seq"] == 4 else on_device
    return jax.shard_map(
        body, mesh=mesh, in_specs=in_specs, out_specs=out_specs, check_vma=False
    )
```

```python
import functools

import jax
import jax.numpy as jnp
from jax import lax
from jax.experimental import pallas as pl
from jax.experimental.pallas import tpu as pltpu
from jax.sharding import PartitionSpec as P

HEADS = 16
KV_HEADS = 4
HEAD_DIM = 128
GROUP = HEADS // KV_HEADS
MESH = pl.DeviceIdType.MESH


def dot(a, b, contract):
    return lax.dot_general(a, b, (contract, ((), ())), preferred_element_type=jnp.float32)


def routing_codes(ids, order_row, order_col, experts, capacity):
    count = max(8, experts)
    rows = ids.shape[1]
    expert_of = lax.broadcasted_iota(jnp.int32, (count, rows), 0).astype(jnp.float32)
    onehot = (expert_of == ids).astype(jnp.float32)
    earlier = (order_col < order_row).astype(jnp.float32)
    before = dot(onehot.astype(jnp.bfloat16), earlier.astype(jnp.bfloat16), ((1,), (0,)))
    slot = jnp.sum(before * onehot, axis=0, keepdims=True)
    return ids * float(capacity) + slot


def spreads(experts):
    return experts <= 8 and experts & (experts - 1) == 0


def kernel(
    dims,
    ids_t, info, go, q, k, v, hid,
    eg_out, gq_out, gk_out, gv_out,
    kbuf, vbuf, idbuf, hraw, hsend, hrecv, gsend, grecv, infos,
    kpart, vpart, kown, vown, kin, vin, precv,
    small_send, small_recv, local_sem, hraw_send, hraw_recv,
    gz_send, gz_recv, gi_send, gi_recv, gs_send, gs_recv, hz_send, hz_recv,
    part_send, part_recv, pair_send, pair_recv,
):
    E, S, T, C, U, D = dims
    half = U // 2
    first = -(-half // 256) * 128
    pieces = [(n, o, w) for n in range(2) for o, w in ((0, first), (first, half - first)) if w > 0]
    spread = spreads(E)
    e = lax.axis_index("expert")
    s = lax.axis_index("seq")
    d = lax.axis_index("dp")
    seq_peer = [lax.rem(s + i, S) for i in range(S)]
    bases = [
        pl.multiple_of((d if n else 1 - d) * half + o, 128) for n, o, _ in pieces
    ]

    def ex_peer(j):
        return lax.rem(e + j, E)

    barrier = pltpu.get_barrier_semaphore()
    for i in range(1, S):
        pl.semaphore_signal(barrier, inc=1, device_id={"seq": seq_peer[i]}, device_id_type=MESH)

    @pl.loop(1, E)
    def _(j):
        pl.semaphore_signal(barrier, inc=1, device_id={"expert": ex_peer(j)}, device_id_type=MESH)

    pl.semaphore_signal(barrier, inc=1, device_id={"dp": 1 - d}, device_id_type=MESH)
    pl.semaphore_wait(barrier, S + E - 1)

    def send(src, dst, ssem, rsem, where):
        return pltpu.make_async_remote_copy(
            src_ref=src, dst_ref=dst, send_sem=ssem, recv_sem=rsem,
            device_id=where, device_id_type=MESH,
        )

    def small_copy(n, i, slot):
        src, dst = ((ids_t, idbuf), (k, kbuf), (v, vbuf))[n]
        return send(src, dst.at[slot], small_send.at[n, i], small_recv.at[n, slot], {"seq": seq_peer[i]})

    def raw_copy(c, i, slot):
        width = pieces[c][2]
        cols = pl.ds(pl.multiple_of(seq_peer[i] * U + bases[c], 128), width)
        return send(
            hid.at[:, :, cols], hraw.at[slot, :, :, pl.ds(bases[c], width)],
            hraw_send.at[c, i], hraw_recv.at[c, slot], {"seq": seq_peer[i]},
        )

    own_cols = pl.ds(pl.multiple_of(s * U, 128), U)
    own_raw = pltpu.make_async_copy(hid.at[:, :, own_cols], hraw.at[s], local_sem.at[0])
    own_raw.start()
    for i in range(1, S):
        for n in range(3):
            small_copy(n, i, s).start()
    for c in range(len(pieces)):
        for i in range(1, S):
            raw_copy(c, i, s).start()
    kbuf[s] = k[...]
    vbuf[s] = v[...]
    idbuf[s] = ids_t[...]

    rows = 2 * T
    col = lax.broadcasted_iota(jnp.int32, (rows, rows), 1)
    row = lax.broadcasted_iota(jnp.int32, (rows, rows), 0)
    place = lax.broadcasted_iota(jnp.int32, (E * C, rows), 0).astype(jnp.float32)

    def expert_rows(p):
        return pl.ds(pl.multiple_of(p * C, 16), C)

    def gs_copy(i, z, slot):
        return send(grecv.at[s, z], grecv.at[slot, z], gs_send.at[i, z], gs_recv.at[slot, z], {"seq": seq_peer[i]})

    def gs_wait(i, z):
        slot = seq_peer[i]
        send(grecv.at[s, z], grecv.at[slot, z], gs_send.at[i, z], gs_recv.at[slot, z], {"seq": slot}).wait_recv()

    def packed_grads(ids, gates, grads, wanted):
        code = routing_codes(
            ids, 2 * lax.rem(col, T) + col // T, 2 * lax.rem(row, T) + row // T, E, C
        )
        picks = (wanted == code).astype(jnp.float32)
        gate = jnp.sum(picks * gates, axis=1, keepdims=True)
        token_picks = (picks[:, :T] + picks[:, T:]).astype(jnp.bfloat16)
        return (dot(token_picks, grads, ((1,), (0,))) * gate).astype(jnp.bfloat16)

    if spread:
        def flip(at, b):
            return at + b - 2 * b * lax.rem(at // b, 2)

        bits = []
        b = E // 2
        while b >= 1:
            bits.append(b)
            b //= 2

        def masks(n):
            held = [0]
            for bit in bits[:n]:
                held = held + [m + bit for m in held]
            return held

        def at_mask(m):
            at = e
            for bit in bits:
                if m & bit:
                    at = flip(at, bit)
            return at

        def gz_pair(m, n, slot):
            to = {"expert": flip(e, bits[n])}
            key = m + bits[n]
            return (
                send(gsend.at[slot], gsend.at[slot], gz_send.at[key], gz_recv.at[slot], to),
                send(infos.at[slot], infos.at[slot], gi_send.at[key], gi_recv.at[slot], to),
            )

        def forward(m):
            z = at_mask(m)
            wanted = (
                lax.broadcasted_iota(jnp.int32, (C, rows), 0) + e * C
            ).astype(jnp.float32)
            grecv[s, z] = packed_grads(infos[z, 0:1, :], infos[z, 8:9, :], gsend[z], wanted)
            for i in range(1, S):
                gs_copy(i, z, s).start()

        def arrive(m, n):
            for copy in gz_pair(m, n, at_mask(m + bits[n])):
                copy.wait_recv()
            for later in range(n + 1, len(bits)):
                for copy in gz_pair(m + bits[n], later, at_mask(m + bits[n])):
                    copy.start()

        gsend[e] = go[...]
        infos[e] = info[...]
        for n in range(len(bits)):
            for copy in gz_pair(0, n, e):
                copy.start()
    else:

        def gz_copy(j, slot):
            p = ex_peer(j)
            return send(gsend.at[expert_rows(p)], grecv.at[s, slot], gz_send.at[j], gz_recv.at[slot], {"expert": p})

        gsend[...] = packed_grads(info[0:1, :], info[8:9, :], go[...], place)

        @pl.loop(1, E)
        def _(j):
            gz_copy(j, e).start()

        grecv[s, e] = gsend[expert_rows(e)]
        for i in range(1, S):
            gs_copy(i, e, s).start()

    def hz_copy(c, i, j, slot):
        p = ex_peer(j)
        src = seq_peer[i]
        units = pl.ds(bases[c], pieces[c][2])
        return send(
            hsend.at[src, expert_rows(p), units], hrecv.at[src, slot, :, units],
            hz_send.at[c, src, j], hz_recv.at[c, src, slot], {"expert": p},
        )

    def pack_hidden(c, i):
        src = seq_peer[i]
        width = pieces[c][2]
        units = pl.ds(bases[c], width)
        hcode = routing_codes(idbuf[src, 0:1, :], col, row, E, C)
        hpicks = (place == hcode).astype(jnp.bfloat16)
        hsend[src, :, units] = dot(
            hpicks, hraw[src, :, :, units].reshape(rows, width), ((1,), (0,))
        ).astype(jnp.bfloat16)

        @pl.loop(1, E)
        def _(j):
            hz_copy(c, i, j, e).start()

        hrecv[src, e, :, units] = hsend[src, expert_rows(e), units]

    own_raw.wait()
    for c in range(len(pieces)):
        pack_hidden(c, 0)
    if spread:
        forward(0)

    scale = HEAD_DIM ** (-0.5)
    length = S * T

    def attention(j):
        lanes = slice(j * HEAD_DIM, (j + 1) * HEAD_DIM)
        heads = [slice(h * HEAD_DIM, (h + 1) * HEAD_DIM) for h in range(j * GROUP, (j + 1) * GROUP)]
        qs = jnp.concatenate([q[:, h] for h in heads], axis=0)
        gs = jnp.concatenate([go[:, h] for h in heads], axis=0)
        kj = kbuf[:, :, lanes].reshape(length, HEAD_DIM)
        vj = vbuf[:, :, lanes].reshape(length, HEAD_DIM)
        scores = dot(qs, kj, ((1,), (1,))) * scale
        raised = jnp.exp(scores - jnp.max(scores, axis=-1, keepdims=True))
        probs = raised / jnp.sum(raised, axis=-1, keepdims=True)
        dprobs = dot(gs, vj, ((1,), (1,)))
        delta = jnp.sum(probs * dprobs, axis=-1, keepdims=True)
        ds = (probs * (dprobs - delta)).astype(jnp.bfloat16)
        dv = dot(probs.astype(jnp.bfloat16), gs, ((0,), (0,)))
        dk = dot(ds, qs, ((0,), (0,))) * scale
        dq = dot(ds, kj, ((1,), (0,))) * scale
        for n, h in enumerate(heads):
            gq_out[:, h] = dq[n * T : (n + 1) * T].astype(jnp.bfloat16)
        dk = dk.reshape(S, T, HEAD_DIM)
        dv = dv.reshape(S, T, HEAD_DIM)
        kown[:, :, lanes] = dk
        vown[:, :, lanes] = dv
        kpart[:, :, lanes] = dk.astype(jnp.bfloat16)
        vpart[:, :, lanes] = dv.astype(jnp.bfloat16)

    for i in range(1, S):
        for n in range(3):
            small_copy(n, i, seq_peer[i]).wait_recv()

    attention(0)

    if spread:
        attention(1)
        for n in range(len(bits)):
            for m in masks(n):
                arrive(m, n)
                forward(m + bits[n])
    else:

        @pl.loop(1, E)
        def _(j):
            z = ex_peer(j)
            gz_copy(j, z).wait_recv()
            for i in range(1, S):
                gs_copy(i, z, s).start()

        attention(1)
    for c in range(len(pieces)):
        for i in range(1, S):
            raw_copy(c, i, seq_peer[i]).wait_recv()
            pack_hidden(c, i)
        if c + 2 < KV_HEADS:
            attention(c + 2)
    for j in range(len(pieces) + 2, KV_HEADS):
        attention(j)

    def part_copy(n, i, slot):
        src, dst = ((kpart, kin), (vpart, vin))[n]
        return send(src.at[seq_peer[i]], dst.at[slot], part_send.at[n, i], part_recv.at[n, slot], {"seq": seq_peer[i]})

    for i in range(1, S):
        for n in range(2):
            part_copy(n, i, s).start()
    for n, (own, got, out) in enumerate(((kown, kin, gk_out), (vown, vin, gv_out))):
        total = own[s]
        for i in range(1, S):
            part_copy(n, i, seq_peer[i]).wait_recv()
            total = total + got[seq_peer[i]].astype(jnp.float32)
        out[...] = total.astype(jnp.bfloat16)

    @pl.loop(0, E)
    def _(z):
        for i in range(1, S):
            gs_wait(i, z)

    wide = 256
    tiles = [
        (o + t, min(wide, w - t)) for n, o, w in pieces if n == 0 for t in range(0, w, wide)
    ]

    def arrived(n, off):
        for c, (m, o, _) in enumerate(pieces):
            if m == n and o == off:

                @pl.loop(1, E)
                def _(j):
                    for i in range(S):
                        hz_copy(c, i, j, ex_peer(j)).wait_recv()

    def product(base, off, width):
        units = pl.ds(pl.multiple_of(base + off, 128), width)
        h = hrecv[:, :, :, units].reshape(S * E * C, width)
        return dot(h, grecv[...].reshape(S * E * C, D), ((0,), (0,)))

    def pair_copy(n):
        off, width = tiles[n]
        return send(eg_out.at[off : off + width], precv.at[off : off + width], pair_send.at[n], pair_recv.at[n], {"dp": 1 - d})

    for n, (off, width) in enumerate(tiles):
        arrived(0, off)
        eg_out[off : off + width, :] = product((1 - d) * half, off, width).astype(jnp.bfloat16)
        pair_copy(n).start()
    for n, (off, width) in enumerate(tiles):
        arrived(1, off)
        mine = product(d * half, off, width)
        pair_copy(n).wait_recv()
        pair_copy(n).wait_send()
        got = precv[off : off + width, :].astype(jnp.float32)
        eg_out[off : off + width, :] = (mine + got).astype(jnp.bfloat16)

    for i in range(1, S):
        for n in range(3):
            small_copy(n, i, s).wait_send()
        for n in range(2):
            part_copy(n, i, s).wait_send()
        for c in range(len(pieces)):
            raw_copy(c, i, s).wait_send()

    @pl.loop(0, E)
    def _(z):
        for i in range(1, S):
            gs_copy(i, z, s).wait_send()

    @pl.loop(1, E)
    def _(j):
        if not spread:
            gz_copy(j, e).wait_send()
        for i in range(S):
            for c in range(len(pieces)):
                hz_copy(c, i, j, e).wait_send()

    if spread:
        for n in range(len(bits)):
            for m in masks(n):
                for copy in gz_pair(m, n, at_mask(m)):
                    copy.wait_send()


def on_device(grad_out, expert_ids, gate_weights, hidden, queries, keys, values):
    E = lax.axis_size("expert")
    S = lax.axis_size("seq")
    T = grad_out.shape[1]
    D = grad_out.shape[2]
    U = hidden.shape[3] // S
    C = -(-(7 * T // (2 * E)) // 16) * 16
    KD = keys.shape[2]
    rows = 2 * T
    bf, f32 = jnp.bfloat16, jnp.float32
    ids = expert_ids[0].astype(f32)
    ids_t = jnp.broadcast_to(ids.reshape(1, rows), (8, rows))
    ids_k = jnp.broadcast_to(ids.T.reshape(1, rows), (8, rows))
    gates_k = jnp.broadcast_to(gate_weights[0].T.reshape(1, rows), (8, rows))
    tiles = -(-(U // 2) // 256)
    info = jnp.concatenate([ids_k, gates_k], axis=0)
    sent = (E, T, D) if spreads(E) else (E * C, D)
    vm = pl.BlockSpec(memory_space=pltpu.VMEM)
    dma = pltpu.SemaphoreType.DMA
    eg, gq, gk, gv = pl.pallas_call(
        functools.partial(kernel, (E, S, T, C, U, D)),
        out_shape=(
            jax.ShapeDtypeStruct((U // 2, D), bf),
            jax.ShapeDtypeStruct((T, queries.shape[2]), bf),
            jax.ShapeDtypeStruct((T, KD), bf),
            jax.ShapeDtypeStruct((T, KD), bf),
        ),
        in_specs=[vm] * 6 + [pl.BlockSpec(memory_space=pl.ANY)],
        out_specs=(vm,) * 4,
        scratch_shapes=[
            pltpu.VMEM((S, T, KD), bf),
            pltpu.VMEM((S, T, KD), bf),
            pltpu.VMEM((S, 8, rows), f32),
            pltpu.VMEM((S, T, 2, U), bf),
            pltpu.VMEM((S, E * C, U), bf),
            pltpu.VMEM((S, E, C, U), bf),
            pltpu.VMEM(sent, bf),
            pltpu.VMEM((S, E, C, D), bf),
            pltpu.VMEM((E if spreads(E) else 1, 16, rows), f32),
            pltpu.VMEM((S, T, KD), bf),
            pltpu.VMEM((S, T, KD), bf),
            pltpu.VMEM((S, T, KD), f32),
            pltpu.VMEM((S, T, KD), f32),
            pltpu.VMEM((S, T, KD), bf),
            pltpu.VMEM((S, T, KD), bf),
            pltpu.VMEM((U // 2, D), bf),
            dma((3, S)), dma((3, S)), dma((1,)), dma((4, S)), dma((4, S)),
            dma((E,)), dma((E,)), dma((E,)), dma((E,)), dma((S, E)), dma((S, E)), dma((4, S, E)), dma((4, S, E)),
            dma((2, S)), dma((2, S)), dma((tiles,)), dma((tiles,)),
        ],
        compiler_params=pltpu.CompilerParams(
            collective_id=0, has_side_effects=True, vmem_limit_bytes=62 * 1024 * 1024
        ),
    )(ids_t, info, grad_out[0], queries[0], keys[0], values[0], hidden[0])
    return (eg[None], gq[None], gk[None], gv[None])


def flip(at, b):
    return at + b - 2 * b * lax.rem(at // b, 2)


def greet(peers):
    barrier = pltpu.get_barrier_semaphore()
    for peer in peers:
        pl.semaphore_signal(barrier, inc=1, device_id=peer, device_id_type=MESH)
    pl.semaphore_wait(barrier, len(peers))


def send(src, dst, ssem, rsem, where):
    return pltpu.make_async_remote_copy(
        src_ref=src, dst_ref=dst, send_sem=ssem, recv_sem=rsem,
        device_id=where, device_id_type=MESH,
    )


def line_pieces(half):
    cut = -(-half // 256) * 128
    return [(n, o, w) for n in range(2) for o, w in ((0, cut), (cut, half - cut))]


def line_tiles(half):
    edges = sorted({0, half} | {p[1] for p in line_pieces(half)})
    return [
        (lo + t, min(256, hi - lo - t)) for lo, hi in zip(edges, edges[1:]) for t in range(0, hi - lo, 256)
    ]


def line_kernel(
    dims,
    ids_in, gates_in, go, q, k, v, hid,
    eg_out, gq_out, gk_out, gv_out, most,
    info, peak, peak_in,
    kbuf, vbuf, hraw, picks, hsend, hrecv, gsend, grecv,
    kpart, vpart, kown, vown, kin, vin, precv,
    kv_send, kv_recv, local_sem, raw_send, raw_recv, gz_send, gz_recv, gs_send, gs_recv,
    hz_send, hz_recv, shared_recv, relay_send, relay_recv, part_send, part_recv, pair_send, pair_recv,
    info_send, info_recv,
):
    E, S, T, C, U, D, K = dims
    W = S * C
    half = U // 2
    rows = 2 * T
    packed = K < 2 * W
    parts = range(0 if packed else 1, 4)
    both = 2 * W - K
    pieces = line_pieces(half)
    tiles = line_tiles(half)
    e, s, d = (lax.axis_index(n) for n in ("expert", "seq", "dp"))
    side = e // 2
    friend, across, corner = flip(e, 1), flip(e, 2), flip(flip(e, 1), 2)
    near, far = 2 - side, 3 - 3 * side
    inner = jnp.logical_or(e == 1, e == 2)
    outer = jnp.logical_not(inner)
    others = [2 - 2 * side, 3 - 2 * side]
    peers = [flip(s, 1), flip(s, 2), flip(flip(s, 1), 2)]
    bases = [pl.multiple_of((d if n else 1 - d) * half + o, 128) for n, o, _ in pieces]
    greet([{"seq": p} for p in peers] + [{"expert": p} for p in (friend, across, corner)] + [{"dp": 1 - d}])

    def cols(c):
        return pl.ds(bases[c], pieces[c][2])

    def kv_copy(n, i, slot):
        src, dst = ((k, kbuf), (v, vbuf))[n]
        return send(src, dst.at[slot], kv_send.at[n, i], kv_recv.at[n, i], {"seq": peers[i]})

    def raw_copy(c, i, slot):
        there = pl.ds(pl.multiple_of(peers[i] * U + bases[c], 128), pieces[c][2])
        return send(
            hid.at[:, :, there], hraw.at[slot, :, :, cols(c)],
            raw_send.at[c, i], raw_recv.at[c, i], {"seq": peers[i]},
        )

    def own_copy(c):
        here = pl.ds(pl.multiple_of(s * U + bases[c], 128), pieces[c][2])
        return pltpu.make_async_copy(hid.at[:, :, here], hraw.at[s, :, :, cols(c)], local_sem.at[c])

    def gz_copy(n, slot):
        src = go if n < 2 else gsend.at[across]
        dst = gsend.at[slot]
        to = across if n == 0 else friend
        return send(src, dst, gz_send.at[n], gz_recv.at[n], {"expert": to})

    z_peers = [friend, across, corner]

    def line(ref):
        flat = jnp.concatenate([ref[0:1, :], ref[1:2, :]], axis=1).astype(jnp.float32)
        return jnp.broadcast_to(flat, (1, 8, rows))

    def info_copy(i, slot):
        if i < 3:
            return send(info.at[e, s], info.at[e, slot], info_send.at[i], info_recv.at[i], {"seq": peers[i]})
        return send(info.at[e], info.at[slot], info_send.at[i], info_recv.at[i], {"expert": z_peers[i - 3]})

    info[e, pl.ds(s, 1)] = line(ids_in)
    info[e, S : S + 1] = line(gates_in)
    for i in range(3):
        info_copy(i, s).start()
    gz_copy(0, e).start()
    gz_copy(1, e).start()
    for c in range(len(pieces)):
        own_copy(c).start()
        for i in range(3):
            raw_copy(c, i, s).start()
    for i in range(3):
        for n in range(2):
            kv_copy(n, i, s).start()
    kbuf[s] = k[...]
    vbuf[s] = v[...]

    col = lax.broadcasted_iota(jnp.int32, (rows, rows), 1)
    row = lax.broadcasted_iota(jnp.int32, (rows, rows), 0)
    f32, bf = jnp.float32, jnp.bfloat16
    experts = lax.broadcasted_iota(jnp.int32, (8, rows), 0).astype(f32)
    by_place = (col < row).astype(bf)
    interleave = (row == lax.rem(col, 2) * T + col // 2).astype(bf)
    in_order = (row < col).astype(bf)
    k_order = (2 * lax.rem(row, T) + row // T < 2 * lax.rem(col, T) + col // T).astype(bf)

    def ranked(ids, earlier):
        onehot = (experts == ids).astype(f32)
        return onehot, dot(onehot.astype(bf), earlier, ((1,), (0,)))

    for i in range(3):
        info_copy(i, peers[i]).wait_recv()
    for i in range(3):
        info_copy(3 + i, e).start()
    total = 2 * W + K
    offsets = jnp.zeros((8, 1), f32)
    places = lax.broadcasted_iota(jnp.int32, (128, rows), 0).astype(f32)

    def mark(b, start):
        ids = dot(info[e, b].astype(bf), interleave, ((1,), (0,)))[0:1, :]
        onehot, before = ranked(ids, in_order)
        rank = jnp.sum(onehot * (before + start), axis=0, keepdims=True)
        back = (W + K - 1) - rank if packed else K + rank
        code = jnp.where(
            ids == friend.astype(f32), rank,
            jnp.where(
                ids == e.astype(f32), W + K + rank,
                jnp.where(ids == near.astype(f32), W + rank, back),
            ),
        )

        @pl.loop(0, total // 128)
        def _(r):
            at = places + (128 * r).astype(f32)
            picks[pl.ds(pl.multiple_of(128 * r, 128), 128), b * rows : (b + 1) * rows] = (at == code).astype(bf)

        return start + jnp.sum(onehot, axis=1, keepdims=True)

    for b in range(S):
        offsets = mark(b, offsets if packed else float(C * b))

    def gs_copy(z, n):
        to = peers[0] if n in (0, 3) else peers[1]
        slot = (s, s, peers[0], peers[1])[n]
        lanes = (slice(0, D), slice(0, D), slice(0, D // 2), slice(D // 2, D))[n]
        block = grecv.at[z, slot, :, lanes]
        return send(block, block, gs_send.at[z, n], gs_recv.at[z, n], {"seq": to})

    def gs_wait(z, n):
        slot = (peers[0], peers[1], peers[2], peers[2])[n]
        lanes = (slice(0, D), slice(0, D), slice(0, D // 2), slice(D // 2, D))[n]
        block = grecv.at[z, slot, :, lanes]
        send(block, block, gs_send.at[z, n], gs_recv.at[z, n], {"seq": peers[0]}).wait_recv()

    wanted = lax.broadcasted_iota(jnp.int32, (C, rows), 0).astype(f32)

    def forward(z, grads):
        ids = info[z, pl.ds(s, 1)][0, 0:1, :]
        onehot, before = ranked(ids, k_order)
        rank = jnp.sum(before * onehot, axis=0, keepdims=True)
        code = jnp.where(ids == e.astype(f32), rank, -1.0)
        chosen = (wanted == code).astype(f32)
        gate = jnp.sum(chosen * info[z, 4, 0:1, :], axis=1, keepdims=True)
        token = (chosen[:, :T] + chosen[:, T:]).astype(bf)
        grecv[z, pl.ds(s, 1)] = (dot(token, grads, ((1,), (0,))) * gate).astype(bf)[None]
        for n in range(2):
            gs_copy(z, n).start()

    def pass_on(z):
        for n in range(2):
            gs_wait(z, n)
            gs_copy(z, 2 + n).start()

    def hz_copy(c, n):
        units = cols(c)
        to = (near, far, near, friend)[n]
        first, low, high = ((K, K - W, W), (2 * W, both, W), (W, 0, K - W), (0, 0, W))[n]
        src = hsend.at[first : first + high - low, units]
        landed = shared_recv if n == 0 else hz_recv
        return send(src, hrecv.at[e, low:high, units], hz_send.at[c, n], landed.at[c, e], {"expert": to})

    def hz_wait(c, z, low, high, landed):
        block = hrecv.at[z, low:high, cols(c)]
        send(block, block, hz_send.at[c, 0], landed.at[c, z], {"expert": friend}).wait_recv()

    def relay_copy(c, z):
        return send(
            hrecv.at[z, K - W : W, cols(c)], hrecv.at[z, 0:both, cols(c)],
            relay_send.at[c, z], relay_recv.at[c, z], {"expert": friend},
        )

    def pack(c):
        own_copy(c).wait()
        for i in range(3):
            raw_copy(c, i, peers[i]).wait_recv()
        width = pieces[c][2]
        sent = (W + K) // 4

        def gather(t, size):
            units = pl.ds(pl.multiple_of(bases[c] + t, 128), size)
            block = hraw[:, :, :, units].reshape(S * rows, size)

            @pl.loop(0, 4)
            def _(r):
                some = pl.ds(pl.multiple_of(r * sent, 16), sent)
                hsend[some, units] = dot(picks[some, :], block, ((1,), (0,))).astype(bf)

            hrecv[pl.ds(e, 1), :, units] = dot(picks[W + K :, :], block, ((1,), (0,))).astype(bf)[None]

        if width >= 256:

            @pl.loop(0, width // 256)
            def _(t):
                gather(t * 256, 256)

        if width % 256:
            gather(width - 128, 128)
        for n in parts:
            hz_copy(c, n).start()

    def relay(c):
        if packed:

            @pl.when(inner)
            def _():
                for z in others:
                    hz_wait(c, z, K - W, W, shared_recv)
                    relay_copy(c, z).start()

    def arrived(c):
        hz_wait(c, friend, 0, W, hz_recv)

        @pl.when(inner)
        def _():
            for z in others:
                hz_wait(c, z, 0, K - W, hz_recv)

        @pl.when(outer)
        def _():
            for z in others:
                hz_wait(c, z, both, W, hz_recv)
                if packed:
                    relay_copy(c, z).wait_recv()

    scale = HEAD_DIM ** (-0.5)
    length = S * T

    def attention(j):
        def lanes_of(h):
            return pl.ds(pl.multiple_of(h * HEAD_DIM, HEAD_DIM), HEAD_DIM)

        lanes = lanes_of(j)
        heads = [lanes_of(j * GROUP + n) for n in range(GROUP)]
        qs = jnp.concatenate([q[:, h] for h in heads], axis=0)
        gs = jnp.concatenate([go[:, h] for h in heads], axis=0)
        kj = kbuf[:, :, lanes].reshape(length, HEAD_DIM)
        vj = vbuf[:, :, lanes].reshape(length, HEAD_DIM)
        scores = dot(qs, kj, ((1,), (1,))) * scale
        raised = jnp.exp(scores - jnp.max(scores, axis=-1, keepdims=True))
        probs = raised / jnp.sum(raised, axis=-1, keepdims=True)
        dprobs = dot(gs, vj, ((1,), (1,)))
        delta = jnp.sum(probs * dprobs, axis=-1, keepdims=True)
        ds = (probs * (dprobs - delta)).astype(jnp.bfloat16)
        dv = dot(probs.astype(jnp.bfloat16), gs, ((0,), (0,)))
        dk = dot(ds, qs, ((0,), (0,))) * scale
        dq = dot(ds, kj, ((1,), (0,))) * scale
        for n, h in enumerate(heads):
            gq_out[:, h] = dq[n * T : (n + 1) * T].astype(jnp.bfloat16)
        dk = dk.reshape(S, T, HEAD_DIM)
        dv = dv.reshape(S, T, HEAD_DIM)
        kown[:, :, lanes] = dk
        vown[:, :, lanes] = dv
        kpart[:, :, lanes] = dk.astype(jnp.bfloat16)
        vpart[:, :, lanes] = dv.astype(jnp.bfloat16)

    pack(0)
    forward(e, go[...])
    pack(1)
    for i in range(3):
        info_copy(3 + i, z_peers[i]).wait_recv()
    gz_copy(0, across).wait_recv()
    gz_copy(2, across).start()
    forward(across, gsend[across])
    pack(2)
    gz_copy(1, friend).wait_recv()
    forward(friend, gsend[friend])
    pack(3)
    relay(0)
    for i in range(3):
        for n in range(2):
            kv_copy(n, i, peers[i]).wait_recv()
    pl.loop(0, KV_HEADS)(attention)
    relay(1)
    pass_on(e)
    gz_copy(2, corner).wait_recv()
    forward(corner, gsend[corner])
    pass_on(across)
    pass_on(friend)

    top = jnp.zeros((1, 1), f32)
    for z in range(E):
        crossing = jnp.zeros((1, rows), f32)
        for b in range(S):
            high = (info[z, b, 0:1, :] >= float(E // 2)).astype(f32)
            crossing = crossing + (high if z < E // 2 else 1.0 - high)
        top = jnp.maximum(top, jnp.sum(crossing, axis=1, keepdims=True))
    peak[...] = jnp.broadcast_to(top, (8, 128))
    top_copy = send(peak, peak_in, info_send.at[6], info_recv.at[6], {"dp": 1 - d})
    top_copy.start()

    def part_copy(n, i, slot):
        src, dst = ((kpart, kin), (vpart, vin))[n]
        return send(src.at[peers[i]], dst.at[slot], part_send.at[n, i], part_recv.at[n, i], {"seq": peers[i]})

    for i in range(3):
        for n in range(2):
            part_copy(n, i, s).start()
    relay(2)
    pass_on(corner)
    for n, (own, got, out) in enumerate(((kown, kin, gk_out), (vown, vin, gv_out))):
        summed = own[s]
        for i in range(3):
            part_copy(n, i, peers[i]).wait_recv()
            summed = summed + got[peers[i]].astype(jnp.float32)
        out[...] = summed.astype(jnp.bfloat16)

    def settle(z):
        for n in (2, 3):
            gs_wait(z, n)
        for n in range(4):
            gs_copy(z, n).wait_send()
        if not packed:
            return
        slots = lax.broadcasted_iota(jnp.int32, (1, W), 1).astype(f32)
        code = jnp.full((1, W), -1.0, f32)
        start = jnp.zeros((1, 1), f32)
        for b in range(S):
            named = (info[z, b, 0:1, :] == e.astype(f32)).astype(f32)
            count = jnp.sum(named, axis=1, keepdims=True)
            inside = jnp.logical_and(slots >= float(C * b), slots - float(C * b) < count)
            inside = jnp.logical_and(inside, slots < float(C * (b + 1)))
            code = jnp.where(inside, slots - float(C * b) + start, code)
            start = start + count
        turned = jnp.logical_and(z // 2 != side, outer).astype(f32)
        code = jnp.where(code >= 0.0, code + turned * (float(W - 1) - 2.0 * code), code)
        moves = (lax.broadcasted_iota(jnp.int32, (W, W), 0).astype(f32) == code).astype(bf)

        @pl.loop(0, D // 512)
        def _(t):
            lanes = pl.ds(pl.multiple_of(t * 512, 512), 512)
            block = grecv[z, :, :, lanes].reshape(W, 512)
            grecv[z, :, :, lanes] = dot(moves, block, ((1,), (0,))).astype(bf).reshape(S, C, 512)

    pl.loop(0, E)(settle)

    def product(base, off, width, use):
        units = pl.ds(pl.multiple_of(base + off, 128), width)
        here = pl.ds(off, width)

        @pl.loop(0, D // 1024)
        def _(t):
            lanes = pl.ds(pl.multiple_of(t * 1024, 1024), 1024)
            h = hrecv[:, :, units].reshape(E * W, width)
            use(here, lanes, dot(h, grecv[:, :, :, lanes].reshape(E * W, 1024), ((0,), (0,))))

    def give(here, lanes, value):
        eg_out[here, lanes] = value.astype(jnp.bfloat16)

    def take(here, lanes, value):
        eg_out[here, lanes] = (value + precv[here, lanes].astype(jnp.float32)).astype(jnp.bfloat16)

    def pair_copy(n):
        off, width = tiles[n]
        return send(eg_out.at[off : off + width], precv.at[off : off + width], pair_send.at[n], pair_recv.at[n], {"dp": 1 - d})

    for c, (m, o, w) in enumerate(pieces):
        if c == 2:
            relay(3)
        arrived(c)
        for n, (off, width) in enumerate(tiles):
            if off < o or off >= o + w:
                continue
            if m == 0:
                product((1 - d) * half, off, width, give)
                pair_copy(n).start()
            else:
                pair_copy(n).wait_recv()
                pair_copy(n).wait_send()
                product(d * half, off, width, take)

    top_copy.wait()
    most[0, 0] = jnp.max(jnp.maximum(peak[...], peak_in[...]))
    for i in range(6):
        info_copy(i, s if i < 3 else e).wait_send()
    for i in range(3):
        for n in range(2):
            kv_copy(n, i, s).wait_send()
            part_copy(n, i, s).wait_send()
        gz_copy(i, across if i == 2 else e).wait_send()
    for c in range(len(pieces)):
        for i in range(3):
            raw_copy(c, i, s).wait_send()
        for n in parts:
            hz_copy(c, n).wait_send()
    if packed:

        @pl.when(inner)
        def _():
            for c in range(len(pieces)):
                for z in others:
                    relay_copy(c, z).wait_send()


def line_call(K, number, ids, gates, grad_out, queries, keys, values, hidden):
    E, S = lax.axis_size("expert"), lax.axis_size("seq")
    T, D = grad_out.shape
    U = hidden.shape[2] // S
    C = -(-(7 * T // (2 * E)) // 16) * 16
    KD = keys.shape[1]
    W, rows, half = S * C, 2 * T, U // 2
    bf, f32 = jnp.bfloat16, jnp.float32
    vm = pl.BlockSpec(memory_space=pltpu.VMEM)
    dma = pltpu.SemaphoreType.DMA
    P_ = len(line_pieces(half))
    tiles = len(line_tiles(half))
    return pl.pallas_call(
        functools.partial(line_kernel, (E, S, T, C, U, D, K)),
        out_shape=(
            pltpu.VMEM((half, D), bf),
            pltpu.VMEM((T, D), bf),
            pltpu.VMEM((T, KD), bf),
            pltpu.VMEM((T, KD), bf),
            jax.ShapeDtypeStruct((1, 1), f32),
        ),
        in_specs=[vm] * 6 + [pl.BlockSpec(memory_space=pl.ANY)],
        out_specs=(vm,) * 4 + (pl.BlockSpec(memory_space=pltpu.SMEM),),
        scratch_shapes=[
            pltpu.VMEM((E, S + 1, 8, rows), f32),
            pltpu.VMEM((8, 128), f32),
            pltpu.VMEM((8, 128), f32),
            pltpu.VMEM((S, T, KD), bf),
            pltpu.VMEM((S, T, KD), bf),
            pltpu.VMEM((S, T, 2, U), bf),
            pltpu.VMEM((2 * W + K, S * rows), bf),
            pltpu.VMEM((W + K, U), bf),
            pltpu.VMEM((E, W, U), bf),
            pltpu.VMEM((E, T, D), bf),
            pltpu.VMEM((E, S, C, D), bf),
            pltpu.VMEM((S, T, KD), bf),
            pltpu.VMEM((S, T, KD), bf),
            pltpu.VMEM((S, T, KD), f32),
            pltpu.VMEM((S, T, KD), f32),
            pltpu.VMEM((S, T, KD), bf),
            pltpu.VMEM((S, T, KD), bf),
            pltpu.VMEM((half, D), bf),
            dma((2, 3)), dma((2, 3)), dma((P_,)), dma((P_, 3)), dma((P_, 3)), dma((3,)), dma((3,)),
            dma((E, 4)), dma((E, 4)), dma((P_, 4)), dma((P_, E)), dma((P_, E)), dma((P_, E)), dma((P_, E)),
            dma((2, 3)), dma((2, 3)), dma((tiles,)), dma((tiles,)), dma((7,)), dma((7,)),
        ],
        compiler_params=pltpu.CompilerParams(
            collective_id=number, has_side_effects=True, vmem_limit_bytes=50 * 1024 * 1024
        ),
    )(ids, gates, grad_out, queries, keys, values, hidden)


def publish_kernel(*refs):
    n = (len(refs) - 1) // 2
    copies = []
    for a in range(n):
        count = 8 if a == 0 else 1
        size = refs[a].shape[0] // count
        for c in range(count):
            part = pl.ds(c * size, size)
            copies.append(
                pltpu.make_async_copy(refs[a].at[part], refs[n + a].at[part], refs[-1].at[len(copies)])
            )
    for copy in copies:
        copy.start()
    for copy in copies:
        copy.wait()


def publish(*grads):
    hbm = pl.BlockSpec(memory_space=pl.ANY)
    return pl.pallas_call(
        publish_kernel,
        out_shape=tuple(jax.ShapeDtypeStruct(g.shape, g.dtype) for g in grads),
        in_specs=[hbm] * len(grads),
        out_specs=(hbm,) * len(grads),
        scratch_shapes=[pltpu.SemaphoreType.DMA((8 + len(grads) - 1,))],
        compiler_params=pltpu.CompilerParams(vmem_limit_bytes=1024 * 1024),
    )(*grads)


def on_line(grad_out, expert_ids, gate_weights, hidden, queries, keys, values):
    E, S = lax.axis_size("expert"), lax.axis_size("seq")
    C = -(-(7 * grad_out.shape[1] // (2 * E)) // 16) * 16
    operands = (expert_ids[0].T, gate_weights[0].T, grad_out[0], queries[0], keys[0], values[0], hidden[0])
    full = 2 * S * C
    tight = full * 6 // 7 // 16 * 16
    *grads, most = line_call(tight, 0, *operands)
    grads = publish(*grads)

    def kept(grads, operands):
        return tuple(grads)

    def again(grads, operands):
        return tuple(publish(*line_call(full, 1, *operands)[:4]))

    eg, gq, gk, gv = lax.cond(most[0, 0] <= float(tight), kept, again, grads, operands)
    return (eg[None], gq[None], gk[None], gv[None])


def solution(mesh):
    split = P(("expert", "dp"), "seq", None)
    in_specs = (split, split, split, P(("expert", "dp"), "seq", None, None), split, split, split)
    out_specs = (P("expert", ("seq", "dp"), None), split, split, split)
    body = on_line if mesh.shape["expert"] == 4 and mesh.shape["seq"] == 4 else on_device
    return jax.shard_map(
        body, mesh=mesh, in_specs=in_specs, out_specs=out_specs, check_vma=False
    )
```
